32 devices in a mesh: gz: 16 (over z, x, core), gy: 2 (over y).
Axes of the slice: x: 2, y: 2, z: 4, core: 2. Of those that a mesh axis runs over, the one named last changes fastest.
Arguments:
- vorticity: float32 [256, 128, 512], P('gz', 'gy'), may hold values from -12 to 12
- keep_one: int32 [7, 128, 64, 256], P(None, 'gz', 'gy'), may hold values 0 or 1
- keep_two: int32 [7, 64, 32, 128], P(None, 'gz', 'gy'), may hold values 0 or 1
- keep_three: int32 [7, 32, 16, 64], P(None, 'gz', 'gy'), may hold values 0 or 1
- keep_four: int32 [7, 16, 8, 32], P(None, 'gz', 'gy'), may hold values 0 or 1
- keep_coarse: int32 [16, 8, 32], P('gz', 'gy'), may hold values 0 or 1
Outputs:
- coherent: float32 [256, 128, 512], P('gz', 'gy')
The draws below stay inside these ranges and needn't reach their ends.
All inputs are finite; a program needn't handle non-finite values. No bound on the sum of `keep_one` or of `keep_two` or of `keep_three` or of `keep_four` or of `keep_coarse` on one device may be relied on, other than what follows from the above.
Results may differ from the reference program's by a relative error of at most 0.00017.
Values sent between devices are 32-bit elements; how exact they have to be, the bound alone decides.
A program may use at most 128 MiB of HBM per device.

```python
import math
import jax
import jax.numpy as jnp
from jax import lax

NX = 512
NZ = 256
NY = 128


def draw_vorticity(key, part):
    rough_key = jax.random.fold_in(key, 11)
    z_key = jax.random.fold_in(key, 12)
    y_key = jax.random.fold_in(key, 13)
    x_key = jax.random.fold_in(key, 14)
    phase_key = jax.random.fold_in(key, 15)
    waves_z = jax.random.randint(z_key, (6,), 1, 22).astype(jnp.float32)
    waves_y = jax.random.randint(y_key, (6,), 1, 22).astype(jnp.float32)
    waves_x = jax.random.randint(x_key, (6,), 0, max(2, NX // 24)).astype(jnp.float32)
    phases = jax.random.uniform(phase_key, (6,), jnp.float32, 0.0, 2.0 * math.pi)
    z_pos = jnp.arange(NZ, dtype=jnp.float32)[:, None, None] / NZ
    y_pos = jnp.arange(NY, dtype=jnp.float32)[None, :, None] / NY
    x_pos = jnp.arange(NX, dtype=jnp.float32)[None, None, :] / NX
    smooth = jnp.zeros((NZ, NY, NX), jnp.float32)
    for mode_no in range(6):
        argument = 2.0 * math.pi * (waves_z[mode_no] * z_pos + waves_y[mode_no] * y_pos + waves_x[mode_no] * x_pos)
        smooth = smooth + jnp.sin(argument + phases[mode_no])
    rough = jnp.clip(jax.random.normal(rough_key, (NZ, NY, NX), jnp.float32), -6.0, 6.0)
    return rough + 0.8 * smooth


def with_ends(array, rng, least, largest):
    shape = array.shape
    index_at = [jax.random.randint(jax.random.fold_in(rng, axis), (), 0, shape[axis]) for axis in range(len(shape))]
    array = array.at[tuple(index_at)].set(least)
    longest = shape.index(max(shape))
    index_at[longest] = (index_at[longest] + 1) % shape[longest]
    return array.at[tuple(index_at)].set(largest)


def setup_inputs(seed: int = 0) -> dict:
    key_of = jax.random.split(jax.random.key(seed), 7)
    return {
        "vorticity": draw_vorticity(jax.random.fold_in(key_of[6], 71), 0),
        "keep_one": with_ends((jax.random.randint(key_of[1], (7, NZ // 2, NY // 2, NX // 2), 0, 2) < 1).astype(jnp.int32), jax.random.fold_in(key_of[1], 1), 0, 1),
        "keep_two": with_ends((jax.random.randint(key_of[2], (7, NZ // 4, NY // 4, NX // 4), 0, 2) < 1).astype(jnp.int32), jax.random.fold_in(key_of[2], 1), 0, 1),
        "keep_three": with_ends((jax.random.randint(key_of[3], (7, NZ // 8, NY // 8, NX // 8), 0, 2) < 1).astype(jnp.int32), jax.random.fold_in(key_of[3], 1), 0, 1),
        "keep_four": with_ends((jax.random.randint(key_of[4], (7, NZ // 16, NY // 16, NX // 16), 0, 2) < 1).astype(jnp.int32), jax.random.fold_in(key_of[4], 1), 0, 1),
        "keep_coarse": with_ends((jax.random.randint(key_of[5], (NZ // 16, NY // 16, NX // 16), 0, 2) < 1).astype(jnp.int32), jax.random.fold_in(key_of[5], 1), 0, 1),
    }


low_taps = (0.11154074335008017, 0.4946238903983854, 0.7511339080215775, 0.3152503517092432,
            -0.22626469396516913, -0.12976686756709563, 0.09750160558707936, 0.02752286553001629,
            -0.031582039318031156, 0.0005538422009938016, 0.004777257511010651, -0.00107730108499558)
high_taps = tuple(((-1.0) ** k) * low_taps[11 - k] for k in range(12))


def wrap_right(source, axis_dim, rim_width):
    length = source.shape[axis_dim]
    copies = 1 + (rim_width + length - 1) // length
    repeated = jnp.concatenate([source] * copies, axis=axis_dim)
    return lax.slice_in_dim(repeated, 0, length + rim_width, axis=axis_dim)


def wrap_left(source, axis_dim, rim_width):
    length = source.shape[axis_dim]
    copies = 1 + (rim_width + length - 1) // length
    repeated = jnp.concatenate([source] * copies, axis=axis_dim)
    total_len = copies * length
    return lax.slice_in_dim(repeated, total_len - length - rim_width, total_len, axis=axis_dim)


def split_pair(extended, axis_dim, length):
    low_part = None
    high_part = None
    for k in range(12):
        sliced = lax.slice_in_dim(extended, k, k + length - 1, stride=2, axis=axis_dim)
        if k == 0:
            low_part = low_taps[k] * sliced
            high_part = high_taps[k] * sliced
        else:
            low_part = low_part + low_taps[k] * sliced
            high_part = high_part + high_taps[k] * sliced
    return low_part, high_part


def merge_pair(low_ext, high_ext, axis_dim, coarse_len):
    even_part = None
    odd_part = None
    for t in range(6):
        low_slice = lax.slice_in_dim(low_ext, 5 - t, 5 - t + coarse_len, axis=axis_dim)
        high_slice = lax.slice_in_dim(high_ext, 5 - t, 5 - t + coarse_len, axis=axis_dim)
        even_term = low_taps[2 * t] * low_slice + high_taps[2 * t] * high_slice
        odd_term = low_taps[2 * t + 1] * low_slice + high_taps[2 * t + 1] * high_slice
        if t == 0:
            even_part = even_term
            odd_part = odd_term
        else:
            even_part = even_part + even_term
            odd_part = odd_part + odd_term
    paired = jnp.stack([even_part, odd_part], axis=axis_dim + 1)
    new_shape = even_part.shape[:axis_dim] + (2 * coarse_len,) + even_part.shape[axis_dim + 1:]
    return paired.reshape(new_shape)


def analyse(source, axis_dim):
    return split_pair(wrap_right(source, axis_dim, 10), axis_dim, source.shape[axis_dim])


def synthesize(low_part, high_part, axis_dim):
    coarse_len = low_part.shape[axis_dim]
    return merge_pair(wrap_left(low_part, axis_dim, 5), wrap_left(high_part, axis_dim, 5), axis_dim, coarse_len)


def reference(vorticity, keep_one, keep_two, keep_three, keep_four, keep_coarse):
    keep_list = (keep_one, keep_two, keep_three, keep_four)
    approx = vorticity
    kept_list = []
    for level_no in range(4):
        subbands = list(analyse(approx, 2))
        for axis_dim in (1, 0):
            pair_list = [analyse(member, axis_dim) for member in subbands]
            subbands = [p[0] for p in pair_list] + [p[1] for p in pair_list]
        kept_list.append(jnp.stack(subbands[1:]) * keep_list[level_no].astype(jnp.float32))
        approx = subbands[0]
    rebuilt = approx * keep_coarse.astype(jnp.float32)
    for level_no in (3, 2, 1, 0):
        subbands = [rebuilt] + [kept_list[level_no][b] for b in range(7)]
        subbands = [synthesize(subbands[b], subbands[b + 4], 0) for b in range(4)]
        subbands = [synthesize(subbands[b], subbands[b + 2], 1) for b in range(2)]
        rebuilt = synthesize(subbands[0], subbands[1], 2)
    return rebuilt
```

```python
import functools

import jax
import jax.numpy as jnp
import ml_dtypes
import numpy as np
from jax import lax
from jax.experimental import pallas as pl
from jax.experimental.pallas import tpu as pltpu
from jax.sharding import PartitionSpec as P

low_taps = (
    0.11154074335008017,
    0.4946238903983854,
    0.7511339080215775,
    0.3152503517092432,
    -0.22626469396516913,
    -0.12976686756709563,
    0.09750160558707936,
    0.02752286553001629,
    -0.031582039318031156,
    0.0005538422009938016,
    0.004777257511010651,
    -0.00107730108499558,
)
high_taps = tuple(((-1.0) ** k * low_taps[11 - k] for k in range(12)))
LEVELS = 4
MESH = pl.DeviceIdType.MESH
BF16 = jnp.bfloat16
F32 = jnp.float32


def rotations():
    h, g = low_taps, high_taps
    now = [np.array([[h[2 * m], h[2 * m + 1]], [g[2 * m], g[2 * m + 1]]]) for m in range(6)]
    found = []
    while len(now) > 1:
        row = now[0][np.argmax(np.linalg.norm(now[0], axis=1))]
        a, b = row / np.linalg.norm(row)
        turn = np.array([[a, b], [-b, a]])
        rest = [m @ turn.T for m in now]
        now = [np.stack([rest[m][:, 0], rest[m + 1][:, 1]], 1) for m in range(len(now) - 1)]
        found.append(turn)
    found.append(now[0])
    sizes = [np.abs(m).max() for m in found]
    return [m / s for m, s in zip(found, sizes)], float(np.prod(sizes))


TURNS, SCALE = rotations()


def mix(a, x, b, y):
    if x is None and y is None:
        return None
    terms = []
    for c, v in ((float(a), x), (float(b), y)):
        if v is not None:
            terms.append((c, v))
    if len(terms) == 1:
        c, v = terms[0]
        return v if c == 1.0 else -v if c == -1.0 else c * v
    (c, v), (d, w) = terms
    if abs(d) == 1.0:
        (c, v), (d, w) = (d, w), (c, v)
    if c == 1.0:
        return v + d * w
    if c == -1.0:
        return d * w - v
    return c * v + d * w


def turn(m, u, w):
    return mix(m[0, 0], u, m[0, 1], w), mix(m[1, 0], u, m[1, 1], w)


def lattice_split(pairs, state=(None,) * 5):
    state = list(state)
    outs = [None] * len(pairs)
    for i in reversed(range(len(pairs))):
        u, w = turn(TURNS[0], *pairs[i]())
        for k in range(1, 6):
            w, state[k - 1] = state[k - 1], w
            u, w = turn(TURNS[k], u, w)
        outs[i] = (u, w)
    return outs, state


def lattice_merge(pairs, state=(None,) * 5):
    state = list(state)
    outs = []
    for pair in pairs:
        u, w = turn(TURNS[5].T, *pair())
        for k in range(5, 0, -1):
            w, state[k - 1] = state[k - 1], w
            u, w = turn(TURNS[k - 1].T, u, w)
        outs.append((u, w))
    return outs, state


def far_weight(lattice, first, last, pairs):
    state = [None] * 5
    state[first] = np.float64(1.0)
    left = lattice([lambda: (None, None)] * pairs, state)[1]
    return float(left[last])


def halves(matrix):
    matrix = matrix.astype(np.float32)
    high = matrix.astype(ml_dtypes.bfloat16)
    low = (matrix - high.astype(np.float32)).astype(ml_dtypes.bfloat16)
    return np.stack([high, low])


def x_matrix(x_len):
    half = x_len // 2
    matrix = np.zeros((x_len, x_len))
    for i in range(half):
        for k in range(12):
            matrix[(2 * i + k) % x_len, i] += low_taps[k]
            matrix[(2 * i + k) % x_len, half + i] += high_taps[k]
    return matrix


def y_split_parts(n):
    half = n // 2
    whole = np.zeros((n, n + 10))
    for i in range(half):
        for k in range(12):
            whole[i, 2 * i + k] = low_taps[k]
            whole[half + i, 2 * i + k] = high_taps[k]
    left, size, right = np.linalg.svd(whole[:, n:])
    return whole[:, :n], left[:, :5] * size[:5], right[:5], whole[:, n:]


def y_merge_parts(n):
    half = n // 2
    own = np.zeros((n, n))
    back = np.zeros((n, 10))
    for j in range(n):
        for t in range(6):
            k = 2 * t + j % 2
            c = j // 2 - t
            if c >= 0:
                own[j, c] += low_taps[k]
                own[j, half + c] += high_taps[k]
            else:
                back[j, 5 + c] += low_taps[k]
                back[j, 10 + c] += high_taps[k]
    left, size, right = np.linalg.svd(back)
    return own, left[:, :5] * size[:5], right[:5], back


class Level:
    def __init__(self, z, y, x):
        self.z, self.y, self.x = z, y, x
        self.zc, self.yc, self.xc = z // 2, y // 2, x // 2
        self.states = self.zc >= 4
        self.far = self.zc == 4
        self.comb = self.yc >= 8
        assert self.states or self.zc <= 2
        assert self.comb or self.yc == 4
        self.used = y + 8 if self.comb else y + 16
        self.rows = y + 16
        self.fwd_planes = z if self.states else z + 10
        self.back = 0 if self.states else 5
        self.group = min(z, 8)

    def matrices(self):
        n, half = self.y, self.yc
        own, ahead, pick, direct = y_split_parts(n)
        fwd = np.zeros((n, self.used))
        fwd[:, :n] = own
        inv_own, behind, inv_pick, inv_direct = y_merge_parts(n)
        inv = np.zeros((n, self.used))
        inv[:, :n] = inv_own
        out = {"x_fwd": halves(x_matrix(self.x)), "x_inv": halves(x_matrix(self.x).T)}
        if self.comb:
            fwd[:, n : n + 5] = ahead
            inv[:, n : n + 5] = behind
            small = np.zeros((8, 16))
            small[:5, :10] = pick
            out["c_fwd"] = halves(np.kron(np.eye(self.group), small))
            small = np.zeros((8, 16))
            small[:5, 3:8] = inv_pick[:, :5]
            small[:5, 11:16] = inv_pick[:, 5:]
            out["c_inv"] = halves(np.kron(np.eye(self.group), small))
        else:
            fwd[:, n : n + 10] = direct
            for c in range(5):
                hop, at = (0, c - 1) if c else (1, half - 1)
                inv[:, n + hop * n + at] = inv_direct[:, c]
                inv[:, n + hop * n + half + at] = inv_direct[:, 5 + c]
        out["y_fwd"] = halves(fwd * SCALE)
        out["y_inv"] = halves(inv * SCALE)
        return out


def hop_list(length, rim):
    pieces = []
    done = 0
    hop = 1
    while done < rim:
        take = min(length, rim - done)
        pieces.append((hop, done, take))
        done += take
        hop += 1
    return pieces


def split_product(data, pair_ref):
    high = data.astype(BF16)
    low = (data - high.astype(F32)).astype(BF16)
    out = jnp.dot(high, pair_ref[0], preferred_element_type=F32)
    out += jnp.dot(low, pair_ref[0], preferred_element_type=F32)
    return out + jnp.dot(high, pair_ref[1], preferred_element_type=F32)


def product_split(pair_ref, data):
    high = data.astype(BF16)
    low = (data - high.astype(F32)).astype(BF16)
    out = jnp.dot(pair_ref[0], high, preferred_element_type=F32)
    out += jnp.dot(pair_ref[0], low, preferred_element_type=F32)
    return out + jnp.dot(pair_ref[1], high, preferred_element_type=F32)


LATE = ("x_fwd0",)
SENDS = 96
LOADS = 8


def kernel(levels, nz, ny, names, *refs):
    r = dict(zip(names, refs))
    lv1 = levels[0]
    half = lv1.xc
    lanes_of = (slice(0, half), slice(half, lv1.x))
    gz = lax.axis_index("gz")
    gy = lax.axis_index("gy")

    def device(dz, dy):
        return (lax.rem(gz + (dz + nz) % nz, nz), lax.rem(gy + (dy + ny) % ny, ny))

    offsets = sorted(
        {(dz % nz, dy % ny) for dz in range(-5, 6) for dy in range(-2, 3)} - {(0, 0)}
    )
    barrier = pltpu.get_barrier_semaphore()
    for dz, dy in offsets:
        pl.semaphore_signal(barrier, inc=1, device_id=device(dz, dy), device_id_type=MESH)

    chunk = lv1.z // 4
    loads = [pltpu.make_async_copy(r["x_fwd0"], r["x_fwd0_v"], r["load_sem"].at[4])]
    for c in range(4):
        at = pl.ds(c * chunk, chunk)
        loads.append(
            pltpu.make_async_copy(r["field"].at[at], r["whole"].at[at], r["load_sem"].at[c])
        )
    loads.append(pltpu.make_async_copy(r["keep0"], r["keep0_v"], r["load_sem"].at[5]))
    for load in loads:
        load.start()

    used = [0]
    sends = []

    def send(src, dst, dz, dy):
        at = used[0]
        used[0] += 1
        copy = pltpu.make_async_remote_copy(
            src_ref=src,
            dst_ref=dst,
            send_sem=r["send_sem"].at[at],
            recv_sem=r["recv_sem"].at[at],
            device_id=device(dz, dy),
            device_id_type=MESH,
        )
        copy.start()
        sends.append(copy)
        return copy

    def arrive(copies):
        for copy in copies:
            copy.wait_recv()

    fx = r["a0"]
    loads[0].wait()
    for c in range(4):
        loads[1 + c].wait()
        at = pl.ds(c * chunk, chunk)
        rows = r["whole"][at].reshape(chunk * lv1.y, lv1.x)
        fx[at, 0 : lv1.y, :] = split_product(rows, r["x_fwd0_v"]).reshape(chunk, lv1.y, lv1.x)

    def comb_forward(no):
        lv, a = levels[no], r[f"a{no}"]
        for start in range(0, lv.z, lv.group):
            at = slice(start, start + lv.group)
            rows = a[at, 0:16, :].reshape(lv.group * 16, lv.x)
            done = product_split(r[f"c_fwd{no}"], rows)
            a[at, lv.y + 8 : lv.y + 16, :] = done.reshape(lv.group, 8, lv.x)

    def row_of(tile, lv):
        return pl.multiple_of(jnp.where(tile < lv.y // 8, tile * 8, lv.y + 8), 8)

    def states_forward(no):
        lv, a, out = levels[no], r[f"a{no}"], r[f"fs{no}"]
        count = min(lv.zc, 5)

        def tile(t, carry):
            at = pl.ds(row_of(t, lv), 8)
            for lanes in [slice(s, s + 256) for s in range(0, lv.x, 256)]:
                pairs = [
                    lambda i=i: (a[2 * i, at, lanes], a[2 * i + 1, at, lanes]) for i in range(count)
                ]
                for k, value in enumerate(lattice_split(pairs)[1]):
                    out[k, at, lanes] = value
            return carry

        lax.fori_loop(0, lv.y // 8 + 1, tile, 0)

    comb_forward(0)
    states_forward(0)

    loads[-1].wait()
    for no, lv in enumerate(levels):
        keep = r["keep0_v"] if no == 0 else r[f"keep{no}"]
        mask = r[f"mask{no}"]

        def fill(i, carry, lv=lv, keep=keep, mask=mask, no=no):
            for bz in range(2):
                for by in range(2):
                    parts = []
                    for bx in range(2):
                        band = 4 * bz + 2 * by + bx
                        if band:
                            parts.append(keep[band - 1, i].astype(F32))
                        elif no == LEVELS - 1:
                            parts.append(r["coarse"][i].astype(F32))
                        else:
                            parts.append(jnp.zeros((lv.yc, lv.xc), F32))
                    at = slice(by * lv.yc, (by + 1) * lv.yc)
                    mask[bz, i, at, :] = jnp.concatenate(parts, axis=1)
            return carry

        lax.fori_loop(0, lv.zc, fill, 0)

    pl.semaphore_wait(barrier, len(offsets))

    def send_states(no, sign, lanes, own, comb):
        lv = levels[no]
        src, dst = (r[f"fs{no}"], r[f"fr{no}"]) if sign < 0 else (r[f"bs{no}"], r[f"br{no}"])
        far = 0 if sign < 0 else 4
        top, in_at = lv.y + 8, slice(lv.y, lv.y + 8)
        copies = []
        if own is not None:
            copies.append(send(src.at[0:5, own, lanes], dst.at[0:5, own, lanes], sign, 0))
            if lv.far:
                copies.append(
                    send(src.at[far, own, lanes], dst.at[5, own, lanes], 2 * sign, 0)
                )
        if comb:
            copies.append(
                send(src.at[0:5, top : top + 8, lanes], dst.at[0:5, in_at, lanes], sign, sign)
            )
            if lv.far:
                copies.append(
                    send(
                        src.at[far, top : top + 8, lanes], dst.at[5, in_at, lanes], 2 * sign, sign
                    )
                )
        return copies

    every = slice(None)

    def send_forward(no, lanes):
        lv, a = levels[no], r[f"a{no}"]
        copies = []
        if lv.states:
            copies += send_states(no, -1, lanes, slice(0, lv.y), True)
            pieces = [(0, 0, lv.z)]
        else:
            pieces = [(0, 0, lv.z)] + hop_list(lv.z, 10)
        for hz, z_at, take in pieces:
            z_to = 0 if hz == 0 else lv.z + z_at
            if hz:
                copies.append(
                    send(a.at[0:take, 0 : lv.y, lanes], a.at[z_to : z_to + take, 0 : lv.y, lanes], -hz, 0)
                )
            if lv.comb:
                copies.append(
                    send(
                        a.at[0:take, lv.y + 8 : lv.y + 16, lanes],
                        a.at[z_to : z_to + take, lv.y : lv.y + 8, lanes],
                        -hz,
                        -1,
                    )
                )
                continue
            for hy in (1, 2):
                if hy % ny:
                    copies.append(
                        send(
                            a.at[0:take, 0 : lv.y, lanes],
                            a.at[z_to : z_to + take, hy * lv.y : (hy + 1) * lv.y, lanes],
                            -hz,
                            -hy,
                        )
                    )
        return copies

    def own_wrap(no, a, lead):
        lv = levels[no]
        if not lv.comb and 2 % ny == 0:
            a[lead + (slice(2 * lv.y, 3 * lv.y),)] = a[lead + (slice(0, lv.y),)]

    def z_split(no, lanes):
        lv, a, out = levels[no], r[f"a{no}"], r[f"zx{no}"]
        tall = 8 if lv.states else lv.used

        def tile(t, carry):
            at = pl.ds(pl.multiple_of(t * 8, 8), 8) if lv.states else slice(0, tall)
            state = [None] * 5
            if lv.states:
                got = r[f"fr{no}"]
                state = [got[k, at, lanes] for k in range(5)]
                if lv.far:
                    state[4] = state[4] + far_weight(lattice_split, 0, 4, 4) * got[5, at, lanes]
            count = lv.zc if lv.states else lv.zc + 5
            pairs = [
                lambda i=i: (a[2 * i, at, lanes], a[2 * i + 1, at, lanes]) for i in range(count)
            ]
            outs = lattice_split(pairs, state)[0]
            for i in range(lv.zc):
                for bz in range(2):
                    out[bz, i, at, lanes] = outs[i][bz]
            return carry

        if lv.states:
            lax.fori_loop(0, lv.used // 8, tile, 0)
        else:
            tile(0, 0)

    def y_split(no, bands, lanes):
        lv, src, coef, mask = levels[no], r[f"zx{no}"], r[f"e{no}"], r[f"mask{no}"]
        low = lanes.start in (None, 0)

        def plane(i, carry):
            for bz in bands:
                mixed = product_split(r[f"y_fwd{no}"], src[bz, i, 0 : lv.used, lanes])
                coef[bz, lv.back + i, 0 : lv.y, lanes] = mixed * mask[bz, i, :, lanes]
                if bz == 0 and low and no < LEVELS - 1:
                    r[f"a{no + 1}"][i, 0 : lv.yc, :] = mixed[0 : lv.yc, 0 : lv.xc]
            return carry

        lax.fori_loop(0, lv.zc, plane, 0)

    def comb_back(no, bands, lanes):
        lv, coef = levels[no], r[f"e{no}"]
        own = slice(lv.back, lv.back + lv.zc)
        planes = [(bz, lv.back + i) for bz in bands for i in range(lv.zc)]
        wide = lv.xc if no == 0 else lv.x
        for start in range(0, len(planes), lv.group):
            part = planes[start : start + lv.group]
            pieces = []
            for bz, i in part:
                pieces.append(coef[bz, i, lv.yc - 8 : lv.yc, lanes])
                pieces.append(coef[bz, i, 2 * lv.yc - 8 : 2 * lv.yc, lanes])
            done = product_split(r[f"c_inv{no}"], jnp.concatenate(pieces, axis=0))
            for n, (bz, i) in enumerate(part):
                coef[bz, i, lv.y + 8 : lv.y + 16, lanes] = done[8 * n : 8 * n + 8]

    def states_back(no, lanes, first, last):
        lv, coef, out = levels[no], r[f"e{no}"], r[f"bs{no}"]
        start = max(lv.zc - 5, 0)

        def tile(t, carry):
            at = pl.ds(row_of(t, lv), 8)
            pairs = [
                lambda i=i: (coef[0, i, at, lanes], coef[1, i, at, lanes])
                for i in range(start, lv.zc)
            ]
            for k, value in enumerate(lattice_merge(pairs)[1]):
                out[k, at, lanes] = value
            return carry

        lax.fori_loop(first, last, tile, 0)

    def send_rows_back(no, bands, lanes):
        lv, coef = levels[no], r[f"e{no}"]
        return [
            send(
                coef.at[bands, lv.back : lv.back + lv.zc, lv.y + 8 : lv.y + 16, lanes],
                coef.at[bands, lv.back : lv.back + lv.zc, lv.y : lv.y + 8, lanes],
                0,
                1,
            )
        ]

    def send_back(no):
        lv, coef = levels[no], r[f"e{no}"]
        copies = []
        if lv.states:
            copies += send_states(no, 1, every, slice(0, lv.y), True)
            return copies + send_rows_back(no, every, every)
        for hz, done, take in [(0, 0, lv.zc)] + hop_list(lv.zc, 5):
            src_at = slice(5 + lv.zc - take, 5 + lv.zc)
            dst_at = src_at if hz == 0 else slice(5 - done - take, 5 - done)
            if hz:
                copies.append(
                    send(coef.at[:, src_at, 0 : lv.y], coef.at[:, dst_at, 0 : lv.y], hz, 0)
                )
            if lv.comb:
                copies.append(
                    send(
                        coef.at[:, src_at, lv.y + 8 : lv.y + 16],
                        coef.at[:, dst_at, lv.y : lv.y + 8],
                        hz,
                        1,
                    )
                )
                continue
            for hy in (1, 2):
                if hy % ny:
                    copies.append(
                        send(
                            coef.at[:, src_at, 0 : lv.y],
                            coef.at[:, dst_at, hy * lv.y : (hy + 1) * lv.y],
                            hz,
                            hy,
                        )
                    )
        return copies

    def z_merge(no, lanes):
        lv, coef, out = levels[no], r[f"e{no}"], r[f"v{no}"]

        def tile(t, carry):
            at = pl.ds(pl.multiple_of(t * 8, 8), 8) if lv.states else slice(0, lv.used)
            state = [None] * 5
            if lv.states:
                got = r[f"br{no}"]
                state = [got[k, at, lanes] for k in range(5)]
                if lv.far:
                    state[0] = state[0] + far_weight(lattice_merge, 4, 0, 4) * got[5, at, lanes]
            pairs = [
                lambda i=i: (coef[0, i, at, lanes], coef[1, i, at, lanes])
                for i in range(lv.back + lv.zc)
            ]
            outs = lattice_merge(pairs, state)[0][lv.back :]
            for i in range(lv.zc):
                for p in range(2):
                    out[2 * i + p, at, lanes] = outs[i][p]
            return carry

        if lv.states:
            lax.fori_loop(0, lv.used // 8, tile, 0)
        else:
            tile(0, 0)

    def y_merge(no, lanes, out):
        lv, src = levels[no], r[f"v{no}"]

        def plane(z, carry):
            out[z, :, lanes] = product_split(r[f"y_inv{no}"], src[z, :, lanes])
            return carry

        lax.fori_loop(0, lv.z, plane, 0)

    low, high = lanes_of
    got = send_forward(0, low)
    arrive(got)
    z_split(0, low)
    y_split(0, (0,), low)

    for no in range(1, LEVELS):
        lv = levels[no]
        if lv.comb:
            comb_forward(no)
        if lv.states:
            states_forward(no)
        got = send_forward(no, every)
        if no == 1:
            later = send_forward(0, high)
            y_split(0, (1,), low)
            comb_back(0, (1,), low)
        if no == 2:
            arrive(later)
            z_split(0, high)
            y_split(0, (0, 1), high)
        if no == 3:
            comb_back(0, (0, 1), high)
            states_back(0, high, 0, lv1.y // 8 + 1)
            states_back(0, low, lv1.yc // 8, lv1.y // 8)
        arrive(got)
        own_wrap(no, r[f"a{no}"], (every,))
        z_split(no, every)
        count = 2 * lv.zc
        rows = r[f"zx{no}"][...].reshape(count * lv.used, lv.x)
        done = split_product(rows, r[f"x_fwd{no}"])
        r[f"zx{no}"][...] = done.reshape(2, lv.zc, lv.used, lv.x)
        y_split(no, (0, 1), every)

    for no in range(LEVELS - 1, 0, -1):
        lv = levels[no]
        if lv.comb:
            comb_back(no, (0, 1), every)
        if lv.states:
            states_back(no, every, 0, lv.y // 8 + 1)
        got = send_back(no)
        if no == 3:
            early = send_states(0, 1, high, slice(0, lv1.y), True)
            early += send_rows_back(0, every, high)
        if no == 2:
            early_low = send_states(0, 1, low, slice(lv1.yc, lv1.y), False)
            early_low += send_rows_back(0, slice(1, 2), low)
        if no == 1:
            arrive(early)
            z_merge(0, high)
            y_merge(0, high, r["out"])
        arrive(got)
        own_wrap(no, r[f"e{no}"], (every, every))
        z_merge(no, every)
        y_merge(no, every, r[f"yv{no}"])
        rows = r[f"yv{no}"][...].reshape(lv.z * lv.y, lv.x)
        done = split_product(rows, r[f"x_inv{no}"]).reshape(lv.z, lv.y, lv.x)
        up = levels[no - 1]
        for p in range(2 if no == 0 else 1):
            r[f"e{no - 1}"][0, up.back : up.back + up.zc, 0 : up.yc, 0 : up.xc] = done

    comb_back(0, (0,), low)
    states_back(0, low, 0, lv1.yc // 8)
    states_back(0, low, lv1.y // 8, lv1.y // 8 + 1)
    got = send_states(0, 1, low, slice(0, lv1.yc), True)
    got += send_rows_back(0, slice(0, 1), low)
    arrive(early_low)
    arrive(got)
    z_merge(0, low)
    y_merge(0, low, r["out"])
    for copy in sends:
        copy.wait_send()
    assert used[0] <= SENDS


def last_kernel(v, pair, out):
    planes, y, x = v.shape
    rows = v[...].reshape(planes * y, x)
    out[...] = split_product(rows, pair).reshape(planes, y, x)


def solution(mesh):
    nz, ny = mesh.shape["gz"], mesh.shape["gy"]

    def on_device(field, k1, k2, k3, k4, coarse):
        z, y, x = field.shape
        levels = [Level(z >> n, y >> n, x >> n) for n in range(LEVELS)]
        vmem = pl.BlockSpec(memory_space=pltpu.VMEM)
        hbm = pl.BlockSpec(memory_space=pl.ANY)
        names = ["field", "keep0", "keep1", "keep2", "keep3", "coarse"]
        operands = [field, k1, k2, k3, k4, coarse]
        specs = [hbm, hbm] + [vmem] * 4
        last = None
        for no, lv in enumerate(levels):
            for name, matrix in lv.matrices().items():
                if no == 0 and name == "x_inv":
                    last = jnp.asarray(matrix)
                    continue
                names.append(f"{name}{no}")
                operands.append(jnp.asarray(matrix))
                specs.append(hbm if f"{name}{no}" in LATE else vmem)
        names.append("out")
        scratch = {
            "whole": pltpu.VMEM((z, y, x), F32),
            "x_fwd0_v": pltpu.VMEM((2, x, x), BF16),
            "keep0_v": pltpu.VMEM(k1.shape, jnp.int32),
        }
        for no, lv in enumerate(levels):
            scratch[f"a{no}"] = pltpu.VMEM((lv.fwd_planes, lv.rows, lv.x), F32)
            scratch[f"zx{no}"] = pltpu.VMEM((2, lv.zc, lv.used, lv.x), F32)
            scratch[f"e{no}"] = pltpu.VMEM((2, lv.back + lv.zc, lv.rows, lv.x), F32)
            scratch[f"v{no}"] = pltpu.VMEM((lv.z, lv.used, lv.x), F32)
            scratch[f"mask{no}"] = pltpu.VMEM((2, lv.zc, lv.y, lv.x), F32)
            if no:
                scratch[f"yv{no}"] = pltpu.VMEM((lv.z, lv.y, lv.x), F32)
            if lv.states:
                for name, planes in (("fs", 5), ("fr", 6), ("bs", 5), ("br", 6)):
                    scratch[f"{name}{no}"] = pltpu.VMEM((planes, lv.rows, lv.x), F32)
        scratch["load_sem"] = pltpu.SemaphoreType.DMA((LOADS,))
        scratch["send_sem"] = pltpu.SemaphoreType.DMA((SENDS,))
        scratch["recv_sem"] = pltpu.SemaphoreType.DMA((SENDS,))
        names += list(scratch)
        merged = pl.pallas_call(
            functools.partial(kernel, levels, nz, ny, names),
            out_shape=jax.ShapeDtypeStruct((z, y, x), F32),
            in_specs=specs,
            out_specs=vmem,
            scratch_shapes=list(scratch.values()),
            compiler_params=pltpu.CompilerParams(
                collective_id=0, has_side_effects=True, vmem_limit_bytes=56 * 1024 * 1024
            ),
        )(*operands)
        planes = z // 4
        block = pl.BlockSpec((planes, y, x), lambda i: (i, 0, 0))
        return pl.pallas_call(
            last_kernel,
            grid=(z // planes,),
            out_shape=jax.ShapeDtypeStruct((z, y, x), F32),
            in_specs=[block, vmem],
            out_specs=block,
            compiler_params=pltpu.CompilerParams(vmem_limit_bytes=48 * 1024 * 1024),
        )(merged, last)

    in_specs = (
        P("gz", "gy", None),
        P(None, "gz", "gy", None),
        P(None, "gz", "gy", None),
        P(None, "gz", "gy", None),
        P(None, "gz", "gy", None),
        P("gz", "gy", None),
    )
    return jax.shard_map(
        on_device, mesh=mesh, in_specs=in_specs, out_specs=P("gz", "gy", None), check_vma=False
    )
```

```python
import functools

import jax
import jax.numpy as jnp
import ml_dtypes
import numpy as np
from jax import lax
from jax.experimental import pallas as pl
from jax.experimental.pallas import tpu as pltpu
from jax.sharding import PartitionSpec as P

low_taps = (
    0.11154074335008017,
    0.4946238903983854,
    0.7511339080215775,
    0.3152503517092432,
    -0.22626469396516913,
    -0.12976686756709563,
    0.09750160558707936,
    0.02752286553001629,
    -0.031582039318031156,
    0.0005538422009938016,
    0.004777257511010651,
    -0.00107730108499558,
)
high_taps = tuple(((-1.0) ** k * low_taps[11 - k] for k in range(12)))
LEVELS = 4
MESH = pl.DeviceIdType.MESH
BF16 = jnp.bfloat16
F32 = jnp.float32


def rotations():
    h, g = low_taps, high_taps
    now = [np.array([[h[2 * m], h[2 * m + 1]], [g[2 * m], g[2 * m + 1]]]) for m in range(6)]
    found = []
    while len(now) > 1:
        row = now[0][np.argmax(np.linalg.norm(now[0], axis=1))]
        a, b = row / np.linalg.norm(row)
        turn = np.array([[a, b], [-b, a]])
        rest = [m @ turn.T for m in now]
        now = [np.stack([rest[m][:, 0], rest[m + 1][:, 1]], 1) for m in range(len(now) - 1)]
        found.append(turn)
    found.append(now[0])
    sizes = [np.abs(m).max() for m in found]
    return [m / s for m, s in zip(found, sizes)], float(np.prod(sizes))


TURNS, SCALE = rotations()


def mix(a, x, b, y):
    if x is None and y is None:
        return None
    terms = []
    for c, v in ((float(a), x), (float(b), y)):
        if v is not None:
            terms.append((c, v))
    if len(terms) == 1:
        c, v = terms[0]
        return v if c == 1.0 else -v if c == -1.0 else c * v
    (c, v), (d, w) = terms
    if abs(d) == 1.0:
        (c, v), (d, w) = (d, w), (c, v)
    if c == 1.0:
        return v + d * w
    if c == -1.0:
        return d * w - v
    return c * v + d * w


def turn(m, u, w):
    return mix(m[0, 0], u, m[0, 1], w), mix(m[1, 0], u, m[1, 1], w)


def lattice_split(pairs, state=(None,) * 5):
    state = list(state)
    outs = [None] * len(pairs)
    for i in reversed(range(len(pairs))):
        u, w = turn(TURNS[0], *pairs[i]())
        for k in range(1, 6):
            w, state[k - 1] = state[k - 1], w
            u, w = turn(TURNS[k], u, w)
        outs[i] = (u, w)
    return outs, state


def lattice_merge(pairs, state=(None,) * 5):
    state = list(state)
    outs = []
    for pair in pairs:
        u, w = turn(TURNS[5].T, *pair())
        for k in range(5, 0, -1):
            w, state[k - 1] = state[k - 1], w
            u, w = turn(TURNS[k - 1].T, u, w)
        outs.append((u, w))
    return outs, state


def far_weight(lattice, first, last, pairs):
    state = [None] * 5
    state[first] = np.float64(1.0)
    left = lattice([lambda: (None, None)] * pairs, state)[1]
    return float(left[last])


def halves(matrix):
    matrix = matrix.astype(np.float32)
    high = matrix.astype(ml_dtypes.bfloat16)
    low = (matrix - high.astype(np.float32)).astype(ml_dtypes.bfloat16)
    return np.stack([high, low])


def x_matrix(x_len):
    half = x_len // 2
    matrix = np.zeros((x_len, x_len))
    for i in range(half):
        for k in range(12):
            matrix[(2 * i + k) % x_len, i] += low_taps[k]
            matrix[(2 * i + k) % x_len, half + i] += high_taps[k]
    return matrix


def y_split_parts(n):
    half = n // 2
    whole = np.zeros((n, n + 10))
    for i in range(half):
        for k in range(12):
            whole[i, 2 * i + k] = low_taps[k]
            whole[half + i, 2 * i + k] = high_taps[k]
    left, size, right = np.linalg.svd(whole[:, n:])
    return whole[:, :n], left[:, :5] * size[:5], right[:5], whole[:, n:]


def y_merge_parts(n):
    half = n // 2
    own = np.zeros((n, n))
    back = np.zeros((n, 10))
    for j in range(n):
        for t in range(6):
            k = 2 * t + j % 2
            c = j // 2 - t
            if c >= 0:
                own[j, c] += low_taps[k]
                own[j, half + c] += high_taps[k]
            else:
                back[j, 5 + c] += low_taps[k]
                back[j, 10 + c] += high_taps[k]
    left, size, right = np.linalg.svd(back)
    return own, left[:, :5] * size[:5], right[:5], back


class Level:
    def __init__(self, z, y, x):
        self.z, self.y, self.x = z, y, x
        self.zc, self.yc, self.xc = z // 2, y // 2, x // 2
        self.states = self.zc >= 4
        self.far = self.zc == 4
        self.comb = self.yc >= 8
        assert self.states or self.zc <= 2
        assert self.comb or self.yc == 4
        self.used = y + 8 if self.comb else y + 16
        self.rows = y + 16
        self.fwd_planes = z if self.states else z + 10
        self.back = 0 if self.states else 5
        self.group = min(z, 8)

    def matrices(self):
        n, half = self.y, self.yc
        own, ahead, pick, direct = y_split_parts(n)
        fwd = np.zeros((n, self.used))
        fwd[:, :n] = own
        inv_own, behind, inv_pick, inv_direct = y_merge_parts(n)
        inv = np.zeros((n, self.used))
        inv[:, :n] = inv_own
        out = {"x_fwd": right_matrix(x_matrix(self.x)), "x_inv": right_matrix(x_matrix(self.x).T)}
        if self.comb:
            fwd[:, n : n + 5] = ahead
            inv[:, n : n + 5] = behind
            small = np.zeros((8, 16))
            small[:5, :10] = pick
            out["c_fwd"] = left_matrix(np.kron(np.eye(self.group), small))
            small = np.zeros((8, 16))
            small[:5, 3:8] = inv_pick[:, :5]
            small[:5, 11:16] = inv_pick[:, 5:]
            out["c_inv"] = left_matrix(np.kron(np.eye(self.group), small))
        else:
            fwd[:, n : n + 10] = direct
            for c in range(5):
                hop, at = (0, c - 1) if c else (1, half - 1)
                inv[:, n + hop * n + at] = inv_direct[:, c]
                inv[:, n + hop * n + half + at] = inv_direct[:, 5 + c]
        out["y_fwd"] = left_matrix(fwd * SCALE)
        out["y_inv"] = left_matrix(inv * SCALE)
        return out


def hop_list(length, rim):
    pieces = []
    done = 0
    hop = 1
    while done < rim:
        take = min(length, rim - done)
        pieces.append((hop, done, take))
        done += take
        hop += 1
    return pieces


def right_matrix(matrix):
    high, low = halves(matrix)
    return np.concatenate([high, high, low], axis=0)


def left_matrix(matrix):
    short = -matrix.shape[1] % 16
    high, low = halves(np.pad(matrix, ((0, 0), (0, short))))
    return np.concatenate([high, high, low], axis=1)


def split_product(data, right):
    high = data.astype(BF16)
    low = (data - high.astype(F32)).astype(BF16)
    depth = data.shape[1]
    if depth % 128:
        out = jnp.dot(high, right[0:depth], preferred_element_type=F32)
        out += jnp.dot(low, right[depth : 2 * depth], preferred_element_type=F32)
        return out + jnp.dot(high, right[2 * depth :], preferred_element_type=F32)
    wide = jnp.concatenate([high, low, high], axis=1)
    return jnp.dot(wide, right, preferred_element_type=F32)


def product_split(left, data):
    short = left.shape[1] // 3 - data.shape[0]
    if short:
        data = jnp.concatenate([data, jnp.zeros((short, data.shape[1]), F32)], axis=0)
    high = data.astype(BF16)
    low = (data - high.astype(F32)).astype(BF16)
    tall = jnp.concatenate([high, low, high], axis=0)
    return jnp.dot(left, tall, preferred_element_type=F32)


LATE = ("x_fwd0",)
SENDS = 96
LOADS = 8


def kernel(levels, nz, ny, names, *refs):
    r = dict(zip(names, refs))
    lv1 = levels[0]
    half = lv1.xc
    lanes_of = (slice(0, half), slice(half, lv1.x))
    gz = lax.axis_index("gz")
    gy = lax.axis_index("gy")

    def device(dz, dy):
        return (lax.rem(gz + (dz + nz) % nz, nz), lax.rem(gy + (dy + ny) % ny, ny))

    offsets = sorted(
        {(dz % nz, dy % ny) for dz in range(-5, 6) for dy in range(-2, 3)} - {(0, 0)}
    )
    barrier = pltpu.get_barrier_semaphore()
    for dz, dy in offsets:
        pl.semaphore_signal(barrier, inc=1, device_id=device(dz, dy), device_id_type=MESH)

    chunk = lv1.z // 4
    loads = [pltpu.make_async_copy(r["x_fwd0"], r["x_fwd0_v"], r["load_sem"].at[4])]
    for c in range(4):
        at = pl.ds(c * chunk, chunk)
        loads.append(
            pltpu.make_async_copy(r["field"].at[at], r["whole"].at[at], r["load_sem"].at[c])
        )
    loads.append(pltpu.make_async_copy(r["keep0"], r["keep0_v"], r["load_sem"].at[5]))
    for load in loads:
        load.start()

    used = [0]
    sends = []

    def send(src, dst, dz, dy):
        at = used[0]
        used[0] += 1
        copy = pltpu.make_async_remote_copy(
            src_ref=src,
            dst_ref=dst,
            send_sem=r["send_sem"].at[at],
            recv_sem=r["recv_sem"].at[at],
            device_id=device(dz, dy),
            device_id_type=MESH,
        )
        copy.start()
        sends.append(copy)
        return copy

    def loop(count, step, unroll=4):
        unroll = min(unroll, count)

        def several(i, carry):
            for n in range(unroll):
                step(i * unroll + n, 0)
            return carry

        if unroll == count:
            several(0, 0)
        else:
            lax.fori_loop(0, count // unroll, several, 0)

    def arrive(copies):
        for copy in copies:
            copy.wait_recv()

    fx = r["a0"]

    def x_split(lanes, first):
        for c in range(4):
            if first:
                loads[1 + c].wait()
                if c == 0:
                    loads[0].wait()
            at = pl.ds(c * chunk, chunk)
            rows = r["whole"][at].reshape(chunk * lv1.y, lv1.x)
            done = split_product(rows, r["x_fwd0_v"][:, lanes])
            fx[at, 0 : lv1.y, lanes] = done.reshape(chunk, lv1.y, half)

    def comb_forward(no, lanes=slice(None)):
        lv, a = levels[no], r[f"a{no}"]
        for start in range(0, lv.z, lv.group):
            at = slice(start, start + lv.group)
            rows = a[at, 0:16, lanes]
            wide = rows.shape[-1]
            done = product_split(r[f"c_fwd{no}"][...], rows.reshape(lv.group * 16, wide))
            a[at, lv.y + 8 : lv.y + 16, lanes] = done.reshape(lv.group, 8, wide)

    def row_of(tile, lv):
        return pl.multiple_of(jnp.where(tile < lv.y // 8, tile * 8, lv.y + 8), 8)

    def states_forward(no, lanes=slice(None)):
        lv, a, out = levels[no], r[f"a{no}"], r[f"fs{no}"]
        count = min(lv.zc, 5)

        def tile(t, carry):
            at = pl.ds(row_of(t, lv), 8)
            pairs = [
                lambda i=i: (a[2 * i, at, lanes], a[2 * i + 1, at, lanes]) for i in range(count)
            ]
            for k, value in enumerate(lattice_split(pairs)[1]):
                out[k, at, lanes] = value
            return carry

        lax.fori_loop(0, lv.y // 8 + 1, tile, 0)

    low, high = lanes_of
    x_split(low, True)
    comb_forward(0, low)
    states_forward(0, low)

    pl.semaphore_wait(barrier, len(offsets))

    def send_states(no, sign, lanes, own, comb):
        lv = levels[no]
        src, dst = (r[f"fs{no}"], r[f"fr{no}"]) if sign < 0 else (r[f"bs{no}"], r[f"br{no}"])
        far = 0 if sign < 0 else 4
        top, in_at = lv.y + 8, slice(lv.y, lv.y + 8)
        copies = []
        if own is not None:
            copies.append(send(src.at[0:5, own, lanes], dst.at[0:5, own, lanes], sign, 0))
            if lv.far:
                copies.append(
                    send(src.at[far, own, lanes], dst.at[5, own, lanes], 2 * sign, 0)
                )
        if comb:
            copies.append(
                send(src.at[0:5, top : top + 8, lanes], dst.at[0:5, in_at, lanes], sign, sign)
            )
            if lv.far:
                copies.append(
                    send(
                        src.at[far, top : top + 8, lanes], dst.at[5, in_at, lanes], 2 * sign, sign
                    )
                )
        return copies

    every = slice(None)

    def send_forward(no, lanes):
        lv, a = levels[no], r[f"a{no}"]
        copies = []
        if lv.states:
            copies += send_states(no, -1, lanes, slice(0, lv.y), True)
            pieces = [(0, 0, lv.z)]
        else:
            pieces = [(0, 0, lv.z)] + hop_list(lv.z, 10)
        for hz, z_at, take in pieces:
            z_to = 0 if hz == 0 else lv.z + z_at
            if hz:
                copies.append(
                    send(a.at[0:take, 0 : lv.y, lanes], a.at[z_to : z_to + take, 0 : lv.y, lanes], -hz, 0)
                )
            if lv.comb:
                copies.append(
                    send(
                        a.at[0:take, lv.y + 8 : lv.y + 16, lanes],
                        a.at[z_to : z_to + take, lv.y : lv.y + 8, lanes],
                        -hz,
                        -1,
                    )
                )
                continue
            for hy in (1, 2):
                if hy % ny:
                    copies.append(
                        send(
                            a.at[0:take, 0 : lv.y, lanes],
                            a.at[z_to : z_to + take, hy * lv.y : (hy + 1) * lv.y, lanes],
                            -hz,
                            -hy,
                        )
                    )
        return copies

    def own_wrap(no, a, lead):
        lv = levels[no]
        if not lv.comb and 2 % ny == 0:
            a[lead + (slice(2 * lv.y, 3 * lv.y),)] = a[lead + (slice(0, lv.y),)]

    def z_split(no, lanes):
        lv, a, out = levels[no], r[f"a{no}"], r[f"zx{no}"]
        tall = 8 if lv.states else lv.used

        def tile(t, carry):
            at = pl.ds(pl.multiple_of(t * 8, 8), 8) if lv.states else slice(0, tall)
            state = [None] * 5
            if lv.states:
                got = r[f"fr{no}"]
                state = [got[k, at, lanes] for k in range(5)]
                if lv.far:
                    state[4] = state[4] + far_weight(lattice_split, 0, 4, 4) * got[5, at, lanes]
            count = lv.zc if lv.states else lv.zc + 5
            pairs = [
                lambda i=i: (a[2 * i, at, lanes], a[2 * i + 1, at, lanes]) for i in range(count)
            ]
            outs = lattice_split(pairs, state)[0]
            for i in range(lv.zc):
                for bz in range(2):
                    out[bz, i, at, lanes] = outs[i][bz]
            return carry

        if lv.states:
            lax.fori_loop(0, lv.used // 8, tile, 0)
        else:
            tile(0, 0)

    def y_split(no, bands, lanes):
        lv, src, coef, mask = levels[no], r[f"zx{no}"], r[f"e{no}"], r[f"mask{no}"]
        low = lanes.start in (None, 0)

        def plane(i, carry):
            for bz in bands:
                mixed = product_split(r[f"y_fwd{no}"][...], src[bz, i, 0 : lv.used, lanes])
                coef[bz, lv.back + i, 0 : lv.y, lanes] = mixed * mask[bz, i, :, lanes]
                if bz == 0 and low and no < LEVELS - 1:
                    r[f"a{no + 1}"][i, 0 : lv.yc, :] = mixed[0 : lv.yc, 0 : lv.xc]
            return carry

        loop(lv.zc, plane)

    def comb_back(no, bands, lanes):
        lv, coef = levels[no], r[f"e{no}"]
        own = slice(lv.back, lv.back + lv.zc)
        planes = [(bz, lv.back + i) for bz in bands for i in range(lv.zc)]
        wide = lv.xc if no == 0 else lv.x
        for start in range(0, len(planes), lv.group):
            part = planes[start : start + lv.group]
            pieces = []
            for bz, i in part:
                pieces.append(coef[bz, i, lv.yc - 8 : lv.yc, lanes])
                pieces.append(coef[bz, i, 2 * lv.yc - 8 : 2 * lv.yc, lanes])
            done = product_split(r[f"c_inv{no}"][...], jnp.concatenate(pieces, axis=0))
            for n, (bz, i) in enumerate(part):
                coef[bz, i, lv.y + 8 : lv.y + 16, lanes] = done[8 * n : 8 * n + 8]

    def states_back(no, lanes, first, last):
        lv, coef, out = levels[no], r[f"e{no}"], r[f"bs{no}"]
        start = max(lv.zc - 5, 0)

        def tile(t, carry):
            at = pl.ds(row_of(t, lv), 8)
            pairs = [
                lambda i=i: (coef[0, i, at, lanes], coef[1, i, at, lanes])
                for i in range(start, lv.zc)
            ]
            for k, value in enumerate(lattice_merge(pairs)[1]):
                out[k, at, lanes] = value
            return carry

        lax.fori_loop(first, last, tile, 0)

    def send_rows_back(no, bands, lanes):
        lv, coef = levels[no], r[f"e{no}"]
        return [
            send(
                coef.at[bands, lv.back : lv.back + lv.zc, lv.y + 8 : lv.y + 16, lanes],
                coef.at[bands, lv.back : lv.back + lv.zc, lv.y : lv.y + 8, lanes],
                0,
                1,
            )
        ]

    def send_back(no):
        lv, coef = levels[no], r[f"e{no}"]
        copies = []
        if lv.states:
            copies += send_states(no, 1, every, slice(0, lv.y), True)
            return copies + send_rows_back(no, every, every)
        for hz, done, take in [(0, 0, lv.zc)] + hop_list(lv.zc, 5):
            src_at = slice(5 + lv.zc - take, 5 + lv.zc)
            dst_at = src_at if hz == 0 else slice(5 - done - take, 5 - done)
            if hz:
                copies.append(
                    send(coef.at[:, src_at, 0 : lv.y], coef.at[:, dst_at, 0 : lv.y], hz, 0)
                )
            if lv.comb:
                copies.append(
                    send(
                        coef.at[:, src_at, lv.y + 8 : lv.y + 16],
                        coef.at[:, dst_at, lv.y : lv.y + 8],
                        hz,
                        1,
                    )
                )
                continue
            for hy in (1, 2):
                if hy % ny:
                    copies.append(
                        send(
                            coef.at[:, src_at, 0 : lv.y],
                            coef.at[:, dst_at, hy * lv.y : (hy + 1) * lv.y],
                            hz,
                            hy,
                        )
                    )
        return copies

    def z_merge(no, lanes):
        lv, coef, out = levels[no], r[f"e{no}"], r[f"v{no}"]

        def tile(t, carry):
            at = pl.ds(pl.multiple_of(t * 8, 8), 8) if lv.states else slice(0, lv.used)
            state = [None] * 5
            if lv.states:
                got = r[f"br{no}"]
                state = [got[k, at, lanes] for k in range(5)]
                if lv.far:
                    state[0] = state[0] + far_weight(lattice_merge, 4, 0, 4) * got[5, at, lanes]
            pairs = [
                lambda i=i: (coef[0, i, at, lanes], coef[1, i, at, lanes])
                for i in range(lv.back + lv.zc)
            ]
            outs = lattice_merge(pairs, state)[0][lv.back :]
            for i in range(lv.zc):
                for p in range(2):
                    out[2 * i + p, at, lanes] = outs[i][p]
            return carry

        if lv.states:
            lax.fori_loop(0, lv.used // 8, tile, 0)
        else:
            tile(0, 0)

    def y_merge(no, lanes, out):
        lv, src = levels[no], r[f"v{no}"]

        def plane(z, carry):
            out[z, :, lanes] = product_split(r[f"y_inv{no}"][...], src[z, :, lanes])
            return carry

        loop(lv.z, plane)

    def fill_masks():
        loads[-1].wait()
        for no, lv in enumerate(levels):
            keep = r["keep0_v"] if no == 0 else r[f"keep{no}"]
            mask = r[f"mask{no}"]

            def fill(i, carry, lv=lv, keep=keep, mask=mask, no=no):
                for bz in range(2):
                    for by in range(2):
                        parts = []
                        for bx in range(2):
                            band = 4 * bz + 2 * by + bx
                            if band:
                                parts.append(keep[band - 1, i].astype(F32))
                            elif no == LEVELS - 1:
                                parts.append(r["coarse"][i].astype(F32))
                            else:
                                parts.append(jnp.zeros((lv.yc, lv.xc), F32))
                        at = slice(by * lv.yc, (by + 1) * lv.yc)
                        mask[bz, i, at, :] = jnp.concatenate(parts, axis=1)
                return carry

            lax.fori_loop(0, lv.zc, fill, 0)

    got = send_forward(0, low)
    x_split(high, False)
    comb_forward(0, high)
    states_forward(0, high)
    fill_masks()
    arrive(got)
    z_split(0, low)
    y_split(0, (0,), low)

    for no in range(1, LEVELS):
        lv = levels[no]
        if lv.comb:
            comb_forward(no)
        if lv.states:
            states_forward(no)
        got = send_forward(no, every)
        if no == 1:
            later = send_forward(0, high)
            y_split(0, (1,), low)
            comb_back(0, (1,), low)
        if no == 2:
            arrive(later)
            z_split(0, high)
            y_split(0, (0, 1), high)
        if no == 3:
            comb_back(0, (0, 1), high)
            states_back(0, high, 0, lv1.y // 8 + 1)
            states_back(0, low, lv1.yc // 8, lv1.y // 8)
        arrive(got)
        own_wrap(no, r[f"a{no}"], (every,))
        z_split(no, every)
        count = 2 * lv.zc
        rows = r[f"zx{no}"][...].reshape(count * lv.used, lv.x)
        done = split_product(rows, r[f"x_fwd{no}"][...])
        r[f"zx{no}"][...] = done.reshape(2, lv.zc, lv.used, lv.x)
        y_split(no, (0, 1), every)

    for no in range(LEVELS - 1, 0, -1):
        lv = levels[no]
        if lv.comb:
            comb_back(no, (0, 1), every)
        if lv.states:
            states_back(no, every, 0, lv.y // 8 + 1)
        got = send_back(no)
        if no == 3:
            early = send_states(0, 1, high, slice(0, lv1.y), True)
            early += send_rows_back(0, every, high)
        if no == 2:
            early_low = send_states(0, 1, low, slice(lv1.yc, lv1.y), False)
            early_low += send_rows_back(0, slice(1, 2), low)
        if no == 1:
            arrive(early)
            z_merge(0, high)
            y_merge(0, high, r["out"])
        arrive(got)
        own_wrap(no, r[f"e{no}"], (every, every))
        z_merge(no, every)
        y_merge(no, every, r[f"yv{no}"])
        rows = r[f"yv{no}"][...].reshape(lv.z * lv.y, lv.x)
        done = split_product(rows, r[f"x_inv{no}"][...]).reshape(lv.z, lv.y, lv.x)
        up = levels[no - 1]
        for p in range(2 if no == 0 else 1):
            r[f"e{no - 1}"][0, up.back : up.back + up.zc, 0 : up.yc, 0 : up.xc] = done

    comb_back(0, (0,), low)
    states_back(0, low, 0, lv1.yc // 8)
    states_back(0, low, lv1.y // 8, lv1.y // 8 + 1)
    got = send_states(0, 1, low, slice(0, lv1.yc), True)
    got += send_rows_back(0, slice(0, 1), low)
    arrive(early_low)
    arrive(got)
    z_merge(0, low)
    y_merge(0, low, r["out"])
    for copy in sends:
        copy.wait_send()
    assert used[0] <= SENDS


def last_kernel(v, pair, out):
    planes, y, x = v.shape
    rows = v[...].reshape(planes * y, x)
    out[...] = split_product(rows, pair[...]).reshape(planes, y, x)


def solution(mesh):
    nz, ny = mesh.shape["gz"], mesh.shape["gy"]

    def on_device(field, k1, k2, k3, k4, coarse):
        z, y, x = field.shape
        levels = [Level(z >> n, y >> n, x >> n) for n in range(LEVELS)]
        vmem = pl.BlockSpec(memory_space=pltpu.VMEM)
        hbm = pl.BlockSpec(memory_space=pl.ANY)
        names = ["field", "keep0", "keep1", "keep2", "keep3", "coarse"]
        operands = [field, k1, k2, k3, k4, coarse]
        specs = [hbm, hbm] + [vmem] * 4
        last = None
        for no, lv in enumerate(levels):
            for name, matrix in lv.matrices().items():
                if no == 0 and name == "x_inv":
                    last = jnp.asarray(matrix)
                    continue
                names.append(f"{name}{no}")
                operands.append(jnp.asarray(matrix))
                specs.append(hbm if f"{name}{no}" in LATE else vmem)
        names.append("out")
        scratch = {
            "whole": pltpu.VMEM((z, y, x), F32),
            "x_fwd0_v": pltpu.VMEM((3 * x, x), BF16),
            "keep0_v": pltpu.VMEM(k1.shape, jnp.int32),
        }
        for no, lv in enumerate(levels):
            scratch[f"a{no}"] = pltpu.VMEM((lv.fwd_planes, lv.rows, lv.x), F32)
            scratch[f"zx{no}"] = pltpu.VMEM((2, lv.zc, lv.used, lv.x), F32)
            scratch[f"e{no}"] = pltpu.VMEM((2, lv.back + lv.zc, lv.rows, lv.x), F32)
            scratch[f"v{no}"] = pltpu.VMEM((lv.z, lv.used, lv.x), F32)
            scratch[f"mask{no}"] = pltpu.VMEM((2, lv.zc, lv.y, lv.x), F32)
            if no:
                scratch[f"yv{no}"] = pltpu.VMEM((lv.z, lv.y, lv.x), F32)
            if lv.states:
                for name, planes in (("fs", 5), ("fr", 6), ("bs", 5), ("br", 6)):
                    scratch[f"{name}{no}"] = pltpu.VMEM((planes, lv.rows, lv.x), F32)
        scratch["load_sem"] = pltpu.SemaphoreType.DMA((LOADS,))
        scratch["send_sem"] = pltpu.SemaphoreType.DMA((SENDS,))
        scratch["recv_sem"] = pltpu.SemaphoreType.DMA((SENDS,))
        names += list(scratch)
        merged = pl.pallas_call(
            functools.partial(kernel, levels, nz, ny, names),
            out_shape=jax.ShapeDtypeStruct((z, y, x), F32),
            in_specs=specs,
            out_specs=vmem,
            scratch_shapes=list(scratch.values()),
            compiler_params=pltpu.CompilerParams(
                collective_id=0, has_side_effects=True, vmem_limit_bytes=56 * 1024 * 1024
            ),
        )(*operands)
        planes = z // 4
        block = pl.BlockSpec((planes, y, x), lambda i: (i, 0, 0))
        return pl.pallas_call(
            last_kernel,
            grid=(z // planes,),
            out_shape=jax.ShapeDtypeStruct((z, y, x), F32),
            in_specs=[block, vmem],
            out_specs=block,
            compiler_params=pltpu.CompilerParams(vmem_limit_bytes=48 * 1024 * 1024),
        )(merged, last)

    in_specs = (
        P("gz", "gy", None),
        P(None, "gz", "gy", None),
        P(None, "gz", "gy", None),
        P(None, "gz", "gy", None),
        P(None, "gz", "gy", None),
        P("gz", "gy", None),
    )
    return jax.shard_map(
        on_device, mesh=mesh, in_specs=in_specs, out_specs=P("gz", "gy", None), check_vma=False
    )
```

```python
import functools

import jax
import jax.numpy as jnp
import ml_dtypes
import numpy as np
from jax import lax
from jax.experimental import pallas as pl
from jax.experimental.pallas import tpu as pltpu
from jax.sharding import PartitionSpec as P

low_taps = (
    0.11154074335008017,
    0.4946238903983854,
    0.7511339080215775,
    0.3152503517092432,
    -0.22626469396516913,
    -0.12976686756709563,
    0.09750160558707936,
    0.02752286553001629,
    -0.031582039318031156,
    0.0005538422009938016,
    0.004777257511010651,
    -0.00107730108499558,
)
high_taps = tuple(((-1.0) ** k * low_taps[11 - k] for k in range(12)))
LEVELS = 4
MESH = pl.DeviceIdType.MESH
BF16 = jnp.bfloat16
F32 = jnp.float32


def rotations():
    h, g = low_taps, high_taps
    now = [np.array([[h[2 * m], h[2 * m + 1]], [g[2 * m], g[2 * m + 1]]]) for m in range(6)]
    found = []
    while len(now) > 1:
        row = now[0][np.argmax(np.linalg.norm(now[0], axis=1))]
        a, b = row / np.linalg.norm(row)
        turn = np.array([[a, b], [-b, a]])
        rest = [m @ turn.T for m in now]
        now = [np.stack([rest[m][:, 0], rest[m + 1][:, 1]], 1) for m in range(len(now) - 1)]
        found.append(turn)
    found.append(now[0])
    sizes = [np.abs(m).max() for m in found]
    return [m / s for m, s in zip(found, sizes)], float(np.prod(sizes))


TURNS, SCALE = rotations()


def mix(a, x, b, y):
    if x is None and y is None:
        return None
    terms = []
    for c, v in ((float(a), x), (float(b), y)):
        if v is not None:
            terms.append((c, v))
    if len(terms) == 1:
        c, v = terms[0]
        return v if c == 1.0 else -v if c == -1.0 else c * v
    (c, v), (d, w) = terms
    if abs(d) == 1.0:
        (c, v), (d, w) = (d, w), (c, v)
    if c == 1.0:
        return v + d * w
    if c == -1.0:
        return d * w - v
    return c * v + d * w


def turn(m, u, w):
    return mix(m[0, 0], u, m[0, 1], w), mix(m[1, 0], u, m[1, 1], w)


def lattice_split(pairs, state=(None,) * 5):
    state = list(state)
    outs = [None] * len(pairs)
    for i in reversed(range(len(pairs))):
        u, w = turn(TURNS[0], *pairs[i]())
        for k in range(1, 6):
            w, state[k - 1] = state[k - 1], w
            u, w = turn(TURNS[k], u, w)
        outs[i] = (u, w)
    return outs, state


def lattice_merge(pairs, state=(None,) * 5):
    state = list(state)
    outs = []
    for pair in pairs:
        u, w = turn(TURNS[5].T, *pair())
        for k in range(5, 0, -1):
            w, state[k - 1] = state[k - 1], w
            u, w = turn(TURNS[k - 1].T, u, w)
        outs.append((u, w))
    return outs, state


def far_weight(lattice, first, last, pairs):
    state = [None] * 5
    state[first] = np.float64(1.0)
    left = lattice([lambda: (None, None)] * pairs, state)[1]
    return float(left[last])


def halves(matrix):
    matrix = matrix.astype(np.float32)
    high = matrix.astype(ml_dtypes.bfloat16)
    low = (matrix - high.astype(np.float32)).astype(ml_dtypes.bfloat16)
    return np.stack([high, low])


def x_matrix(x_len):
    half = x_len // 2
    matrix = np.zeros((x_len, x_len))
    for i in range(half):
        for k in range(12):
            matrix[(2 * i + k) % x_len, i] += low_taps[k]
            matrix[(2 * i + k) % x_len, half + i] += high_taps[k]
    return matrix


def y_split_parts(n):
    half = n // 2
    whole = np.zeros((n, n + 10))
    for i in range(half):
        for k in range(12):
            whole[i, 2 * i + k] = low_taps[k]
            whole[half + i, 2 * i + k] = high_taps[k]
    left, size, right = np.linalg.svd(whole[:, n:])
    return whole[:, :n], left[:, :5] * size[:5], right[:5], whole[:, n:]


def y_merge_parts(n):
    half = n // 2
    own = np.zeros((n, n))
    back = np.zeros((n, 10))
    for j in range(n):
        for t in range(6):
            k = 2 * t + j % 2
            c = j // 2 - t
            if c >= 0:
                own[j, c] += low_taps[k]
                own[j, half + c] += high_taps[k]
            else:
                back[j, 5 + c] += low_taps[k]
                back[j, 10 + c] += high_taps[k]
    left, size, right = np.linalg.svd(back)
    return own, left[:, :5] * size[:5], right[:5], back


class Level:
    def __init__(self, z, y, x):
        self.z, self.y, self.x = z, y, x
        self.zc, self.yc, self.xc = z // 2, y // 2, x // 2
        self.states = self.zc >= 4
        self.far = self.zc == 4
        self.comb = self.yc >= 8
        assert self.states or self.zc <= 2
        assert self.comb or self.yc == 4
        self.used = y + 8 if self.comb else y + 16
        self.rows = y + 16
        self.fwd_planes = z if self.states else z + 10
        self.back = 0 if self.states else 5
        self.group = min(z, 8)

    def matrices(self):
        n, half = self.y, self.yc
        own, ahead, pick, direct = y_split_parts(n)
        fwd = np.zeros((n, self.used))
        fwd[:, :n] = own
        inv_own, behind, inv_pick, inv_direct = y_merge_parts(n)
        inv = np.zeros((n, self.used))
        inv[:, :n] = inv_own
        out = {"x_fwd": right_matrix(x_matrix(self.x)), "x_inv": right_matrix(x_matrix(self.x).T)}
        if self.comb:
            fwd[:, n : n + 5] = ahead
            inv[:, n : n + 5] = behind
            small = np.zeros((8, 16))
            small[:5, :10] = pick
            out["c_fwd"] = left_matrix(np.kron(np.eye(self.group), small))
            small = np.zeros((8, 16))
            small[:5, 3:8] = inv_pick[:, :5]
            small[:5, 11:16] = inv_pick[:, 5:]
            out["c_inv"] = left_matrix(np.kron(np.eye(self.group), small))
        else:
            fwd[:, n : n + 10] = direct
            for c in range(5):
                hop, at = (0, c - 1) if c else (1, half - 1)
                inv[:, n + hop * n + at] = inv_direct[:, c]
                inv[:, n + hop * n + half + at] = inv_direct[:, 5 + c]
        out["y_fwd"] = left_matrix(fwd * SCALE)
        out["y_inv"] = left_matrix(inv * SCALE)
        return out


def hop_list(length, rim):
    pieces = []
    done = 0
    hop = 1
    while done < rim:
        take = min(length, rim - done)
        pieces.append((hop, done, take))
        done += take
        hop += 1
    return pieces


def right_matrix(matrix):
    high, low = halves(matrix)
    return np.concatenate([high, high, low], axis=0)


def left_matrix(matrix):
    short = -matrix.shape[1] % 16
    high, low = halves(np.pad(matrix, ((0, 0), (0, short))))
    return np.concatenate([high, high, low], axis=1)


def split_product(data, right):
    high = data.astype(BF16)
    low = (data - high.astype(F32)).astype(BF16)
    depth = data.shape[1]
    if depth % 128:
        out = jnp.dot(high, right[0:depth], preferred_element_type=F32)
        out += jnp.dot(low, right[depth : 2 * depth], preferred_element_type=F32)
        return out + jnp.dot(high, right[2 * depth :], preferred_element_type=F32)
    wide = jnp.concatenate([high, low, high], axis=1)
    return jnp.dot(wide, right, preferred_element_type=F32)


def product_split(left, data):
    short = left.shape[1] // 3 - data.shape[0]
    if short:
        data = jnp.concatenate([data, jnp.zeros((short, data.shape[1]), F32)], axis=0)
    high = data.astype(BF16)
    low = (data - high.astype(F32)).astype(BF16)
    tall = jnp.concatenate([high, low, high], axis=0)
    return jnp.dot(left, tall, preferred_element_type=F32)


LATE = ("x_fwd0",)
SENDS = 96
LOADS = 8


def kernel(levels, nz, ny, names, *refs):
    r = dict(zip(names, refs))
    lv1 = levels[0]
    half = lv1.xc
    lanes_of = (slice(0, half), slice(half, lv1.x))
    gz = lax.axis_index("gz")
    gy = lax.axis_index("gy")

    def device(dz, dy):
        return (lax.rem(gz + (dz + nz) % nz, nz), lax.rem(gy + (dy + ny) % ny, ny))

    offsets = sorted(
        {(dz % nz, dy % ny) for dz in range(-5, 6) for dy in range(-2, 3)} - {(0, 0)}
    )
    barrier = pltpu.get_barrier_semaphore()
    for dz, dy in offsets:
        pl.semaphore_signal(barrier, inc=1, device_id=device(dz, dy), device_id_type=MESH)

    chunk = lv1.z // 4
    loads = [pltpu.make_async_copy(r["x_fwd0"], r["x_fwd0_v"], r["load_sem"].at[4])]
    for c in range(4):
        at = pl.ds(c * chunk, chunk)
        loads.append(
            pltpu.make_async_copy(r["field"].at[at], r["whole"].at[at], r["load_sem"].at[c])
        )
    loads.append(pltpu.make_async_copy(r["keep0"], r["keep0_v"], r["load_sem"].at[5]))
    for load in loads:
        load.start()

    used = [0]
    sends = []

    def send(src, dst, dz, dy):
        at = used[0]
        used[0] += 1
        copy = pltpu.make_async_remote_copy(
            src_ref=src,
            dst_ref=dst,
            send_sem=r["send_sem"].at[at],
            recv_sem=r["recv_sem"].at[at],
            device_id=device(dz, dy),
            device_id_type=MESH,
        )
        copy.start()
        sends.append(copy)
        return copy

    def loop(count, step, unroll=4):
        unroll = min(unroll, count)

        def several(i, carry):
            for n in range(unroll):
                step(i * unroll + n, 0)
            return carry

        if unroll == count:
            several(0, 0)
        else:
            lax.fori_loop(0, count // unroll, several, 0)

    def arrive(copies):
        for copy in copies:
            copy.wait_recv()

    fx = r["a0"]

    def x_split(lanes, first):
        for c in range(4):
            if first:
                loads[1 + c].wait()
                if c == 0:
                    loads[0].wait()
            at = pl.ds(c * chunk, chunk)
            rows = r["whole"][at].reshape(chunk * lv1.y, lv1.x)
            done = split_product(rows, r["x_fwd0_v"][:, lanes])
            fx[at, 0 : lv1.y, lanes] = done.reshape(chunk, lv1.y, half)

    def comb_forward(no, lanes=slice(None)):
        lv, a = levels[no], r[f"a{no}"]
        for start in range(0, lv.z, lv.group):
            at = slice(start, start + lv.group)
            rows = a[at, 0:16, lanes]
            wide = rows.shape[-1]
            done = product_split(r[f"c_fwd{no}"][...], rows.reshape(lv.group * 16, wide))
            a[at, lv.y + 8 : lv.y + 16, lanes] = done.reshape(lv.group, 8, wide)

    def row_of(tile, lv):
        return pl.multiple_of(jnp.where(tile < lv.y // 8, tile * 8, lv.y + 8), 8)

    def states_forward(no, lanes=slice(None)):
        lv, a, out = levels[no], r[f"a{no}"], r[f"fs{no}"]
        count = min(lv.zc, 5)

        def tile(t, carry):
            at = pl.ds(row_of(t, lv), 8)
            pairs = [
                lambda i=i: (a[2 * i, at, lanes], a[2 * i + 1, at, lanes]) for i in range(count)
            ]
            for k, value in enumerate(lattice_split(pairs)[1]):
                out[k, at, lanes] = value
            return carry

        lax.fori_loop(0, lv.y // 8 + 1, tile, 0)

    low, high = lanes_of
    x_split(low, True)
    comb_forward(0, low)
    states_forward(0, low)

    pl.semaphore_wait(barrier, len(offsets))

    def send_states(no, sign, lanes, own, comb):
        lv = levels[no]
        src, dst = (r[f"fs{no}"], r[f"fr{no}"]) if sign < 0 else (r[f"bs{no}"], r[f"br{no}"])
        far = 0 if sign < 0 else 4
        top, in_at = lv.y + 8, slice(lv.y, lv.y + 8)
        copies = []
        if own is not None:
            copies.append(send(src.at[0:5, own, lanes], dst.at[0:5, own, lanes], sign, 0))
            if lv.far:
                copies.append(
                    send(src.at[far, own, lanes], dst.at[5, own, lanes], 2 * sign, 0)
                )
        if comb:
            copies.append(
                send(src.at[0:5, top : top + 8, lanes], dst.at[0:5, in_at, lanes], sign, sign)
            )
            if lv.far:
                copies.append(
                    send(
                        src.at[far, top : top + 8, lanes], dst.at[5, in_at, lanes], 2 * sign, sign
                    )
                )
        return copies

    every = slice(None)

    def send_forward(no, lanes):
        lv, a = levels[no], r[f"a{no}"]
        copies = []
        if lv.states:
            copies += send_states(no, -1, lanes, slice(0, lv.y), True)
            pieces = [(0, 0, lv.z)]
        else:
            pieces = [(0, 0, lv.z)] + hop_list(lv.z, 10)
        for hz, z_at, take in pieces:
            z_to = 0 if hz == 0 else lv.z + z_at
            if hz:
                copies.append(
                    send(a.at[0:take, 0 : lv.y, lanes], a.at[z_to : z_to + take, 0 : lv.y, lanes], -hz, 0)
                )
            if lv.comb:
                copies.append(
                    send(
                        a.at[0:take, lv.y + 8 : lv.y + 16, lanes],
                        a.at[z_to : z_to + take, lv.y : lv.y + 8, lanes],
                        -hz,
                        -1,
                    )
                )
                continue
            for hy in (1, 2):
                if hy % ny:
                    copies.append(
                        send(
                            a.at[0:take, 0 : lv.y, lanes],
                            a.at[z_to : z_to + take, hy * lv.y : (hy + 1) * lv.y, lanes],
                            -hz,
                            -hy,
                        )
                    )
        return copies

    def own_wrap(no, a, lead):
        lv = levels[no]
        if not lv.comb and 2 % ny == 0:
            a[lead + (slice(2 * lv.y, 3 * lv.y),)] = a[lead + (slice(0, lv.y),)]

    def z_split(no, lanes):
        lv, a, out = levels[no], r[f"a{no}"], r[f"zx{no}"]
        tall = 8 if lv.states else lv.used

        def tile(t, carry):
            at = pl.ds(pl.multiple_of(t * 8, 8), 8) if lv.states else slice(0, tall)
            state = [None] * 5
            if lv.states:
                got = r[f"fr{no}"]
                state = [got[k, at, lanes] for k in range(5)]
                if lv.far:
                    state[4] = state[4] + far_weight(lattice_split, 0, 4, 4) * got[5, at, lanes]
            count = lv.zc if lv.states else lv.zc + 5
            pairs = [
                lambda i=i: (a[2 * i, at, lanes], a[2 * i + 1, at, lanes]) for i in range(count)
            ]
            outs = lattice_split(pairs, state)[0]
            for i in range(lv.zc):
                for bz in range(2):
                    out[bz, i, at, lanes] = outs[i][bz]
            return carry

        if lv.states:
            lax.fori_loop(0, lv.used // 8, tile, 0)
        else:
            tile(0, 0)

    def y_split(no, bands, lanes):
        lv, src, coef, mask = levels[no], r[f"zx{no}"], r[f"e{no}"], r[f"mask{no}"]
        low = lanes.start in (None, 0)

        def plane(i, carry):
            for bz in bands:
                mixed = product_split(r[f"y_fwd{no}"][...], src[bz, i, 0 : lv.used, lanes])
                coef[bz, lv.back + i, 0 : lv.y, lanes] = mixed * mask[bz, i, :, lanes]
                if bz == 0 and low and no < LEVELS - 1:
                    r[f"a{no + 1}"][i, 0 : lv.yc, :] = mixed[0 : lv.yc, 0 : lv.xc]
            return carry

        loop(lv.zc, plane)

    def comb_back(no, bands, lanes):
        lv, coef = levels[no], r[f"e{no}"]
        own = slice(lv.back, lv.back + lv.zc)
        planes = [(bz, lv.back + i) for bz in bands for i in range(lv.zc)]
        wide = lv.xc if no == 0 else lv.x
        for start in range(0, len(planes), lv.group):
            part = planes[start : start + lv.group]
            pieces = []
            for bz, i in part:
                pieces.append(coef[bz, i, lv.yc - 8 : lv.yc, lanes])
                pieces.append(coef[bz, i, 2 * lv.yc - 8 : 2 * lv.yc, lanes])
            done = product_split(r[f"c_inv{no}"][...], jnp.concatenate(pieces, axis=0))
            for n, (bz, i) in enumerate(part):
                coef[bz, i, lv.y + 8 : lv.y + 16, lanes] = done[8 * n : 8 * n + 8]

    def states_back(no, lanes, first, last):
        lv, coef, out = levels[no], r[f"e{no}"], r[f"bs{no}"]
        start = max(lv.zc - 5, 0)

        def tile(t, carry):
            at = pl.ds(row_of(t, lv), 8)
            pairs = [
                lambda i=i: (coef[0, i, at, lanes], coef[1, i, at, lanes])
                for i in range(start, lv.zc)
            ]
            for k, value in enumerate(lattice_merge(pairs)[1]):
                out[k, at, lanes] = value
            return carry

        lax.fori_loop(first, last, tile, 0)

    def send_rows_back(no, bands, lanes):
        lv, coef = levels[no], r[f"e{no}"]
        return [
            send(
                coef.at[bands, lv.back : lv.back + lv.zc, lv.y + 8 : lv.y + 16, lanes],
                coef.at[bands, lv.back : lv.back + lv.zc, lv.y : lv.y + 8, lanes],
                0,
                1,
            )
        ]

    def send_back(no):
        lv, coef = levels[no], r[f"e{no}"]
        copies = []
        if lv.states:
            copies += send_states(no, 1, every, slice(0, lv.y), True)
            return copies + send_rows_back(no, every, every)
        for hz, done, take in [(0, 0, lv.zc)] + hop_list(lv.zc, 5):
            src_at = slice(5 + lv.zc - take, 5 + lv.zc)
            dst_at = src_at if hz == 0 else slice(5 - done - take, 5 - done)
            if hz:
                copies.append(
                    send(coef.at[:, src_at, 0 : lv.y], coef.at[:, dst_at, 0 : lv.y], hz, 0)
                )
            if lv.comb:
                copies.append(
                    send(
                        coef.at[:, src_at, lv.y + 8 : lv.y + 16],
                        coef.at[:, dst_at, lv.y : lv.y + 8],
                        hz,
                        1,
                    )
                )
                continue
            for hy in (1, 2):
                if hy % ny:
                    copies.append(
                        send(
                            coef.at[:, src_at, 0 : lv.y],
                            coef.at[:, dst_at, hy * lv.y : (hy + 1) * lv.y],
                            hz,
                            hy,
                        )
                    )
        return copies

    def z_merge(no, lanes):
        lv, coef, out = levels[no], r[f"e{no}"], r[f"v{no}"]

        def tile(t, carry):
            at = pl.ds(pl.multiple_of(t * 8, 8), 8) if lv.states else slice(0, lv.used)
            state = [None] * 5
            if lv.states:
                got = r[f"br{no}"]
                state = [got[k, at, lanes] for k in range(5)]
                if lv.far:
                    state[0] = state[0] + far_weight(lattice_merge, 4, 0, 4) * got[5, at, lanes]
            pairs = [
                lambda i=i: (coef[0, i, at, lanes], coef[1, i, at, lanes])
                for i in range(lv.back + lv.zc)
            ]
            outs = lattice_merge(pairs, state)[0][lv.back :]
            for i in range(lv.zc):
                for p in range(2):
                    out[2 * i + p, at, lanes] = outs[i][p]
            return carry

        if lv.states:
            lax.fori_loop(0, lv.used // 8, tile, 0)
        else:
            tile(0, 0)

    def y_merge(no, lanes, out):
        lv, src = levels[no], r[f"v{no}"]

        def plane(z, carry):
            out[z, :, lanes] = product_split(r[f"y_inv{no}"][...], src[z, :, lanes])
            return carry

        loop(lv.z, plane)

    def fill_masks():
        loads[-1].wait()
        for no, lv in enumerate(levels):
            keep = r["keep0_v"] if no == 0 else r[f"keep{no}"]
            mask = r[f"mask{no}"]

            def fill(i, carry, lv=lv, keep=keep, mask=mask, no=no):
                for bz in range(2):
                    for by in range(2):
                        parts = []
                        for bx in range(2):
                            band = 4 * bz + 2 * by + bx
                            if band:
                                parts.append(keep[band - 1, i].astype(F32))
                            elif no == LEVELS - 1:
                                parts.append(r["coarse"][i].astype(F32))
                            else:
                                parts.append(jnp.zeros((lv.yc, lv.xc), F32))
                        at = slice(by * lv.yc, (by + 1) * lv.yc)
                        mask[bz, i, at, :] = jnp.concatenate(parts, axis=1)
                return carry

            lax.fori_loop(0, lv.zc, fill, 0)

    got = send_forward(0, low)
    x_split(high, False)
    comb_forward(0, high)
    states_forward(0, high)
    fill_masks()
    arrive(got)
    z_split(0, low)
    y_split(0, (0,), low)

    for no in range(1, LEVELS):
        lv = levels[no]
        if lv.comb:
            comb_forward(no)
        if lv.states:
            states_forward(no)
        got = send_forward(no, every)
        if no == 1:
            later = send_forward(0, high)
            y_split(0, (1,), low)
            comb_back(0, (1,), low)
        if no == 2:
            arrive(later)
            z_split(0, high)
            y_split(0, (0, 1), high)
        if no == 3:
            comb_back(0, (0, 1), high)
            states_back(0, high, 0, lv1.y // 8 + 1)
            states_back(0, low, lv1.yc // 8, lv1.y // 8)
        arrive(got)
        own_wrap(no, r[f"a{no}"], (every,))
        z_split(no, every)
        count = 2 * lv.zc
        rows = r[f"zx{no}"][...].reshape(count * lv.used, lv.x)
        done = split_product(rows, r[f"x_fwd{no}"][...])
        r[f"zx{no}"][...] = done.reshape(2, lv.zc, lv.used, lv.x)
        y_split(no, (0, 1), every)

    for no in range(LEVELS - 1, 0, -1):
        lv = levels[no]
        if lv.comb:
            comb_back(no, (0, 1), every)
        if lv.states:
            states_back(no, every, 0, lv.y // 8 + 1)
        got = send_back(no)
        if no == 3:
            early = send_states(0, 1, high, slice(0, lv1.y), True)
            early += send_rows_back(0, every, high)
        if no == 2:
            early_low = send_states(0, 1, low, slice(lv1.yc, lv1.y), False)
            early_low += send_rows_back(0, slice(1, 2), low)
        if no == 1:
            arrive(early)
            z_merge(0, high)
            y_merge(0, high, r["out"])
        arrive(got)
        own_wrap(no, r[f"e{no}"], (every, every))
        z_merge(no, every)
        y_merge(no, every, r[f"yv{no}"])
        rows = r[f"yv{no}"][...].reshape(lv.z * lv.y, lv.x)
        done = split_product(rows, r[f"x_inv{no}"][...]).reshape(lv.z, lv.y, lv.x)
        up = levels[no - 1]
        for p in range(2 if no == 0 else 1):
            r[f"e{no - 1}"][0, up.back : up.back + up.zc, 0 : up.yc, 0 : up.xc] = done

    comb_back(0, (0,), low)
    states_back(0, low, 0, lv1.yc // 8)
    states_back(0, low, lv1.y // 8, lv1.y // 8 + 1)
    got = send_states(0, 1, low, slice(0, lv1.yc), True)
    got += send_rows_back(0, slice(0, 1), low)
    arrive(early_low)
    arrive(got)
    z_merge(0, low)
    y_merge(0, low, r["out"])
    for copy in sends:
        copy.wait_send()
    assert used[0] <= SENDS


def last_kernel(v, pair, out):
    planes, y, x = v.shape
    rows = v[...].reshape(planes * y, x)
    out[...] = split_product(rows, pair[...]).reshape(planes, y, x)


def solution(mesh):
    nz, ny = mesh.shape["gz"], mesh.shape["gy"]

    def on_device(field, k1, k2, k3, k4, coarse):
        z, y, x = field.shape
        levels = [Level(z >> n, y >> n, x >> n) for n in range(LEVELS)]
        vmem = pl.BlockSpec(memory_space=pltpu.VMEM)
        hbm = pl.BlockSpec(memory_space=pl.ANY)
        names = ["field", "keep0", "keep1", "keep2", "keep3", "coarse"]
        operands = [field, k1, k2, k3, k4, coarse]
        specs = [hbm, hbm] + [vmem] * 4
        last = None
        for no, lv in enumerate(levels):
            for name, matrix in lv.matrices().items():
                if no == 0 and name == "x_inv":
                    last = jnp.asarray(matrix)
                    continue
                names.append(f"{name}{no}")
                operands.append(jnp.asarray(matrix))
                specs.append(hbm if f"{name}{no}" in LATE else vmem)
        names.append("out")
        scratch = {
            "whole": pltpu.VMEM((z, y, x), F32),
            "x_fwd0_v": pltpu.VMEM((3 * x, x), BF16),
            "keep0_v": pltpu.VMEM(k1.shape, jnp.int32),
        }
        for no, lv in enumerate(levels):
            scratch[f"a{no}"] = pltpu.VMEM((lv.fwd_planes, lv.rows, lv.x), F32)
            scratch[f"zx{no}"] = pltpu.VMEM((2, lv.zc, lv.used, lv.x), F32)
            scratch[f"e{no}"] = pltpu.VMEM((2, lv.back + lv.zc, lv.rows, lv.x), F32)
            scratch[f"v{no}"] = pltpu.VMEM((lv.z, lv.used, lv.x), F32)
            scratch[f"mask{no}"] = pltpu.VMEM((2, lv.zc, lv.y, lv.x), F32)
            if no:
                scratch[f"yv{no}"] = pltpu.VMEM((lv.z, lv.y, lv.x), F32)
            if lv.states:
                for name, planes in (("fs", 5), ("fr", 6), ("bs", 5), ("br", 6)):
                    scratch[f"{name}{no}"] = pltpu.VMEM((planes, lv.rows, lv.x), F32)
        scratch["load_sem"] = pltpu.SemaphoreType.DMA((LOADS,))
        scratch["send_sem"] = pltpu.SemaphoreType.DMA((SENDS,))
        scratch["recv_sem"] = pltpu.SemaphoreType.DMA((SENDS,))
        names += list(scratch)
        merged = pl.pallas_call(
            functools.partial(kernel, levels, nz, ny, names),
            out_shape=jax.ShapeDtypeStruct((z, y, x), F32),
            in_specs=specs,
            out_specs=vmem,
            scratch_shapes=list(scratch.values()),
            compiler_params=pltpu.CompilerParams(
                collective_id=0, has_side_effects=True, vmem_limit_bytes=36 * 1024 * 1024
            ),
        )(*[pltpu.with_memory_space_constraint(o, pltpu.HBM) for o in operands])
        planes = z // 4
        block = pl.BlockSpec((planes, y, x), lambda i: (i, 0, 0))
        return pl.pallas_call(
            last_kernel,
            grid=(z // planes,),
            out_shape=jax.ShapeDtypeStruct((z, y, x), F32),
            in_specs=[block, vmem],
            out_specs=block,
            compiler_params=pltpu.CompilerParams(vmem_limit_bytes=48 * 1024 * 1024),
        )(merged, last)

    in_specs = (
        P("gz", "gy", None),
        P(None, "gz", "gy", None),
        P(None, "gz", "gy", None),
        P(None, "gz", "gy", None),
        P(None, "gz", "gy", None),
        P("gz", "gy", None),
    )
    return jax.shard_map(
        on_device, mesh=mesh, in_specs=in_specs, out_specs=P("gz", "gy", None), check_vma=False
    )
```

```python
import functools

import jax
import jax.numpy as jnp
import ml_dtypes
import numpy as np
from jax import lax
from jax.experimental import pallas as pl
from jax.experimental.pallas import tpu as pltpu
from jax.sharding import PartitionSpec as P

low_taps = (
    0.11154074335008017,
    0.4946238903983854,
    0.7511339080215775,
    0.3152503517092432,
    -0.22626469396516913,
    -0.12976686756709563,
    0.09750160558707936,
    0.02752286553001629,
    -0.031582039318031156,
    0.0005538422009938016,
    0.004777257511010651,
    -0.00107730108499558,
)
high_taps = tuple(((-1.0) ** k * low_taps[11 - k] for k in range(12)))
LEVELS = 4
MESH = pl.DeviceIdType.MESH
BF16 = jnp.bfloat16
F32 = jnp.float32


def rotations():
    h, g = low_taps, high_taps
    now = [np.array([[h[2 * m], h[2 * m + 1]], [g[2 * m], g[2 * m + 1]]]) for m in range(6)]
    found = []
    while len(now) > 1:
        row = now[0][np.argmax(np.linalg.norm(now[0], axis=1))]
        a, b = row / np.linalg.norm(row)
        turn = np.array([[a, b], [-b, a]])
        rest = [m @ turn.T for m in now]
        now = [np.stack([rest[m][:, 0], rest[m + 1][:, 1]], 1) for m in range(len(now) - 1)]
        found.append(turn)
    found.append(now[0])
    sizes = [np.abs(m).max() for m in found]
    return [m / s for m, s in zip(found, sizes)], float(np.prod(sizes))


TURNS, SCALE = rotations()


def mix(a, x, b, y):
    if x is None and y is None:
        return None
    terms = []
    for c, v in ((float(a), x), (float(b), y)):
        if v is not None:
            terms.append((c, v))
    if len(terms) == 1:
        c, v = terms[0]
        return v if c == 1.0 else -v if c == -1.0 else c * v
    (c, v), (d, w) = terms
    if abs(d) == 1.0:
        (c, v), (d, w) = (d, w), (c, v)
    if c == 1.0:
        return v + d * w
    if c == -1.0:
        return d * w - v
    return c * v + d * w


def turn(m, u, w):
    return mix(m[0, 0], u, m[0, 1], w), mix(m[1, 0], u, m[1, 1], w)


def lattice_split(pairs, state=(None,) * 5):
    state = list(state)
    outs = [None] * len(pairs)
    for i in reversed(range(len(pairs))):
        u, w = turn(TURNS[0], *pairs[i]())
        for k in range(1, 6):
            w, state[k - 1] = state[k - 1], w
            u, w = turn(TURNS[k], u, w)
        outs[i] = (u, w)
    return outs, state


def lattice_merge(pairs, state=(None,) * 5):
    state = list(state)
    outs = []
    for pair in pairs:
        u, w = turn(TURNS[5].T, *pair())
        for k in range(5, 0, -1):
            w, state[k - 1] = state[k - 1], w
            u, w = turn(TURNS[k - 1].T, u, w)
        outs.append((u, w))
    return outs, state


def far_weight(lattice, first, last, pairs):
    state = [None] * 5
    state[first] = np.float64(1.0)
    left = lattice([lambda: (None, None)] * pairs, state)[1]
    return float(left[last])


def halves(matrix):
    matrix = matrix.astype(np.float32)
    high = matrix.astype(ml_dtypes.bfloat16)
    low = (matrix - high.astype(np.float32)).astype(ml_dtypes.bfloat16)
    return np.stack([high, low])


def x_matrix(x_len):
    half = x_len // 2
    matrix = np.zeros((x_len, x_len))
    for i in range(half):
        for k in range(12):
            matrix[(2 * i + k) % x_len, i] += low_taps[k]
            matrix[(2 * i + k) % x_len, half + i] += high_taps[k]
    return matrix


def y_split_parts(n):
    half = n // 2
    whole = np.zeros((n, n + 10))
    for i in range(half):
        for k in range(12):
            whole[i, 2 * i + k] = low_taps[k]
            whole[half + i, 2 * i + k] = high_taps[k]
    left, size, right = np.linalg.svd(whole[:, n:])
    return whole[:, :n], left[:, :5] * size[:5], right[:5]


def y_merge_parts(n):
    half = n // 2
    own = np.zeros((n, n))
    back = np.zeros((n, 10))
    for j in range(n):
        for t in range(6):
            k = 2 * t + j % 2
            c = j // 2 - t
            if c >= 0:
                own[j, c] += low_taps[k]
                own[j, half + c] += high_taps[k]
            else:
                back[j, 5 + c] += low_taps[k]
                back[j, 10 + c] += high_taps[k]
    left, size, right = np.linalg.svd(back)
    return own, left[:, :5] * size[:5], right[:5]


def distinct(offsets, n):
    found = []
    for o in sorted(offsets, key=abs):
        if all((o - p) % n for p in found):
            found.append(o)
    return sorted(found)


AHEAD, BEHIND = 5, 8


class Last:
    def __init__(self, z, y, x, ny):
        assert z == 2 and y == 8
        self.z, self.y, self.x = z, y, x
        self.zc, self.yc, self.xc = 1, 4, x // 2
        self.ny = ny
        self.columns = distinct(range(-2, 3), ny)
        self.kept = distinct(range(-2, 1), ny)
        self.in_rows, self.out_rows = 8 * len(self.columns), 8 * len(self.kept)
        self.z_own, self.y_own = 2 * BEHIND, 8 * self.columns.index(0)
        self.k_own = 8 * self.kept.index(0)

    def slot(self, found, o):
        return [(o - p) % self.ny == 0 for p in found].index(True)

    def matrices(self):
        fwd = np.zeros((self.out_rows, self.in_rows))
        for s, c in enumerate(self.kept):
            for i in range(4):
                for k in range(12):
                    at = 8 * c + 2 * i + k
                    col = 8 * self.slot(self.columns, at // 8) + at % 8
                    fwd[8 * s + i, col] += low_taps[k]
                    fwd[8 * s + 4 + i, col] += high_taps[k]
        inv = np.zeros((16, self.out_rows))
        for j in range(-5, 8):
            for t in range(6):
                k = 2 * t + j % 2
                c = j // 2 - t
                col = 8 * self.slot(self.kept, c // 4) + c % 4
                inv[8 + j, col] += low_taps[k]
                inv[8 + j, col + 4] += high_taps[k]
        return {
            "x_fwd": right_matrix(x_matrix(self.x)),
            "x_inv": right_matrix(x_matrix(self.x).T),
            "y_fwd": left_matrix(np.kron(np.eye(6), fwd * SCALE)),
            "y_inv": left_matrix(np.kron(np.eye(8), inv * SCALE)),
        }


class Level:
    z_own = y_own = 0

    def __init__(self, z, y, x):
        self.z, self.y, self.x = z, y, x
        self.zc, self.yc, self.xc = z // 2, y // 2, x // 2
        self.states = self.zc >= 4
        self.far = self.zc == 4
        self.comb = self.yc >= 8
        assert self.states or self.zc <= 2
        assert self.comb
        self.used = y + 8
        self.rows = y + 16
        self.fwd_planes = z if self.states else z + 10
        self.back = 0 if self.states else 5
        self.group = min(z, 8)

    def matrices(self):
        n, half = self.y, self.yc
        own, ahead, pick = y_split_parts(n)
        fwd = np.zeros((n, self.used))
        fwd[:, :n] = own
        inv_own, behind, inv_pick = y_merge_parts(n)
        inv = np.zeros((n, self.used))
        inv[:, :n] = inv_own
        out = {"x_fwd": right_matrix(x_matrix(self.x)), "x_inv": right_matrix(x_matrix(self.x).T)}
        if self.comb:
            fwd[:, n : n + 5] = ahead
            inv[:, n : n + 5] = behind
            small = np.zeros((8, 16))
            small[:5, :10] = pick
            out["c_fwd"] = left_matrix(np.kron(np.eye(self.group), small))
            small = np.zeros((8, 16))
            small[:5, 3:8] = inv_pick[:, :5]
            small[:5, 11:16] = inv_pick[:, 5:]
            out["c_inv"] = left_matrix(np.kron(np.eye(self.group), small))
            if self.yc == 8:
                out["c_low"] = left_matrix(np.kron(np.eye(8), small[:, :8]))
        out["y_fwd"] = left_matrix(fwd * SCALE)
        out["y_inv"] = left_matrix(inv * SCALE)
        return out


def hop_list(length, rim):
    pieces = []
    done = 0
    hop = 1
    while done < rim:
        take = min(length, rim - done)
        pieces.append((hop, done, take))
        done += take
        hop += 1
    return pieces


def right_matrix(matrix):
    high, low = halves(matrix)
    return np.concatenate([high, high, low], axis=0)


def left_matrix(matrix):
    short = -matrix.shape[1] % 16
    high, low = halves(np.pad(matrix, ((0, 0), (0, short))))
    return np.concatenate([high, high, low], axis=1)


def split_product(data, right):
    high = data.astype(BF16)
    low = (data - high.astype(F32)).astype(BF16)
    depth = data.shape[1]
    if depth % 128:
        out = jnp.dot(high, right[0:depth], preferred_element_type=F32)
        out += jnp.dot(low, right[depth : 2 * depth], preferred_element_type=F32)
        return out + jnp.dot(high, right[2 * depth :], preferred_element_type=F32)
    wide = jnp.concatenate([high, low, high], axis=1)
    return jnp.dot(wide, right, preferred_element_type=F32)


def product_split(left, data):
    short = left.shape[1] // 3 - data.shape[0]
    if short:
        data = jnp.concatenate([data, jnp.zeros((short, data.shape[1]), F32)], axis=0)
    high = data.astype(BF16)
    low = (data - high.astype(F32)).astype(BF16)
    tall = jnp.concatenate([high, low, high], axis=0)
    return jnp.dot(left, tall, preferred_element_type=F32)


LATE = ("x_fwd0", "x_inv0")
SENDS = 192
LOADS = 8


def kernel(levels, nz, ny, names, *refs):
    r = dict(zip(names, refs))
    lv1 = levels[0]
    half = lv1.xc
    lanes_of = (slice(0, half), slice(half, lv1.x))
    gz = lax.axis_index("gz")
    gy = lax.axis_index("gy")

    def device(dz, dy):
        return (lax.rem(gz + (dz + nz) % nz, nz), lax.rem(gy + (dy + ny) % ny, ny))

    offsets = sorted(
        {(dz % nz, dy % ny) for dz in range(-8, 9) for dy in range(-2, 3)} - {(0, 0)}
    )
    barrier = pltpu.get_barrier_semaphore()
    for dz, dy in offsets:
        pl.semaphore_signal(barrier, inc=1, device_id=device(dz, dy), device_id_type=MESH)

    chunk = lv1.z // 4
    loads = [pltpu.make_async_copy(r["x_fwd0"], r["x_fwd0_v"], r["load_sem"].at[4])]
    for c in range(4):
        at = pl.ds(c * chunk, chunk)
        loads.append(
            pltpu.make_async_copy(r["field"].at[at], r["whole"].at[at], r["load_sem"].at[c])
        )
    loads.append(pltpu.make_async_copy(r["keep0"], r["keep0_v"], r["load_sem"].at[5]))
    loads.append(pltpu.make_async_copy(r["x_inv0"], r["x_inv0_v"], r["load_sem"].at[6]))
    for load in loads:
        load.start()

    used = [0]
    sends = []

    def send(src, dst, dz, dy):
        at = used[0]
        used[0] += 1
        copy = pltpu.make_async_remote_copy(
            src_ref=src,
            dst_ref=dst,
            send_sem=r["send_sem"].at[at],
            recv_sem=r["recv_sem"].at[at],
            device_id=device(dz, dy),
            device_id_type=MESH,
        )
        copy.start()
        sends.append(copy)
        return copy

    def loop(count, step, unroll=4):
        unroll = min(unroll, count)

        def several(i, carry):
            for n in range(unroll):
                step(i * unroll + n, 0)
            return carry

        if unroll == count:
            several(0, 0)
        else:
            lax.fori_loop(0, count // unroll, several, 0)

    def arrive(copies):
        for copy in copies:
            copy.wait_recv()

    fx = r["a0"]

    def x_split(lanes, first):
        for c in range(4):
            if first:
                loads[1 + c].wait()
                if c == 0:
                    loads[0].wait()
            at = pl.ds(c * chunk, chunk)
            rows = r["whole"][at].reshape(chunk * lv1.y, lv1.x)
            done = split_product(rows, r["x_fwd0_v"][:, lanes])
            fx[at, 0 : lv1.y, lanes] = done.reshape(chunk, lv1.y, half)

    def comb_forward(no, lanes=slice(None)):
        lv, a = levels[no], r[f"a{no}"]
        for start in range(0, lv.z, lv.group):
            at = slice(start, start + lv.group)
            rows = a[at, 0:16, lanes]
            wide = rows.shape[-1]
            done = product_split(r[f"c_fwd{no}"][...], rows.reshape(lv.group * 16, wide))
            a[at, lv.y + 8 : lv.y + 16, lanes] = done.reshape(lv.group, 8, wide)

    def row_of(tile, lv):
        return pl.multiple_of(jnp.where(tile < lv.y // 8, tile * 8, lv.y + 8), 8)

    def states_forward(no, lanes=slice(None)):
        lv, a, out = levels[no], r[f"a{no}"], r[f"fs{no}"]
        count = min(lv.zc, 5)

        def tile(t, carry):
            at = pl.ds(row_of(t, lv), 8)
            pairs = [
                lambda i=i: (a[2 * i, at, lanes], a[2 * i + 1, at, lanes]) for i in range(count)
            ]
            for k, value in enumerate(lattice_split(pairs)[1]):
                out[k, at, lanes] = value
            return carry

        lax.fori_loop(0, lv.y // 8 + 1, tile, 0)

    low, high = lanes_of
    x_split(low, True)
    comb_forward(0, low)
    states_forward(0, low)

    pl.semaphore_wait(barrier, len(offsets))

    def send_states(no, sign, lanes, own, comb):
        lv = levels[no]
        src, dst = (r[f"fs{no}"], r[f"fr{no}"]) if sign < 0 else (r[f"bs{no}"], r[f"br{no}"])
        far = 0 if sign < 0 else 4
        top, in_at = lv.y + 8, slice(lv.y, lv.y + 8)
        copies = []
        if own is not None:
            copies.append(send(src.at[0:5, own, lanes], dst.at[0:5, own, lanes], sign, 0))
            if lv.far:
                copies.append(
                    send(src.at[far, own, lanes], dst.at[5, own, lanes], 2 * sign, 0)
                )
        if comb:
            copies.append(
                send(src.at[0:5, top : top + 8, lanes], dst.at[0:5, in_at, lanes], sign, sign)
            )
            if lv.far:
                copies.append(
                    send(
                        src.at[far, top : top + 8, lanes], dst.at[5, in_at, lanes], 2 * sign, sign
                    )
                )
        return copies

    every = slice(None)

    def send_forward(no, lanes):
        lv, a = levels[no], r[f"a{no}"]
        copies = []
        if lv.states:
            copies += send_states(no, -1, lanes, slice(0, lv.y), True)
            pieces = [(0, 0, lv.z)]
        else:
            pieces = [(0, 0, lv.z)] + hop_list(lv.z, 10)
        for hz, z_at, take in pieces:
            z_to = 0 if hz == 0 else lv.z + z_at
            if hz:
                copies.append(
                    send(a.at[0:take, 0 : lv.y, lanes], a.at[z_to : z_to + take, 0 : lv.y, lanes], -hz, 0)
                )
            copies.append(
                send(
                    a.at[0:take, lv.y + 8 : lv.y + 16, lanes],
                    a.at[z_to : z_to + take, lv.y : lv.y + 8, lanes],
                    -hz,
                    -1,
                )
            )
        return copies

    def z_split(no, lanes):
        lv, a, out = levels[no], r[f"a{no}"], r[f"zx{no}"]
        tall = 8 if lv.states else lv.used

        def tile(t, carry):
            at = pl.ds(pl.multiple_of(t * 8, 8), 8) if lv.states else slice(0, tall)
            state = [None] * 5
            if lv.states:
                got = r[f"fr{no}"]
                state = [got[k, at, lanes] for k in range(5)]
                if lv.far:
                    state[4] = state[4] + far_weight(lattice_split, 0, 4, 4) * got[5, at, lanes]
            count = lv.zc if lv.states else lv.zc + 5
            pairs = [
                lambda i=i: (a[2 * i, at, lanes], a[2 * i + 1, at, lanes]) for i in range(count)
            ]
            outs = lattice_split(pairs, state)[0]
            for i in range(lv.zc):
                for bz in range(2):
                    out[bz, i, at, lanes] = outs[i][bz]
            return carry

        if lv.states:
            lax.fori_loop(0, lv.used // 8, tile, 0)
        else:
            tile(0, 0)

    def y_split(no, bands, lanes):
        lv, src, coef, mask = levels[no], r[f"zx{no}"], r[f"e{no}"], r[f"mask{no}"]
        low = lanes.start in (None, 0)

        def plane(i, carry):
            for bz in bands:
                mixed = product_split(r[f"y_fwd{no}"][...], src[bz, i, 0 : lv.used, lanes])
                coef[bz, lv.back + i, 0 : lv.y, lanes] = mixed * mask[bz, i, :, lanes]
                if bz == 0 and low and no < LEVELS - 1:
                    down = levels[no + 1]
                    at = slice(down.y_own, down.y_own + lv.yc)
                    r[f"a{no + 1}"][down.z_own + i, at, :] = mixed[0 : lv.yc, 0 : lv.xc]
            return carry

        loop(lv.zc, plane)

    def comb_back(no, bands, lanes):
        lv, coef = levels[no], r[f"e{no}"]
        own = slice(lv.back, lv.back + lv.zc)
        planes = [(bz, lv.back + i) for bz in bands for i in range(lv.zc)]
        wide = lv.xc if no == 0 else lv.x
        for start in range(0, len(planes), lv.group):
            part = planes[start : start + lv.group]
            pieces = []
            for bz, i in part:
                pieces.append(coef[bz, i, lv.yc - 8 : lv.yc, lanes])
                pieces.append(coef[bz, i, 2 * lv.yc - 8 : 2 * lv.yc, lanes])
            done = product_split(r[f"c_inv{no}"][...], jnp.concatenate(pieces, axis=0))
            for n, (bz, i) in enumerate(part):
                coef[bz, i, lv.y + 8 : lv.y + 16, lanes] = done[8 * n : 8 * n + 8]

    def states_back(no, lanes, first, last):
        lv, coef, out = levels[no], r[f"e{no}"], r[f"bs{no}"]
        start = max(lv.zc - 5, 0)

        def tile(t, carry):
            at = pl.ds(row_of(t, lv), 8)
            pairs = [
                lambda i=i: (coef[0, i, at, lanes], coef[1, i, at, lanes])
                for i in range(start, lv.zc)
            ]
            for k, value in enumerate(lattice_merge(pairs)[1]):
                out[k, at, lanes] = value
            return carry

        lax.fori_loop(first, last, tile, 0)

    def send_rows_back(no, bands, lanes):
        lv, coef = levels[no], r[f"e{no}"]
        return [
            send(
                coef.at[bands, lv.back : lv.back + lv.zc, lv.y + 8 : lv.y + 16, lanes],
                coef.at[bands, lv.back : lv.back + lv.zc, lv.y : lv.y + 8, lanes],
                0,
                1,
            )
        ]

    def send_back(no):
        lv, coef = levels[no], r[f"e{no}"]
        copies = []
        if lv.states:
            copies += send_states(no, 1, every, slice(0, lv.y), True)
            return copies + send_rows_back(no, every, every)
        for hz, done, take in [(0, 0, lv.zc)] + hop_list(lv.zc, 5):
            src_at = slice(5 + lv.zc - take, 5 + lv.zc)
            dst_at = src_at if hz == 0 else slice(5 - done - take, 5 - done)
            if hz:
                copies.append(
                    send(coef.at[:, src_at, 0 : lv.y], coef.at[:, dst_at, 0 : lv.y], hz, 0)
                )
            copies.append(
                send(
                    coef.at[:, src_at, lv.y + 8 : lv.y + 16],
                    coef.at[:, dst_at, lv.y : lv.y + 8],
                    hz,
                    1,
                )
            )
        return copies

    def z_merge(no, lanes):
        lv, coef, out = levels[no], r[f"e{no}"], r[f"v{no}"]

        def tile(t, carry):
            at = pl.ds(pl.multiple_of(t * 8, 8), 8) if lv.states else slice(0, lv.used)
            state = [None] * 5
            if lv.states:
                got = r[f"br{no}"]
                state = [got[k, at, lanes] for k in range(5)]
                if lv.far:
                    state[0] = state[0] + far_weight(lattice_merge, 4, 0, 4) * got[5, at, lanes]
            pairs = [
                lambda i=i: (coef[0, i, at, lanes], coef[1, i, at, lanes])
                for i in range(lv.back + lv.zc)
            ]
            outs = lattice_merge(pairs, state)[0][lv.back :]
            for i in range(lv.zc):
                for p in range(2):
                    out[2 * i + p, at, lanes] = outs[i][p]
            return carry

        if lv.states:
            lax.fori_loop(0, lv.used // 8, tile, 0)
        else:
            tile(0, 0)

    def y_merge(no, lanes, out):
        lv, src = levels[no], r[f"v{no}"]

        def plane(z, carry):
            out[z, :, lanes] = product_split(r[f"y_inv{no}"][...], src[z, :, lanes])
            return carry

        loop(lv.z, plane)

    def fill_masks():
        loads[-2].wait()
        for no, lv in enumerate(levels):
            keep = r["keep0_v"] if no == 0 else r[f"keep{no}"]
            mask = r[f"mask{no}"]

            def fill(i, carry, lv=lv, keep=keep, mask=mask, no=no):
                for bz in range(2):
                    for by in range(2):
                        parts = []
                        for bx in range(2):
                            band = 4 * bz + 2 * by + bx
                            if band:
                                parts.append(keep[band - 1, i].astype(F32))
                            elif no == LEVELS - 1:
                                parts.append(r["coarse"][i].astype(F32))
                            else:
                                parts.append(jnp.zeros((lv.yc, lv.xc), F32))
                        first, z_first = by * lv.yc, 0
                        if no == LEVELS - 1:
                            first, z_first = first + lv.k_own, BEHIND
                        at = slice(first, first + lv.yc)
                        mask[bz, z_first + i, at, :] = jnp.concatenate(parts, axis=1)
                return carry

            lax.fori_loop(0, lv.zc, fill, 0)

    got = send_forward(0, low)
    x_split(high, False)
    comb_forward(0, high)
    states_forward(0, high)
    fill_masks()
    arrive(got)
    z_split(0, low)
    y_split(0, (0,), low)

    last = levels[LEVELS - 1]
    edge = levels[LEVELS - 2]

    def gather(buf, lead, block, span, columns, own):
        copies = []
        for dz in range(-BEHIND, span + 1):
            for c, dy in enumerate(columns):
                if dz == 0 and dy == 0:
                    continue
                mine = slice(BEHIND * block, BEHIND * block + block)
                there = slice((BEHIND + dz) * block, (BEHIND + dz) * block + block)
                src = buf.at[lead + (mine, slice(own, own + 8))]
                dst = buf.at[lead + (there, slice(8 * c, 8 * c + 8))]
                copies.append(send(src, dst, -dz, -dy))
        return copies

    def last_level():
        no = LEVELS - 1
        a, zx, coef, v = r[f"a{no}"], r[f"zx{no}"], r[f"e{no}"], r[f"v{no}"]
        count = BEHIND + 1
        for t in range(last.in_rows // 8):
            at = slice(8 * t, 8 * t + 8)
            pairs = [
                lambda i=i: (a[2 * i, at, :], a[2 * i + 1, at, :]) for i in range(count + AHEAD)
            ]
            outs = lattice_split(pairs)[0]
            for i in range(count):
                for bz in range(2):
                    zx[bz * count + i, at, :] = outs[i][bz]
        rows = zx[...].reshape(2 * count * last.in_rows, last.x)
        done = split_product(rows, r[f"x_fwd{no}"][...])
        for g in range(2 * count // 6):
            part = done[6 * g * last.in_rows : 6 * (g + 1) * last.in_rows]
            mixed = product_split(r[f"y_fwd{no}"][...], part)
            mask = r[f"mask{no}"]
            for n in range(6):
                bz, i = divmod(6 * g + n, count)
                piece = mixed[n * last.out_rows : (n + 1) * last.out_rows]
                coef[bz, i] = piece * mask[bz, i]
        for t in range(last.out_rows // 8):
            at = slice(8 * t, 8 * t + 8)
            pairs = [lambda i=i: (coef[0, i, at, :], coef[1, i, at, :]) for i in range(count)]
            outs = lattice_merge(pairs)[0][count - 4 :]
            for i in range(4):
                for p in range(2):
                    v[2 * i + p, at, :] = outs[i][p]
        rows = v[...].reshape(8 * last.out_rows, last.x)
        done = product_split(r[f"y_inv{no}"][...], rows)
        return split_product(done, r[f"x_inv{no}"][...]).reshape(8, 16, last.x)

    def place_last(value):
        coef, planes = r[f"e{LEVELS - 2}"], edge.back + edge.zc
        coef[0, :, 0 : edge.yc, 0 : edge.xc] = value[8 - planes :, 8:16]
        done = product_split(r[f"c_low{LEVELS - 2}"][...], value[:, 0:8].reshape(64, last.x))
        done = done.reshape(8, 8, last.x)[8 - planes :]
        rim = slice(edge.y, edge.y + 8)
        coef[0, :, rim, 0 : edge.xc] = coef[0, :, rim, 0 : edge.xc] + done

    for no in range(1, LEVELS - 1):
        lv = levels[no]
        comb_forward(no)
        if lv.states:
            states_forward(no)
        got = send_forward(no, every)
        if no == 1:
            later = send_forward(0, high)
            y_split(0, (1,), low)
            comb_back(0, (1,), low)
        if no == 2:
            mask_got = gather(
                r[f"mask{LEVELS - 1}"], (every,), 1, 0, last.kept, last.k_own
            )
            arrive(later)
            z_split(0, high)
            y_split(0, (0, 1), high)
        arrive(got)
        z_split(no, every)
        count = 2 * lv.zc
        rows = r[f"zx{no}"][...].reshape(count * lv.used, lv.x)
        done = split_product(rows, r[f"x_fwd{no}"][...])
        r[f"zx{no}"][...] = done.reshape(2, lv.zc, lv.used, lv.x)
        y_split(no, (0, 1), every)

    got = gather(r[f"a{LEVELS - 1}"], (), 2, AHEAD, last.columns, last.y_own)
    comb_back(LEVELS - 2, (0, 1), every)
    edge_got = send_back(LEVELS - 2)
    comb_back(0, (0, 1), high)
    states_back(0, high, 0, lv1.y // 8 + 1)
    states_back(0, low, lv1.yc // 8, lv1.y // 8)
    arrive(mask_got)
    arrive(got)
    value = last_level()
    arrive(edge_got)
    for copy in edge_got:
        copy.wait_send()
    done_ids = [id(copy) for copy in edge_got]
    sends[:] = [copy for copy in sends if id(copy) not in done_ids]
    place_last(value)

    for no in range(LEVELS - 2, 0, -1):
        lv = levels[no]
        if no < LEVELS - 2:
            comb_back(no, (0, 1), every)
            states_back(no, every, 0, lv.y // 8 + 1)
            got = send_back(no)
            early = send_states(0, 1, high, slice(0, lv1.y), True)
            early += send_rows_back(0, every, high)
            early_low = send_states(0, 1, low, slice(lv1.yc, lv1.y), False)
            early_low += send_rows_back(0, slice(1, 2), low)
            arrive(got)
        z_merge(no, every)
        y_merge(no, every, r[f"yv{no}"])
        rows = r[f"yv{no}"][...].reshape(lv.z * lv.y, lv.x)
        done = split_product(rows, r[f"x_inv{no}"][...]).reshape(lv.z, lv.y, lv.x)
        up = levels[no - 1]
        r[f"e{no - 1}"][0, up.back : up.back + up.zc, 0 : up.yc, 0 : up.xc] = done

    comb_back(0, (0,), low)
    states_back(0, low, 0, lv1.yc // 8)
    states_back(0, low, lv1.y // 8, lv1.y // 8 + 1)
    got = send_states(0, 1, low, slice(0, lv1.yc), True)
    got += send_rows_back(0, slice(0, 1), low)
    arrive(early)
    z_merge(0, high)
    y_merge(0, high, r["yv0"])
    loads[-1].wait()

    def x_part(c):
        at = pl.ds(c * chunk, chunk)
        rows = r["yv0"][at, :, high].reshape(chunk * lv1.y, half)
        r["part"][at] = split_product(rows, r["x_inv0_v"][...]).reshape(chunk, lv1.y, lv1.x)

    for c in range(4):
        x_part(c)
    arrive(early_low)
    arrive(got)
    z_merge(0, low)
    y_merge(0, low, r["out"])
    for copy in sends:
        copy.wait_send()
    assert used[0] <= SENDS


def last_kernel(v, part, right, out, whole, sem):
    planes, y, x = part.shape
    half = x // 2
    copies = []
    for n in range(2):
        lanes = slice(n * half, (n + 1) * half)
        rows = v[...].reshape(planes * y, half)
        done = split_product(rows, right[:, lanes]).reshape(planes, y, half)
        whole[:, :, lanes] = done + part[:, :, lanes]
        copies.append(pltpu.make_async_copy(whole.at[:, :, lanes], out.at[:, :, lanes], sem.at[n]))
        copies[-1].start()
    for copy in copies:
        copy.wait()


def solution(mesh):
    nz, ny = mesh.shape["gz"], mesh.shape["gy"]

    def on_device(field, k1, k2, k3, k4, coarse):
        z, y, x = field.shape
        levels = [Level(z >> n, y >> n, x >> n) for n in range(LEVELS - 1)]
        levels.append(Last(z >> 3, y >> 3, x >> 3, ny))
        vmem = pl.BlockSpec(memory_space=pltpu.VMEM)
        hbm = pl.BlockSpec(memory_space=pl.ANY)
        names = ["field", "keep0", "keep1", "keep2", "keep3", "coarse"]
        operands = [field, k1, k2, k3, k4, coarse]
        specs = [hbm, hbm] + [vmem] * 4
        last = None
        for no, lv in enumerate(levels):
            for name, matrix in lv.matrices().items():
                if no == 0 and name == "x_inv":
                    whole = x_matrix(x).T
                    last = jnp.asarray(right_matrix(whole[: x // 2]))
                    matrix = right_matrix(whole[x // 2 :])
                names.append(f"{name}{no}")
                operands.append(jnp.asarray(matrix))
                specs.append(hbm if f"{name}{no}" in LATE else vmem)
        names += ["out", "part"]
        scratch = {
            "whole": pltpu.VMEM((z, y, x), F32),
            "x_fwd0_v": pltpu.VMEM((3 * x, x), BF16),
            "x_inv0_v": pltpu.VMEM((3 * x // 2, x), BF16),
            "yv0": pltpu.VMEM((z, y, x), F32),
            "keep0_v": pltpu.VMEM(k1.shape, jnp.int32),
        }
        end = levels[-1]
        pairs = BEHIND + 1
        last_shapes = {
            "a": (2 * (pairs + AHEAD), end.in_rows),
            "zx": (2 * pairs, end.in_rows),
            "e": (2, pairs, end.out_rows),
            "v": (8, end.out_rows),
            "mask": (2, pairs, end.out_rows),
        }
        for name, shape in last_shapes.items():
            scratch[f"{name}{LEVELS - 1}"] = pltpu.VMEM(shape + (end.x,), F32)
        for no, lv in enumerate(levels[:-1]):
            scratch[f"a{no}"] = pltpu.VMEM((lv.fwd_planes, lv.rows, lv.x), F32)
            scratch[f"zx{no}"] = pltpu.VMEM((2, lv.zc, lv.used, lv.x), F32)
            scratch[f"e{no}"] = pltpu.VMEM((2, lv.back + lv.zc, lv.rows, lv.x), F32)
            scratch[f"v{no}"] = pltpu.VMEM((lv.z, lv.used, lv.x), F32)
            scratch[f"mask{no}"] = pltpu.VMEM((2, lv.zc, lv.y, lv.x), F32)
            if no:
                scratch[f"yv{no}"] = pltpu.VMEM((lv.z, lv.y, lv.x), F32)
            if lv.states:
                for name, planes in (("fs", 5), ("fr", 6), ("bs", 5), ("br", 6)):
                    scratch[f"{name}{no}"] = pltpu.VMEM((planes, lv.rows, lv.x), F32)
        scratch["load_sem"] = pltpu.SemaphoreType.DMA((LOADS,))
        scratch["send_sem"] = pltpu.SemaphoreType.DMA((SENDS,))
        scratch["recv_sem"] = pltpu.SemaphoreType.DMA((SENDS,))
        names += list(scratch)
        merged, part = pl.pallas_call(
            functools.partial(kernel, levels, nz, ny, names),
            out_shape=[
                jax.ShapeDtypeStruct((z, y, x // 2), F32),
                jax.ShapeDtypeStruct((z, y, x), F32),
            ],
            in_specs=specs,
            out_specs=[vmem, vmem],
            scratch_shapes=list(scratch.values()),
            compiler_params=pltpu.CompilerParams(
                collective_id=0, has_side_effects=True, vmem_limit_bytes=36 * 1024 * 1024
            ),
        )(*[pltpu.with_memory_space_constraint(o, pltpu.HBM) for o in operands])
        return pl.pallas_call(
            last_kernel,
            out_shape=jax.ShapeDtypeStruct((z, y, x), F32),
            in_specs=[vmem] * 3,
            out_specs=hbm,
            scratch_shapes=[pltpu.VMEM((z, y, x), F32), pltpu.SemaphoreType.DMA((2,))],
            compiler_params=pltpu.CompilerParams(vmem_limit_bytes=48 * 1024 * 1024),
        )(merged, part, last)

    in_specs = (
        P("gz", "gy", None),
        P(None, "gz", "gy", None),
        P(None, "gz", "gy", None),
        P(None, "gz", "gy", None),
        P(None, "gz", "gy", None),
        P("gz", "gy", None),
    )
    return jax.shard_map(
        on_device, mesh=mesh, in_specs=in_specs, out_specs=P("gz", "gy", None), check_vma=False
    )
```

```python
import functools

import jax
import jax.numpy as jnp
import ml_dtypes
import numpy as np
from jax import lax
from jax.experimental import pallas as pl
from jax.experimental.pallas import tpu as pltpu
from jax.sharding import PartitionSpec as P

low_taps = (
    0.11154074335008017,
    0.4946238903983854,
    0.7511339080215775,
    0.3152503517092432,
    -0.22626469396516913,
    -0.12976686756709563,
    0.09750160558707936,
    0.02752286553001629,
    -0.031582039318031156,
    0.0005538422009938016,
    0.004777257511010651,
    -0.00107730108499558,
)
high_taps = tuple(((-1.0) ** k * low_taps[11 - k] for k in range(12)))
LEVELS = 4
MESH = pl.DeviceIdType.MESH
BF16 = jnp.bfloat16
F32 = jnp.float32


def rotations():
    h, g = low_taps, high_taps
    now = [np.array([[h[2 * m], h[2 * m + 1]], [g[2 * m], g[2 * m + 1]]]) for m in range(6)]
    found = []
    while len(now) > 1:
        row = now[0][np.argmax(np.linalg.norm(now[0], axis=1))]
        a, b = row / np.linalg.norm(row)
        turn = np.array([[a, b], [-b, a]])
        rest = [m @ turn.T for m in now]
        now = [np.stack([rest[m][:, 0], rest[m + 1][:, 1]], 1) for m in range(len(now) - 1)]
        found.append(turn)
    found.append(now[0])
    sizes = [np.abs(m).max() for m in found]
    return [m / s for m, s in zip(found, sizes)], float(np.prod(sizes))


TURNS, SCALE = rotations()


def mix(a, x, b, y):
    if x is None and y is None:
        return None
    terms = []
    for c, v in ((float(a), x), (float(b), y)):
        if v is not None:
            terms.append((c, v))
    if len(terms) == 1:
        c, v = terms[0]
        return v if c == 1.0 else -v if c == -1.0 else c * v
    (c, v), (d, w) = terms
    if abs(d) == 1.0:
        (c, v), (d, w) = (d, w), (c, v)
    if c == 1.0:
        return v + d * w
    if c == -1.0:
        return d * w - v
    return c * v + d * w


def turn(m, u, w):
    return mix(m[0, 0], u, m[0, 1], w), mix(m[1, 0], u, m[1, 1], w)


def lattice_split(pairs, state=(None,) * 5):
    state = list(state)
    outs = [None] * len(pairs)
    for i in reversed(range(len(pairs))):
        u, w = turn(TURNS[0], *pairs[i]())
        for k in range(1, 6):
            w, state[k - 1] = state[k - 1], w
            u, w = turn(TURNS[k], u, w)
        outs[i] = (u, w)
    return outs, state


def lattice_merge(pairs, state=(None,) * 5):
    state = list(state)
    outs = []
    for pair in pairs:
        u, w = turn(TURNS[5].T, *pair())
        for k in range(5, 0, -1):
            w, state[k - 1] = state[k - 1], w
            u, w = turn(TURNS[k - 1].T, u, w)
        outs.append((u, w))
    return outs, state


def far_weight(lattice, first, last, pairs):
    state = [None] * 5
    state[first] = np.float64(1.0)
    left = lattice([lambda: (None, None)] * pairs, state)[1]
    return float(left[last])


def halves(matrix):
    matrix = matrix.astype(np.float32)
    high = matrix.astype(ml_dtypes.bfloat16)
    low = (matrix - high.astype(np.float32)).astype(ml_dtypes.bfloat16)
    return np.stack([high, low])


def x_matrix(x_len):
    half = x_len // 2
    matrix = np.zeros((x_len, x_len))
    for i in range(half):
        for k in range(12):
            matrix[(2 * i + k) % x_len, i] += low_taps[k]
            matrix[(2 * i + k) % x_len, half + i] += high_taps[k]
    return matrix


def y_split_parts(n):
    half = n // 2
    whole = np.zeros((n, n + 10))
    for i in range(half):
        for k in range(12):
            whole[i, 2 * i + k] = low_taps[k]
            whole[half + i, 2 * i + k] = high_taps[k]
    left, size, right = np.linalg.svd(whole[:, n:])
    return whole[:, :n], left[:, :5] * size[:5], right[:5]


def y_merge_parts(n):
    half = n // 2
    own = np.zeros((n, n))
    back = np.zeros((n, 10))
    for j in range(n):
        for t in range(6):
            k = 2 * t + j % 2
            c = j // 2 - t
            if c >= 0:
                own[j, c] += low_taps[k]
                own[j, half + c] += high_taps[k]
            else:
                back[j, 5 + c] += low_taps[k]
                back[j, 10 + c] += high_taps[k]
    left, size, right = np.linalg.svd(back)
    return own, left[:, :5] * size[:5], right[:5]


def distinct(offsets, n):
    found = []
    for o in sorted(offsets, key=abs):
        if all((o - p) % n for p in found):
            found.append(o)
    return sorted(found)


AHEAD, BEHIND = 5, 8


class Last:
    def __init__(self, z, y, x, ny):
        assert z == 2 and y == 8
        self.z, self.y, self.x = z, y, x
        self.zc, self.yc, self.xc = 1, 4, x // 2
        self.ny = ny
        self.columns = distinct(range(-2, 3), ny)
        self.kept = distinct(range(-2, 1), ny)
        self.in_rows, self.out_rows = 8 * len(self.columns), 8 * len(self.kept)
        self.z_own, self.y_own = 2 * BEHIND, 8 * self.columns.index(0)
        self.k_own = 8 * self.kept.index(0)

    def slot(self, found, o):
        return [(o - p) % self.ny == 0 for p in found].index(True)

    def matrices(self):
        fwd = np.zeros((self.out_rows, self.in_rows))
        for s, c in enumerate(self.kept):
            for i in range(4):
                for k in range(12):
                    at = 8 * c + 2 * i + k
                    col = 8 * self.slot(self.columns, at // 8) + at % 8
                    fwd[8 * s + i, col] += low_taps[k]
                    fwd[8 * s + 4 + i, col] += high_taps[k]
        inv = np.zeros((16, self.out_rows))
        for j in range(-5, 8):
            for t in range(6):
                k = 2 * t + j % 2
                c = j // 2 - t
                col = 8 * self.slot(self.kept, c // 4) + c % 4
                inv[8 + j, col] += low_taps[k]
                inv[8 + j, col + 4] += high_taps[k]
        return {
            "x_fwd": right_matrix(x_matrix(self.x)),
            "x_inv": right_matrix(x_matrix(self.x).T),
            "y_fwd": left_matrix(np.kron(np.eye(6), fwd * SCALE)),
            "y_inv": left_matrix(np.kron(np.eye(8), inv * SCALE)),
        }


class Level:
    z_own = y_own = 0

    def __init__(self, z, y, x):
        self.z, self.y, self.x = z, y, x
        self.zc, self.yc, self.xc = z // 2, y // 2, x // 2
        self.states = self.zc >= 4
        self.far = self.zc == 4
        self.comb = self.yc >= 8
        assert self.states or self.zc <= 2
        assert self.comb
        self.used = y + 8
        self.rows = y + 16
        self.fwd_planes = z if self.states else z + 10
        self.back = 0 if self.states else 5
        self.group = min(z, 8)
        self.back_group = max(min(self.zc, 8), 4)

    def matrices(self):
        n, half = self.y, self.yc
        own, ahead, pick = y_split_parts(n)
        fwd = np.zeros((n, self.used))
        fwd[:, :n] = own
        inv_own, behind, inv_pick = y_merge_parts(n)
        inv = np.zeros((n, self.used))
        inv[:, :n] = inv_own
        out = {"x_fwd": right_matrix(x_matrix(self.x)), "x_inv": right_matrix(x_matrix(self.x).T)}
        if self.comb:
            fwd[:, n : n + 5] = ahead
            inv[:, n : n + 5] = behind
            small = np.zeros((8, 16))
            small[:5, :10] = pick
            out["c_fwd"] = left_matrix(np.kron(np.eye(self.group), small))
            small = np.zeros((8, 16))
            small[:5, 3:8] = inv_pick[:, :5]
            small[:5, 11:16] = inv_pick[:, 5:]
            out["c_inv"] = left_matrix(np.kron(np.eye(self.back_group), small))
            if self.yc == 8:
                out["c_low"] = left_matrix(np.kron(np.eye(8), small[:, :8]))
        out["y_fwd"] = left_matrix(fwd * SCALE)
        out["y_inv"] = left_matrix(inv * SCALE)
        return out


def hop_list(length, rim):
    pieces = []
    done = 0
    hop = 1
    while done < rim:
        take = min(length, rim - done)
        pieces.append((hop, done, take))
        done += take
        hop += 1
    return pieces


def right_matrix(matrix):
    high, low = halves(matrix)
    return np.concatenate([high, high, low], axis=0)


def left_matrix(matrix):
    short = -matrix.shape[1] % 16
    high, low = halves(np.pad(matrix, ((0, 0), (0, short))))
    return np.concatenate([high, high, low], axis=1)


def split_product(data, right):
    high = data.astype(BF16)
    low = (data - high.astype(F32)).astype(BF16)
    depth = data.shape[1]
    if depth % 128:
        out = jnp.dot(high, right[0:depth], preferred_element_type=F32)
        out += jnp.dot(low, right[depth : 2 * depth], preferred_element_type=F32)
        return out + jnp.dot(high, right[2 * depth :], preferred_element_type=F32)
    wide = jnp.concatenate([high, low, high], axis=1)
    return jnp.dot(wide, right, preferred_element_type=F32)


def product_split(left, data):
    short = left.shape[1] // 3 - data.shape[0]
    if short:
        data = jnp.concatenate([data, jnp.zeros((short, data.shape[1]), F32)], axis=0)
    high = data.astype(BF16)
    low = (data - high.astype(F32)).astype(BF16)
    tall = jnp.concatenate([high, low, high], axis=0)
    return jnp.dot(left, tall, preferred_element_type=F32)


LATE = ("x_fwd0", "x_inv0")
SENDS = 192
LOADS = 8


def kernel(levels, nz, ny, names, *refs):
    r = dict(zip(names, refs))
    lv1 = levels[0]
    half = lv1.xc
    lanes_of = (slice(0, half), slice(half, lv1.x))
    gz = lax.axis_index("gz")
    gy = lax.axis_index("gy")

    def device(dz, dy):
        return (lax.rem(gz + (dz + nz) % nz, nz), lax.rem(gy + (dy + ny) % ny, ny))

    offsets = sorted(
        {(dz % nz, dy % ny) for dz in range(-8, 9) for dy in range(-2, 3)} - {(0, 0)}
    )
    for no, lv in enumerate(levels[:-1]):
        for name in ("a", "e", "fr", "br"):
            if name in ("a", "e") or lv.states:
                buf = r[f"{name}{no}"]
                at = (slice(None),) * (len(buf.shape) - 2) + (slice(lv.y, lv.y + 8),)
                buf[at] = jnp.zeros(buf.shape[:-2] + (8, lv.x), F32)
    barrier = pltpu.get_barrier_semaphore()
    for dz, dy in offsets:
        pl.semaphore_signal(barrier, inc=1, device_id=device(dz, dy), device_id_type=MESH)

    chunk = lv1.z // 4
    loads = [pltpu.make_async_copy(r["x_fwd0"], r["x_fwd0_v"], r["load_sem"].at[4])]
    for c in range(4):
        at = pl.ds(c * chunk, chunk)
        loads.append(
            pltpu.make_async_copy(r["field"].at[at], r["whole"].at[at], r["load_sem"].at[c])
        )
    loads.append(pltpu.make_async_copy(r["keep0"], r["keep0_v"], r["load_sem"].at[5]))
    loads.append(pltpu.make_async_copy(r["x_inv0"], r["x_inv0_v"], r["load_sem"].at[6]))
    for load in loads:
        load.start()

    used = [0]
    sends = []

    def send(src, dst, dz, dy):
        at = used[0]
        used[0] += 1
        copy = pltpu.make_async_remote_copy(
            src_ref=src,
            dst_ref=dst,
            send_sem=r["send_sem"].at[at],
            recv_sem=r["recv_sem"].at[at],
            device_id=device(dz, dy),
            device_id_type=MESH,
        )
        copy.start()
        sends.append(copy)
        return copy

    def loop(count, step, unroll=4):
        unroll = min(unroll, count)

        def several(i, carry):
            for n in range(unroll):
                step(i * unroll + n, 0)
            return carry

        if unroll == count:
            several(0, 0)
        else:
            lax.fori_loop(0, count // unroll, several, 0)

    def arrive(copies):
        for copy in copies:
            copy.wait_recv()

    fx = r["a0"]

    def x_split(lanes, first):
        for c in range(4):
            if first:
                loads[1 + c].wait()
                if c == 0:
                    loads[0].wait()
            at = pl.ds(c * chunk, chunk)
            rows = r["whole"][at].reshape(chunk * lv1.y, lv1.x)
            done = split_product(rows, r["x_fwd0_v"][:, lanes])
            fx[at, 0 : lv1.y, lanes] = done.reshape(chunk, lv1.y, half)

    def comb_forward(no, lanes=slice(None)):
        lv, a = levels[no], r[f"a{no}"]
        for start in range(0, lv.z, lv.group):
            at = slice(start, start + lv.group)
            rows = a[at, 0:16, lanes]
            wide = rows.shape[-1]
            done = product_split(r[f"c_fwd{no}"][...], rows.reshape(lv.group * 16, wide))
            a[at, lv.y + 8 : lv.y + 16, lanes] = done.reshape(lv.group, 8, wide)

    def row_of(tile, lv):
        return pl.multiple_of(jnp.where(tile < lv.y // 8, tile * 8, lv.y + 8), 8)

    def states_forward(no, lanes=slice(None)):
        lv, a, out = levels[no], r[f"a{no}"], r[f"fs{no}"]
        count = min(lv.zc, 5)

        def tile(t, carry):
            at = pl.ds(row_of(t, lv), 8)
            pairs = [
                lambda i=i: (a[2 * i, at, lanes], a[2 * i + 1, at, lanes]) for i in range(count)
            ]
            for k, value in enumerate(lattice_split(pairs)[1]):
                out[k, at, lanes] = value
            return carry

        lax.fori_loop(0, lv.y // 8 + 1, tile, 0)

    low, high = lanes_of
    x_split(low, True)
    comb_forward(0, low)
    states_forward(0, low)

    pl.semaphore_wait(barrier, len(offsets))

    def send_states(no, sign, lanes, own, comb):
        lv = levels[no]
        src, dst = (r[f"fs{no}"], r[f"fr{no}"]) if sign < 0 else (r[f"bs{no}"], r[f"br{no}"])
        far = 0 if sign < 0 else 4
        top, in_at = lv.y + 8, slice(lv.y, lv.y + 5)
        copies = []
        if own is not None:
            copies.append(send(src.at[0:5, own, lanes], dst.at[0:5, own, lanes], sign, 0))
            if lv.far:
                copies.append(
                    send(src.at[far, own, lanes], dst.at[5, own, lanes], 2 * sign, 0)
                )
        if comb:
            copies.append(
                send(src.at[0:5, top : top + 5, lanes], dst.at[0:5, in_at, lanes], sign, sign)
            )
            if lv.far:
                copies.append(
                    send(
                        src.at[far, top : top + 5, lanes], dst.at[5, in_at, lanes], 2 * sign, sign
                    )
                )
        return copies

    every = slice(None)

    def send_forward(no, lanes):
        lv, a = levels[no], r[f"a{no}"]
        copies = []
        if lv.states:
            copies += send_states(no, -1, lanes, slice(0, lv.y), True)
            pieces = [(0, 0, lv.z)]
        else:
            pieces = [(0, 0, lv.z)] + hop_list(lv.z, 10)
        for hz, z_at, take in pieces:
            z_to = 0 if hz == 0 else lv.z + z_at
            if hz:
                copies.append(
                    send(a.at[0:take, 0 : lv.y, lanes], a.at[z_to : z_to + take, 0 : lv.y, lanes], -hz, 0)
                )
            copies.append(
                send(
                    a.at[0:take, lv.y + 8 : lv.y + 13, lanes],
                    a.at[z_to : z_to + take, lv.y : lv.y + 5, lanes],
                    -hz,
                    -1,
                )
            )
        return copies

    def z_split(no, lanes):
        lv, a, out = levels[no], r[f"a{no}"], r[f"zx{no}"]
        tall = 8 if lv.states else lv.used

        def tile(t, carry):
            at = pl.ds(pl.multiple_of(t * 8, 8), 8) if lv.states else slice(0, tall)
            state = [None] * 5
            if lv.states:
                got = r[f"fr{no}"]
                state = [got[k, at, lanes] for k in range(5)]
                if lv.far:
                    state[4] = state[4] + far_weight(lattice_split, 0, 4, 4) * got[5, at, lanes]
            count = lv.zc if lv.states else lv.zc + 5
            pairs = [
                lambda i=i: (a[2 * i, at, lanes], a[2 * i + 1, at, lanes]) for i in range(count)
            ]
            outs = lattice_split(pairs, state)[0]
            for i in range(lv.zc):
                for bz in range(2):
                    out[bz, i, at, lanes] = outs[i][bz]
            return carry

        if lv.states:
            lax.fori_loop(0, lv.used // 8, tile, 0)
        else:
            tile(0, 0)

    def y_split(no, bands, lanes):
        lv, src, coef, mask = levels[no], r[f"zx{no}"], r[f"e{no}"], r[f"mask{no}"]
        low = lanes.start in (None, 0)

        def plane(i, carry):
            for bz in bands:
                mixed = product_split(r[f"y_fwd{no}"][...], src[bz, i, 0 : lv.used, lanes])
                coef[bz, lv.back + i, 0 : lv.y, lanes] = mixed * mask[bz, i, :, lanes]
                if bz == 0 and low and no < LEVELS - 1:
                    down = levels[no + 1]
                    at = slice(down.y_own, down.y_own + lv.yc)
                    r[f"a{no + 1}"][down.z_own + i, at, :] = mixed[0 : lv.yc, 0 : lv.xc]
            return carry

        loop(lv.zc, plane)

    def comb_back(no, bands, lanes):
        lv, coef = levels[no], r[f"e{no}"]
        own = slice(lv.back, lv.back + lv.zc)
        planes = [(bz, lv.back + i) for bz in bands for i in range(lv.zc)]
        wide = lv.xc if no == 0 else lv.x
        for start in range(0, len(planes), lv.back_group):
            part = planes[start : start + lv.back_group]
            pieces = []
            for bz, i in part:
                pieces.append(coef[bz, i, lv.yc - 8 : lv.yc, lanes])
                pieces.append(coef[bz, i, 2 * lv.yc - 8 : 2 * lv.yc, lanes])
            done = product_split(r[f"c_inv{no}"][...], jnp.concatenate(pieces, axis=0))
            for n, (bz, i) in enumerate(part):
                coef[bz, i, lv.y + 8 : lv.y + 16, lanes] = done[8 * n : 8 * n + 8]

    def states_back(no, lanes, first, last):
        lv, coef, out = levels[no], r[f"e{no}"], r[f"bs{no}"]
        start = max(lv.zc - 5, 0)

        def tile(t, carry):
            at = pl.ds(row_of(t, lv), 8)
            pairs = [
                lambda i=i: (coef[0, i, at, lanes], coef[1, i, at, lanes])
                for i in range(start, lv.zc)
            ]
            for k, value in enumerate(lattice_merge(pairs)[1]):
                out[k, at, lanes] = value
            return carry

        lax.fori_loop(first, last, tile, 0)

    def send_rows_back(no, bands, lanes):
        lv, coef = levels[no], r[f"e{no}"]
        return [
            send(
                coef.at[bands, lv.back : lv.back + lv.zc, lv.y + 8 : lv.y + 13, lanes],
                coef.at[bands, lv.back : lv.back + lv.zc, lv.y : lv.y + 5, lanes],
                0,
                1,
            )
        ]

    def send_back(no):
        lv, coef = levels[no], r[f"e{no}"]
        copies = []
        if lv.states:
            copies += send_states(no, 1, every, slice(0, lv.y), True)
            return copies + send_rows_back(no, every, every)
        for hz, done, take in [(0, 0, lv.zc)] + hop_list(lv.zc, 5):
            src_at = slice(5 + lv.zc - take, 5 + lv.zc)
            dst_at = src_at if hz == 0 else slice(5 - done - take, 5 - done)
            if hz:
                copies.append(
                    send(coef.at[:, src_at, 0 : lv.y], coef.at[:, dst_at, 0 : lv.y], hz, 0)
                )
            copies.append(
                send(
                    coef.at[:, src_at, lv.y + 8 : lv.y + 13],
                    coef.at[:, dst_at, lv.y : lv.y + 5],
                    hz,
                    1,
                )
            )
        return copies

    def z_merge(no, lanes):
        lv, coef, out = levels[no], r[f"e{no}"], r[f"v{no}"]

        def tile(t, carry):
            at = pl.ds(pl.multiple_of(t * 8, 8), 8) if lv.states else slice(0, lv.used)
            state = [None] * 5
            if lv.states:
                got = r[f"br{no}"]
                state = [got[k, at, lanes] for k in range(5)]
                if lv.far:
                    state[0] = state[0] + far_weight(lattice_merge, 4, 0, 4) * got[5, at, lanes]
            pairs = [
                lambda i=i: (coef[0, i, at, lanes], coef[1, i, at, lanes])
                for i in range(lv.back + lv.zc)
            ]
            outs = lattice_merge(pairs, state)[0][lv.back :]
            for i in range(lv.zc):
                for p in range(2):
                    out[2 * i + p, at, lanes] = outs[i][p]
            return carry

        if lv.states:
            lax.fori_loop(0, lv.used // 8, tile, 0)
        else:
            tile(0, 0)

    def y_merge(no, lanes, out):
        lv, src = levels[no], r[f"v{no}"]

        def plane(z, carry):
            out[z, :, lanes] = product_split(r[f"y_inv{no}"][...], src[z, :, lanes])
            return carry

        loop(lv.z, plane)

    def fill_masks():
        loads[-2].wait()
        for no, lv in enumerate(levels):
            keep = r["keep0_v"] if no == 0 else r[f"keep{no}"]
            mask = r[f"mask{no}"]

            def fill(i, carry, lv=lv, keep=keep, mask=mask, no=no):
                for bz in range(2):
                    for by in range(2):
                        parts = []
                        for bx in range(2):
                            band = 4 * bz + 2 * by + bx
                            if band:
                                parts.append(keep[band - 1, i].astype(F32))
                            elif no == LEVELS - 1:
                                parts.append(r["coarse"][i].astype(F32))
                            else:
                                parts.append(jnp.zeros((lv.yc, lv.xc), F32))
                        first, z_first = by * lv.yc, 0
                        if no == LEVELS - 1:
                            first, z_first = first + lv.k_own, BEHIND
                        at = slice(first, first + lv.yc)
                        mask[bz, z_first + i, at, :] = jnp.concatenate(parts, axis=1)
                return carry

            lax.fori_loop(0, lv.zc, fill, 0)

    got = send_forward(0, low)
    x_split(high, False)
    comb_forward(0, high)
    states_forward(0, high)
    fill_masks()
    arrive(got)
    z_split(0, low)
    y_split(0, (0,), low)

    mid = levels[1]
    mid_low, mid_high = slice(0, mid.xc), slice(mid.xc, mid.x)
    last = levels[LEVELS - 1]
    edge = levels[LEVELS - 2]

    def gather(buf, lead, block, span, columns, own):
        copies = []
        for dz in range(-BEHIND, span + 1):
            for c, dy in enumerate(columns):
                if dz == 0 and dy == 0:
                    continue
                mine = slice(BEHIND * block, BEHIND * block + block)
                there = slice((BEHIND + dz) * block, (BEHIND + dz) * block + block)
                src = buf.at[lead + (mine, slice(own, own + 8))]
                dst = buf.at[lead + (there, slice(8 * c, 8 * c + 8))]
                copies.append(send(src, dst, -dz, -dy))
        return copies

    def last_level():
        no = LEVELS - 1
        a, zx, coef, v = r[f"a{no}"], r[f"zx{no}"], r[f"e{no}"], r[f"v{no}"]
        count = BEHIND + 1
        for t in range(last.in_rows // 8):
            at = slice(8 * t, 8 * t + 8)
            pairs = [
                lambda i=i: (a[2 * i, at, :], a[2 * i + 1, at, :]) for i in range(count + AHEAD)
            ]
            outs = lattice_split(pairs)[0]
            for i in range(count):
                for bz in range(2):
                    zx[bz * count + i, at, :] = outs[i][bz]
        rows = zx[...].reshape(2 * count * last.in_rows, last.x)
        done = split_product(rows, r[f"x_fwd{no}"][...])
        for g in range(2 * count // 6):
            part = done[6 * g * last.in_rows : 6 * (g + 1) * last.in_rows]
            mixed = product_split(r[f"y_fwd{no}"][...], part)
            mask = r[f"mask{no}"]
            for n in range(6):
                bz, i = divmod(6 * g + n, count)
                piece = mixed[n * last.out_rows : (n + 1) * last.out_rows]
                coef[bz, i] = piece * mask[bz, i]
        for t in range(last.out_rows // 8):
            at = slice(8 * t, 8 * t + 8)
            pairs = [lambda i=i: (coef[0, i, at, :], coef[1, i, at, :]) for i in range(count)]
            outs = lattice_merge(pairs)[0][count - 4 :]
            for i in range(4):
                for p in range(2):
                    v[2 * i + p, at, :] = outs[i][p]
        rows = v[...].reshape(8 * last.out_rows, last.x)
        done = product_split(r[f"y_inv{no}"][...], rows)
        return split_product(done, r[f"x_inv{no}"][...]).reshape(8, 16, last.x)

    def place_last(value):
        coef, planes = r[f"e{LEVELS - 2}"], edge.back + edge.zc
        coef[0, :, 0 : edge.yc, 0 : edge.xc] = value[8 - planes :, 8:16]
        done = product_split(r[f"c_low{LEVELS - 2}"][...], value[:, 0:8].reshape(64, last.x))
        done = done.reshape(8, 8, last.x)[8 - planes :]
        rim = slice(edge.y, edge.y + 8)
        coef[0, :, rim, 0 : edge.xc] = coef[0, :, rim, 0 : edge.xc] + done

    for no in range(1, LEVELS - 1):
        lv = levels[no]
        comb_forward(no)
        if lv.states:
            states_forward(no)
        got = send_forward(no, every)
        if no == 1:
            later = send_forward(0, high)
            y_split(0, (1,), low)
            comb_back(0, (1,), low)
        if no == 2:
            comb_back(1, (0, 1), mid_high)
            comb_back(1, (1,), mid_low)
            states_back(1, mid_high, 0, mid.y // 8 + 1)
            states_back(1, mid_low, mid.yc // 8, mid.y // 8)
            mask_got = gather(
                r[f"mask{LEVELS - 1}"], (every,), 1, 0, last.kept, last.k_own
            )
            arrive(later)
            z_split(0, high)
            y_split(0, (0, 1), high)
        arrive(got)
        z_split(no, every)
        count = 2 * lv.zc
        rows = r[f"zx{no}"][...].reshape(count * lv.used, lv.x)
        done = split_product(rows, r[f"x_fwd{no}"][...])
        r[f"zx{no}"][...] = done.reshape(2, lv.zc, lv.used, lv.x)
        y_split(no, (0, 1), every)

    got = gather(r[f"a{LEVELS - 1}"], (), 2, AHEAD, last.columns, last.y_own)
    comb_back(LEVELS - 2, (0, 1), every)
    edge_got = send_back(LEVELS - 2)
    comb_back(0, (0, 1), high)
    states_back(0, high, 0, lv1.y // 8 + 1)
    states_back(0, low, lv1.yc // 8, lv1.y // 8)
    arrive(mask_got)
    arrive(got)
    mid_got = send_states(1, 1, mid_high, slice(0, mid.y), True)
    mid_got += send_rows_back(1, every, mid_high)
    mid_got += send_states(1, 1, mid_low, slice(mid.yc, mid.y), False)
    mid_got += send_rows_back(1, slice(1, 2), mid_low)
    value = last_level()
    arrive(edge_got)
    for copy in edge_got:
        copy.wait_send()
    done_ids = [id(copy) for copy in edge_got]
    sends[:] = [copy for copy in sends if id(copy) not in done_ids]
    place_last(value)

    for no in range(LEVELS - 2, 0, -1):
        lv = levels[no]
        if no < LEVELS - 2:
            comb_back(no, (0,), mid_low)
            states_back(no, mid_low, 0, lv.yc // 8)
            states_back(no, mid_low, lv.y // 8, lv.y // 8 + 1)
            got = send_rows_back(no, slice(0, 1), mid_low)
            got += send_states(no, 1, mid_low, slice(0, lv.yc), True)
            got += mid_got
            early = send_states(0, 1, high, slice(0, lv1.y), True)
            early += send_rows_back(0, every, high)
            early_low = send_states(0, 1, low, slice(lv1.yc, lv1.y), False)
            early_low += send_rows_back(0, slice(1, 2), low)
            arrive(got)
        z_merge(no, every)
        y_merge(no, every, r[f"yv{no}"])
        rows = r[f"yv{no}"][...].reshape(lv.z * lv.y, lv.x)
        done = split_product(rows, r[f"x_inv{no}"][...]).reshape(lv.z, lv.y, lv.x)
        up = levels[no - 1]
        r[f"e{no - 1}"][0, up.back : up.back + up.zc, 0 : up.yc, 0 : up.xc] = done

    comb_back(0, (0,), low)
    states_back(0, low, 0, lv1.yc // 8)
    states_back(0, low, lv1.y // 8, lv1.y // 8 + 1)
    got = send_states(0, 1, low, slice(0, lv1.yc), True)
    got += send_rows_back(0, slice(0, 1), low)
    arrive(early)
    z_merge(0, high)
    y_merge(0, high, r["yv0"])
    loads[-1].wait()

    def x_part(c):
        at = pl.ds(c * chunk, chunk)
        rows = r["yv0"][at, :, high].reshape(chunk * lv1.y, half)
        r["part"][at] = split_product(rows, r["x_inv0_v"][...]).reshape(chunk, lv1.y, lv1.x)

    for c in range(4):
        x_part(c)
    arrive(early_low)
    arrive(got)
    z_merge(0, low)
    y_merge(0, low, r["out"])
    for copy in sends:
        copy.wait_send()
    assert used[0] <= SENDS


def last_kernel(v, part, right, out, whole, sem):
    planes, y, x = part.shape
    half = x // 2
    copies = []
    for n in range(2):
        lanes = slice(n * half, (n + 1) * half)
        rows = v[...].reshape(planes * y, half)
        done = split_product(rows, right[:, lanes]).reshape(planes, y, half)
        whole[:, :, lanes] = done + part[:, :, lanes]
        copies.append(pltpu.make_async_copy(whole.at[:, :, lanes], out.at[:, :, lanes], sem.at[n]))
        copies[-1].start()
    for copy in copies:
        copy.wait()


def solution(mesh):
    nz, ny = mesh.shape["gz"], mesh.shape["gy"]

    def on_device(field, k1, k2, k3, k4, coarse):
        z, y, x = field.shape
        levels = [Level(z >> n, y >> n, x >> n) for n in range(LEVELS - 1)]
        levels.append(Last(z >> 3, y >> 3, x >> 3, ny))
        vmem = pl.BlockSpec(memory_space=pltpu.VMEM)
        hbm = pl.BlockSpec(memory_space=pl.ANY)
        names = ["field", "keep0", "keep1", "keep2", "keep3", "coarse"]
        operands = [field, k1, k2, k3, k4, coarse]
        specs = [hbm, hbm] + [vmem] * 4
        last = None
        for no, lv in enumerate(levels):
            for name, matrix in lv.matrices().items():
                if no == 0 and name == "x_inv":
                    whole = x_matrix(x).T
                    last = jnp.asarray(right_matrix(whole[: x // 2]))
                    matrix = right_matrix(whole[x // 2 :])
                names.append(f"{name}{no}")
                operands.append(jnp.asarray(matrix))
                specs.append(hbm if f"{name}{no}" in LATE else vmem)
        names += ["out", "part"]
        scratch = {
            "whole": pltpu.VMEM((z, y, x), F32),
            "x_fwd0_v": pltpu.VMEM((3 * x, x), BF16),
            "x_inv0_v": pltpu.VMEM((3 * x // 2, x), BF16),
            "yv0": pltpu.VMEM((z, y, x), F32),
            "keep0_v": pltpu.VMEM(k1.shape, jnp.int32),
        }
        end = levels[-1]
        pairs = BEHIND + 1
        last_shapes = {
            "a": (2 * (pairs + AHEAD), end.in_rows),
            "zx": (2 * pairs, end.in_rows),
            "e": (2, pairs, end.out_rows),
            "v": (8, end.out_rows),
            "mask": (2, pairs, end.out_rows),
        }
        for name, shape in last_shapes.items():
            scratch[f"{name}{LEVELS - 1}"] = pltpu.VMEM(shape + (end.x,), F32)
        for no, lv in enumerate(levels[:-1]):
            scratch[f"a{no}"] = pltpu.VMEM((lv.fwd_planes, lv.rows, lv.x), F32)
            scratch[f"zx{no}"] = pltpu.VMEM((2, lv.zc, lv.used, lv.x), F32)
            scratch[f"e{no}"] = pltpu.VMEM((2, lv.back + lv.zc, lv.rows, lv.x), F32)
            scratch[f"v{no}"] = pltpu.VMEM((lv.z, lv.used, lv.x), F32)
            scratch[f"mask{no}"] = pltpu.VMEM((2, lv.zc, lv.y, lv.x), F32)
            if no:
                scratch[f"yv{no}"] = pltpu.VMEM((lv.z, lv.y, lv.x), F32)
            if lv.states:
                for name, planes in (("fs", 5), ("fr", 6), ("bs", 5), ("br", 6)):
                    scratch[f"{name}{no}"] = pltpu.VMEM((planes, lv.rows, lv.x), F32)
        scratch["load_sem"] = pltpu.SemaphoreType.DMA((LOADS,))
        scratch["send_sem"] = pltpu.SemaphoreType.DMA((SENDS,))
        scratch["recv_sem"] = pltpu.SemaphoreType.DMA((SENDS,))
        names += list(scratch)
        merged, part = pl.pallas_call(
            functools.partial(kernel, levels, nz, ny, names),
            out_shape=[
                jax.ShapeDtypeStruct((z, y, x // 2), F32),
                jax.ShapeDtypeStruct((z, y, x), F32),
            ],
            in_specs=specs,
            out_specs=[vmem, vmem],
            scratch_shapes=list(scratch.values()),
            compiler_params=pltpu.CompilerParams(
                collective_id=0, has_side_effects=True, vmem_limit_bytes=36 * 1024 * 1024
            ),
        )(*[pltpu.with_memory_space_constraint(o, pltpu.HBM) for o in operands])
        return pl.pallas_call(
            last_kernel,
            out_shape=jax.ShapeDtypeStruct((z, y, x), F32),
            in_specs=[vmem] * 3,
            out_specs=hbm,
            scratch_shapes=[pltpu.VMEM((z, y, x), F32), pltpu.SemaphoreType.DMA((2,))],
            compiler_params=pltpu.CompilerParams(vmem_limit_bytes=48 * 1024 * 1024),
        )(merged, part, last)

    in_specs = (
        P("gz", "gy", None),
        P(None, "gz", "gy", None),
        P(None, "gz", "gy", None),
        P(None, "gz", "gy", None),
        P(None, "gz", "gy", None),
        P("gz", "gy", None),
    )
    return jax.shard_map(
        on_device, mesh=mesh, in_specs=in_specs, out_specs=P("gz", "gy", None), check_vma=False
    )
```

```python
import functools

import jax
import jax.numpy as jnp
import ml_dtypes
import numpy as np
from jax import lax
from jax.experimental import pallas as pl
from jax.experimental.pallas import tpu as pltpu
from jax.sharding import PartitionSpec as P

low_taps = (
    0.11154074335008017,
    0.4946238903983854,
    0.7511339080215775,
    0.3152503517092432,
    -0.22626469396516913,
    -0.12976686756709563,
    0.09750160558707936,
    0.02752286553001629,
    -0.031582039318031156,
    0.0005538422009938016,
    0.004777257511010651,
    -0.00107730108499558,
)
high_taps = tuple(((-1.0) ** k * low_taps[11 - k] for k in range(12)))
LEVELS = 4
MESH = pl.DeviceIdType.MESH
BF16 = jnp.bfloat16
F32 = jnp.float32


def rotations():
    h, g = low_taps, high_taps
    now = [np.array([[h[2 * m], h[2 * m + 1]], [g[2 * m], g[2 * m + 1]]]) for m in range(6)]
    found = []
    while len(now) > 1:
        row = now[0][np.argmax(np.linalg.norm(now[0], axis=1))]
        a, b = row / np.linalg.norm(row)
        turn = np.array([[a, b], [-b, a]])
        rest = [m @ turn.T for m in now]
        now = [np.stack([rest[m][:, 0], rest[m + 1][:, 1]], 1) for m in range(len(now) - 1)]
        found.append(turn)
    found.append(now[0])
    sizes = [np.abs(m).max() for m in found]
    return [m / s for m, s in zip(found, sizes)], float(np.prod(sizes))


TURNS, SCALE = rotations()


def mix(a, x, b, y):
    if x is None and y is None:
        return None
    terms = []
    for c, v in ((float(a), x), (float(b), y)):
        if v is not None:
            terms.append((c, v))
    if len(terms) == 1:
        c, v = terms[0]
        return v if c == 1.0 else -v if c == -1.0 else c * v
    (c, v), (d, w) = terms
    if abs(d) == 1.0:
        (c, v), (d, w) = (d, w), (c, v)
    if c == 1.0:
        return v + d * w
    if c == -1.0:
        return d * w - v
    return c * v + d * w


def turn(m, u, w):
    return mix(m[0, 0], u, m[0, 1], w), mix(m[1, 0], u, m[1, 1], w)


def lattice_split(pairs, state=(None,) * 5):
    state = list(state)
    outs = [None] * len(pairs)
    for i in reversed(range(len(pairs))):
        u, w = turn(TURNS[0], *pairs[i]())
        for k in range(1, 6):
            w, state[k - 1] = state[k - 1], w
            u, w = turn(TURNS[k], u, w)
        outs[i] = (u, w)
    return outs, state


def lattice_merge(pairs, state=(None,) * 5):
    state = list(state)
    outs = []
    for pair in pairs:
        u, w = turn(TURNS[5].T, *pair())
        for k in range(5, 0, -1):
            w, state[k - 1] = state[k - 1], w
            u, w = turn(TURNS[k - 1].T, u, w)
        outs.append((u, w))
    return outs, state


def far_weight(lattice, first, last, pairs):
    state = [None] * 5
    state[first] = np.float64(1.0)
    left = lattice([lambda: (None, None)] * pairs, state)[1]
    return float(left[last])


def halves(matrix):
    matrix = matrix.astype(np.float32)
    high = matrix.astype(ml_dtypes.bfloat16)
    low = (matrix - high.astype(np.float32)).astype(ml_dtypes.bfloat16)
    return np.stack([high, low])


def x_matrix(x_len):
    half = x_len // 2
    matrix = np.zeros((x_len, x_len))
    for i in range(half):
        for k in range(12):
            matrix[(2 * i + k) % x_len, i] += low_taps[k]
            matrix[(2 * i + k) % x_len, half + i] += high_taps[k]
    return matrix


def y_split_parts(n):
    half = n // 2
    whole = np.zeros((n, n + 10))
    for i in range(half):
        for k in range(12):
            whole[i, 2 * i + k] = low_taps[k]
            whole[half + i, 2 * i + k] = high_taps[k]
    left, size, right = np.linalg.svd(whole[:, n:])
    return whole[:, :n], left[:, :5] * size[:5], right[:5]


def y_merge_parts(n):
    half = n // 2
    own = np.zeros((n, n))
    back = np.zeros((n, 10))
    for j in range(n):
        for t in range(6):
            k = 2 * t + j % 2
            c = j // 2 - t
            if c >= 0:
                own[j, c] += low_taps[k]
                own[j, half + c] += high_taps[k]
            else:
                back[j, 5 + c] += low_taps[k]
                back[j, 10 + c] += high_taps[k]
    left, size, right = np.linalg.svd(back)
    return own, left[:, :5] * size[:5], right[:5]


def distinct(offsets, n):
    found = []
    for o in sorted(offsets, key=abs):
        if all((o - p) % n for p in found):
            found.append(o)
    return sorted(found)


AHEAD, BEHIND = 5, 8


class Last:
    def __init__(self, z, y, x, ny):
        assert z == 2 and y == 8
        self.z, self.y, self.x = z, y, x
        self.zc, self.yc, self.xc = 1, 4, x // 2
        self.ny = ny
        self.columns = distinct(range(-2, 3), ny)
        self.kept = distinct(range(-2, 1), ny)
        self.in_rows, self.out_rows = 8 * len(self.columns), 8 * len(self.kept)
        self.z_own, self.y_own = 2 * BEHIND, 8 * self.columns.index(0)
        self.k_own = 8 * self.kept.index(0)

    def slot(self, found, o):
        return [(o - p) % self.ny == 0 for p in found].index(True)

    def matrices(self):
        fwd = np.zeros((self.out_rows, self.in_rows))
        for s, c in enumerate(self.kept):
            for i in range(4):
                for k in range(12):
                    at = 8 * c + 2 * i + k
                    col = 8 * self.slot(self.columns, at // 8) + at % 8
                    fwd[8 * s + i, col] += low_taps[k]
                    fwd[8 * s + 4 + i, col] += high_taps[k]
        inv = np.zeros((16, self.out_rows))
        for j in range(-5, 8):
            for t in range(6):
                k = 2 * t + j % 2
                c = j // 2 - t
                col = 8 * self.slot(self.kept, c // 4) + c % 4
                inv[8 + j, col] += low_taps[k]
                inv[8 + j, col + 4] += high_taps[k]
        return {
            "x_fwd": right_matrix(x_matrix(self.x)),
            "x_inv": right_matrix(x_matrix(self.x).T),
            "y_fwd": left_matrix(np.kron(np.eye(6), fwd * SCALE)),
            "y_inv": left_matrix(np.kron(np.eye(8), inv * SCALE)),
        }


class Level:
    z_own = y_own = 0

    def __init__(self, z, y, x):
        self.z, self.y, self.x = z, y, x
        self.zc, self.yc, self.xc = z // 2, y // 2, x // 2
        self.states = self.zc >= 4
        self.far = self.zc == 4
        self.comb = self.yc >= 8
        assert self.states or self.zc <= 2
        assert self.comb
        self.used = y + 8
        self.rows = y + 16
        self.fwd_planes = z if self.states else z + 10
        self.back = 0 if self.states else 5
        self.group = min(z, 8)
        self.back_group = max(min(self.zc, 8), 4)

    def matrices(self):
        n, half = self.y, self.yc
        own, ahead, pick = y_split_parts(n)
        fwd = np.zeros((n, self.used))
        fwd[:, :n] = own
        inv_own, behind, inv_pick = y_merge_parts(n)
        inv = np.zeros((n, self.used))
        inv[:, :n] = inv_own
        out = {"x_fwd": right_matrix(x_matrix(self.x)), "x_inv": right_matrix(x_matrix(self.x).T)}
        if self.comb:
            fwd[:, n : n + 5] = ahead
            inv[:, n : n + 5] = behind
            small = np.zeros((8, 16))
            small[:5, :10] = pick
            out["c_fwd"] = left_matrix(np.kron(np.eye(self.group), small))
            small = np.zeros((8, 16))
            small[:5, 3:8] = inv_pick[:, :5]
            small[:5, 11:16] = inv_pick[:, 5:]
            out["c_inv"] = left_matrix(np.kron(np.eye(self.back_group), small))
            if self.yc == 8:
                out["c_low"] = left_matrix(np.kron(np.eye(8), small[:, :8]))
        out["y_fwd"] = left_matrix(fwd * SCALE)
        out["y_inv"] = left_matrix(inv * SCALE)
        return out


def hop_list(length, rim):
    pieces = []
    done = 0
    hop = 1
    while done < rim:
        take = min(length, rim - done)
        pieces.append((hop, done, take))
        done += take
        hop += 1
    return pieces


def right_matrix(matrix):
    high, low = halves(matrix)
    return np.concatenate([high, high, low], axis=0)


def left_matrix(matrix):
    short = -matrix.shape[1] % 16
    high, low = halves(np.pad(matrix, ((0, 0), (0, short))))
    return np.concatenate([high, high, low], axis=1)


def split_product(data, right):
    high = data.astype(BF16)
    low = (data - high.astype(F32)).astype(BF16)
    depth = data.shape[1]
    if depth % 128:
        out = jnp.dot(high, right[0:depth], preferred_element_type=F32)
        out += jnp.dot(low, right[depth : 2 * depth], preferred_element_type=F32)
        return out + jnp.dot(high, right[2 * depth :], preferred_element_type=F32)
    wide = jnp.concatenate([high, low, high], axis=1)
    return jnp.dot(wide, right, preferred_element_type=F32)


def product_split(left, data):
    short = left.shape[1] // 3 - data.shape[0]
    if short:
        data = jnp.concatenate([data, jnp.zeros((short, data.shape[1]), F32)], axis=0)
    high = data.astype(BF16)
    low = (data - high.astype(F32)).astype(BF16)
    tall = jnp.concatenate([high, low, high], axis=0)
    return jnp.dot(left, tall, preferred_element_type=F32)


LATE = ("x_fwd0", "x_inv0", "keep0")
SENDS = 192
LOADS = 8


def kernel(levels, nz, ny, names, *refs):
    r = dict(zip(names, refs))
    lv1 = levels[0]
    half = lv1.xc
    lanes_of = (slice(0, half), slice(half, lv1.x))
    gz = lax.axis_index("gz")
    gy = lax.axis_index("gy")

    def device(dz, dy):
        return (lax.rem(gz + (dz + nz) % nz, nz), lax.rem(gy + (dy + ny) % ny, ny))

    offsets = sorted(
        {(dz % nz, dy % ny) for dz in range(-8, 9) for dy in range(-2, 3)} - {(0, 0)}
    )
    for no, lv in enumerate(levels[:-1]):
        for name in ("a", "e", "fr", "br"):
            if name in ("a", "e") or lv.states:
                buf = r[f"{name}{no}"]
                at = (slice(None),) * (len(buf.shape) - 2) + (slice(lv.y, lv.y + 8),)
                buf[at] = jnp.zeros(buf.shape[:-2] + (8, lv.x), F32)
    barrier = pltpu.get_barrier_semaphore()
    for dz, dy in offsets:
        pl.semaphore_signal(barrier, inc=1, device_id=device(dz, dy), device_id_type=MESH)

    chunk = lv1.z // 4
    loads = [pltpu.make_async_copy(r["x_fwd0"], r["x_fwd0_v"], r["load_sem"].at[4])]
    for c in range(4):
        at = pl.ds(c * chunk, chunk)
        loads.append(
            pltpu.make_async_copy(r["field"].at[at], r["whole"].at[at], r["load_sem"].at[c])
        )
    loads.append(pltpu.make_async_copy(r["keep0"], r["keep0_v"], r["load_sem"].at[5]))
    loads.append(pltpu.make_async_copy(r["x_inv0"], r["x_inv0_v"], r["load_sem"].at[6]))
    for load in loads:
        load.start()
    small = [name for name in names if f"{name}_v" in r and name not in LATE]
    small_loads = []
    for n, name in enumerate(small):
        small_loads.append(
            pltpu.make_async_copy(r[name], r[f"{name}_v"], r["small_sem"].at[n])
        )
        small_loads[-1].start()
        r[name] = r[f"{name}_v"]

    used = [0]
    sends = []

    def send(src, dst, dz, dy):
        at = used[0]
        used[0] += 1
        copy = pltpu.make_async_remote_copy(
            src_ref=src,
            dst_ref=dst,
            send_sem=r["send_sem"].at[at],
            recv_sem=r["recv_sem"].at[at],
            device_id=device(dz, dy),
            device_id_type=MESH,
        )
        copy.start()
        sends.append(copy)
        return copy

    def loop(count, step, unroll=4):
        unroll = min(unroll, count)

        def several(i, carry):
            for n in range(unroll):
                step(i * unroll + n, 0)
            return carry

        if unroll == count:
            several(0, 0)
        else:
            lax.fori_loop(0, count // unroll, several, 0)

    def arrive(copies):
        for copy in copies:
            copy.wait_recv()

    fx = r["a0"]

    def x_split(lanes, first):
        for c in range(4):
            if first:
                loads[1 + c].wait()
                if c == 0:
                    loads[0].wait()
            at = pl.ds(c * chunk, chunk)
            rows = r["whole"][at].reshape(chunk * lv1.y, lv1.x)
            done = split_product(rows, r["x_fwd0_v"][:, lanes])
            fx[at, 0 : lv1.y, lanes] = done.reshape(chunk, lv1.y, half)

    def comb_forward(no, lanes=slice(None)):
        lv, a = levels[no], r[f"a{no}"]
        for start in range(0, lv.z, lv.group):
            at = slice(start, start + lv.group)
            rows = a[at, 0:16, lanes]
            wide = rows.shape[-1]
            done = product_split(r[f"c_fwd{no}"][...], rows.reshape(lv.group * 16, wide))
            a[at, lv.y + 8 : lv.y + 16, lanes] = done.reshape(lv.group, 8, wide)

    def row_of(tile, lv):
        return pl.multiple_of(jnp.where(tile < lv.y // 8, tile * 8, lv.y + 8), 8)

    def states_forward(no, lanes=slice(None)):
        lv, a, out = levels[no], r[f"a{no}"], r[f"fs{no}"]
        count = min(lv.zc, 5)

        def tile(t, carry):
            at = pl.ds(row_of(t, lv), 8)
            pairs = [
                lambda i=i: (a[2 * i, at, lanes], a[2 * i + 1, at, lanes]) for i in range(count)
            ]
            for k, value in enumerate(lattice_split(pairs)[1]):
                out[k, at, lanes] = value
            return carry

        lax.fori_loop(0, lv.y // 8 + 1, tile, 0)

    low, high = lanes_of
    x_split(low, True)
    for load in small_loads:
        load.wait()
    comb_forward(0, low)
    states_forward(0, low)

    pl.semaphore_wait(barrier, len(offsets))

    def send_states(no, sign, lanes, own, comb):
        lv = levels[no]
        src, dst = (r[f"fs{no}"], r[f"fr{no}"]) if sign < 0 else (r[f"bs{no}"], r[f"br{no}"])
        far = 0 if sign < 0 else 4
        top, in_at = lv.y + 8, slice(lv.y, lv.y + 5)
        copies = []
        if own is not None:
            copies.append(send(src.at[0:5, own, lanes], dst.at[0:5, own, lanes], sign, 0))
            if lv.far:
                copies.append(
                    send(src.at[far, own, lanes], dst.at[5, own, lanes], 2 * sign, 0)
                )
        if comb:
            copies.append(
                send(src.at[0:5, top : top + 5, lanes], dst.at[0:5, in_at, lanes], sign, sign)
            )
            if lv.far:
                copies.append(
                    send(
                        src.at[far, top : top + 5, lanes], dst.at[5, in_at, lanes], 2 * sign, sign
                    )
                )
        return copies

    every = slice(None)

    def send_forward(no, lanes):
        lv, a = levels[no], r[f"a{no}"]
        copies = []
        if lv.states:
            copies += send_states(no, -1, lanes, slice(0, lv.y), True)
            pieces = [(0, 0, lv.z)]
        else:
            pieces = [(0, 0, lv.z)] + hop_list(lv.z, 10)
        for hz, z_at, take in pieces:
            z_to = 0 if hz == 0 else lv.z + z_at
            if hz:
                copies.append(
                    send(a.at[0:take, 0 : lv.y, lanes], a.at[z_to : z_to + take, 0 : lv.y, lanes], -hz, 0)
                )
            copies.append(
                send(
                    a.at[0:take, lv.y + 8 : lv.y + 13, lanes],
                    a.at[z_to : z_to + take, lv.y : lv.y + 5, lanes],
                    -hz,
                    -1,
                )
            )
        return copies

    def z_split(no, lanes):
        lv, a, out = levels[no], r[f"a{no}"], r[f"zx{no}"]
        tall = 8 if lv.states else lv.used

        def tile(t, carry):
            at = pl.ds(pl.multiple_of(t * 8, 8), 8) if lv.states else slice(0, tall)
            state = [None] * 5
            if lv.states:
                got = r[f"fr{no}"]
                state = [got[k, at, lanes] for k in range(5)]
                if lv.far:
                    state[4] = state[4] + far_weight(lattice_split, 0, 4, 4) * got[5, at, lanes]
            count = lv.zc if lv.states else lv.zc + 5
            pairs = [
                lambda i=i: (a[2 * i, at, lanes], a[2 * i + 1, at, lanes]) for i in range(count)
            ]
            outs = lattice_split(pairs, state)[0]
            for i in range(lv.zc):
                for bz in range(2):
                    out[bz, i, at, lanes] = outs[i][bz]
            return carry

        if lv.states:
            lax.fori_loop(0, lv.used // 8, tile, 0)
        else:
            tile(0, 0)

    def y_split(no, bands, lanes):
        lv, src, coef, mask = levels[no], r[f"zx{no}"], r[f"e{no}"], r[f"mask{no}"]
        low = lanes.start in (None, 0)

        def plane(i, carry):
            for bz in bands:
                mixed = product_split(r[f"y_fwd{no}"][...], src[bz, i, 0 : lv.used, lanes])
                coef[bz, lv.back + i, 0 : lv.y, lanes] = mixed * mask[bz, i, :, lanes]
                if bz == 0 and low and no < LEVELS - 1:
                    down = levels[no + 1]
                    at = slice(down.y_own, down.y_own + lv.yc)
                    r[f"a{no + 1}"][down.z_own + i, at, :] = mixed[0 : lv.yc, 0 : lv.xc]
            return carry

        loop(lv.zc, plane)

    def comb_back(no, bands, lanes):
        lv, coef = levels[no], r[f"e{no}"]
        own = slice(lv.back, lv.back + lv.zc)
        planes = [(bz, lv.back + i) for bz in bands for i in range(lv.zc)]
        wide = lv.xc if no == 0 else lv.x
        for start in range(0, len(planes), lv.back_group):
            part = planes[start : start + lv.back_group]
            pieces = []
            for bz, i in part:
                pieces.append(coef[bz, i, lv.yc - 8 : lv.yc, lanes])
                pieces.append(coef[bz, i, 2 * lv.yc - 8 : 2 * lv.yc, lanes])
            done = product_split(r[f"c_inv{no}"][...], jnp.concatenate(pieces, axis=0))
            for n, (bz, i) in enumerate(part):
                coef[bz, i, lv.y + 8 : lv.y + 16, lanes] = done[8 * n : 8 * n + 8]

    def states_back(no, lanes, first, last):
        lv, coef, out = levels[no], r[f"e{no}"], r[f"bs{no}"]
        start = max(lv.zc - 5, 0)

        def tile(t, carry):
            at = pl.ds(row_of(t, lv), 8)
            pairs = [
                lambda i=i: (coef[0, i, at, lanes], coef[1, i, at, lanes])
                for i in range(start, lv.zc)
            ]
            for k, value in enumerate(lattice_merge(pairs)[1]):
                out[k, at, lanes] = value
            return carry

        lax.fori_loop(first, last, tile, 0)

    def send_rows_back(no, bands, lanes):
        lv, coef = levels[no], r[f"e{no}"]
        return [
            send(
                coef.at[bands, lv.back : lv.back + lv.zc, lv.y + 8 : lv.y + 13, lanes],
                coef.at[bands, lv.back : lv.back + lv.zc, lv.y : lv.y + 5, lanes],
                0,
                1,
            )
        ]

    def send_back(no):
        lv, coef = levels[no], r[f"e{no}"]
        copies = []
        if lv.states:
            copies += send_states(no, 1, every, slice(0, lv.y), True)
            return copies + send_rows_back(no, every, every)
        for hz, done, take in [(0, 0, lv.zc)] + hop_list(lv.zc, 5):
            src_at = slice(5 + lv.zc - take, 5 + lv.zc)
            dst_at = src_at if hz == 0 else slice(5 - done - take, 5 - done)
            if hz:
                copies.append(
                    send(coef.at[:, src_at, 0 : lv.y], coef.at[:, dst_at, 0 : lv.y], hz, 0)
                )
            copies.append(
                send(
                    coef.at[:, src_at, lv.y + 8 : lv.y + 13],
                    coef.at[:, dst_at, lv.y : lv.y + 5],
                    hz,
                    1,
                )
            )
        return copies

    def z_merge(no, lanes):
        lv, coef, out = levels[no], r[f"e{no}"], r[f"v{no}"]

        def tile(t, carry):
            at = pl.ds(pl.multiple_of(t * 8, 8), 8) if lv.states else slice(0, lv.used)
            state = [None] * 5
            if lv.states:
                got = r[f"br{no}"]
                state = [got[k, at, lanes] for k in range(5)]
                if lv.far:
                    state[0] = state[0] + far_weight(lattice_merge, 4, 0, 4) * got[5, at, lanes]
            pairs = [
                lambda i=i: (coef[0, i, at, lanes], coef[1, i, at, lanes])
                for i in range(lv.back + lv.zc)
            ]
            outs = lattice_merge(pairs, state)[0][lv.back :]
            for i in range(lv.zc):
                for p in range(2):
                    out[2 * i + p, at, lanes] = outs[i][p]
            return carry

        if lv.states:
            lax.fori_loop(0, lv.used // 8, tile, 0)
        else:
            tile(0, 0)

    def y_merge(no, lanes, out):
        lv, src = levels[no], r[f"v{no}"]

        def plane(z, carry):
            out[z, :, lanes] = product_split(r[f"y_inv{no}"][...], src[z, :, lanes])
            return carry

        loop(lv.z, plane)

    def fill_masks():
        loads[-2].wait()
        for no, lv in enumerate(levels):
            keep = r["keep0_v"] if no == 0 else r[f"keep{no}"]
            mask = r[f"mask{no}"]

            def fill(i, carry, lv=lv, keep=keep, mask=mask, no=no):
                for bz in range(2):
                    for by in range(2):
                        parts = []
                        for bx in range(2):
                            band = 4 * bz + 2 * by + bx
                            if band:
                                parts.append(keep[band - 1, i].astype(F32))
                            elif no == LEVELS - 1:
                                parts.append(r["coarse"][i].astype(F32))
                            else:
                                parts.append(jnp.zeros((lv.yc, lv.xc), F32))
                        first, z_first = by * lv.yc, 0
                        if no == LEVELS - 1:
                            first, z_first = first + lv.k_own, BEHIND
                        at = slice(first, first + lv.yc)
                        mask[bz, z_first + i, at, :] = jnp.concatenate(parts, axis=1)
                return carry

            lax.fori_loop(0, lv.zc, fill, 0)

    got = send_forward(0, low)
    x_split(high, False)
    comb_forward(0, high)
    states_forward(0, high)
    fill_masks()
    arrive(got)
    z_split(0, low)
    y_split(0, (0,), low)

    mid = levels[1]
    mid_low, mid_high = slice(0, mid.xc), slice(mid.xc, mid.x)
    last = levels[LEVELS - 1]
    edge = levels[LEVELS - 2]

    def gather(buf, lead, block, span, columns, own):
        copies = []
        for dz in range(-BEHIND, span + 1):
            for c, dy in enumerate(columns):
                if dz == 0 and dy == 0:
                    continue
                mine = slice(BEHIND * block, BEHIND * block + block)
                there = slice((BEHIND + dz) * block, (BEHIND + dz) * block + block)
                src = buf.at[lead + (mine, slice(own, own + 8))]
                dst = buf.at[lead + (there, slice(8 * c, 8 * c + 8))]
                copies.append(send(src, dst, -dz, -dy))
        return copies

    def last_level():
        no = LEVELS - 1
        a, zx, coef, v = r[f"a{no}"], r[f"zx{no}"], r[f"e{no}"], r[f"v{no}"]
        count = BEHIND + 1
        for t in range(last.in_rows // 8):
            at = slice(8 * t, 8 * t + 8)
            pairs = [
                lambda i=i: (a[2 * i, at, :], a[2 * i + 1, at, :]) for i in range(count + AHEAD)
            ]
            outs = lattice_split(pairs)[0]
            for i in range(count):
                for bz in range(2):
                    zx[bz * count + i, at, :] = outs[i][bz]
        rows = zx[...].reshape(2 * count * last.in_rows, last.x)
        done = split_product(rows, r[f"x_fwd{no}"][...])
        for g in range(2 * count // 6):
            part = done[6 * g * last.in_rows : 6 * (g + 1) * last.in_rows]
            mixed = product_split(r[f"y_fwd{no}"][...], part)
            mask = r[f"mask{no}"]
            for n in range(6):
                bz, i = divmod(6 * g + n, count)
                piece = mixed[n * last.out_rows : (n + 1) * last.out_rows]
                coef[bz, i] = piece * mask[bz, i]
        for t in range(last.out_rows // 8):
            at = slice(8 * t, 8 * t + 8)
            pairs = [lambda i=i: (coef[0, i, at, :], coef[1, i, at, :]) for i in range(count)]
            outs = lattice_merge(pairs)[0][count - 4 :]
            for i in range(4):
                for p in range(2):
                    v[2 * i + p, at, :] = outs[i][p]
        rows = v[...].reshape(8 * last.out_rows, last.x)
        done = product_split(r[f"y_inv{no}"][...], rows)
        return split_product(done, r[f"x_inv{no}"][...]).reshape(8, 16, last.x)

    def place_last(value):
        coef, planes = r[f"e{LEVELS - 2}"], edge.back + edge.zc
        coef[0, :, 0 : edge.yc, 0 : edge.xc] = value[8 - planes :, 8:16]
        done = product_split(r[f"c_low{LEVELS - 2}"][...], value[:, 0:8].reshape(64, last.x))
        done = done.reshape(8, 8, last.x)[8 - planes :]
        rim = slice(edge.y, edge.y + 8)
        coef[0, :, rim, 0 : edge.xc] = coef[0, :, rim, 0 : edge.xc] + done

    for no in range(1, LEVELS - 1):
        lv = levels[no]
        comb_forward(no)
        if lv.states:
            states_forward(no)
        got = send_forward(no, every)
        if no == 1:
            later = send_forward(0, high)
            y_split(0, (1,), low)
            comb_back(0, (1,), low)
        if no == 2:
            comb_back(1, (0, 1), mid_high)
            comb_back(1, (1,), mid_low)
            states_back(1, mid_high, 0, mid.y // 8 + 1)
            states_back(1, mid_low, mid.yc // 8, mid.y // 8)
            mask_got = gather(
                r[f"mask{LEVELS - 1}"], (every,), 1, 0, last.kept, last.k_own
            )
            arrive(later)
            z_split(0, high)
            y_split(0, (0, 1), high)
        arrive(got)
        z_split(no, every)
        count = 2 * lv.zc
        rows = r[f"zx{no}"][...].reshape(count * lv.used, lv.x)
        done = split_product(rows, r[f"x_fwd{no}"][...])
        r[f"zx{no}"][...] = done.reshape(2, lv.zc, lv.used, lv.x)
        y_split(no, (0, 1), every)

    got = gather(r[f"a{LEVELS - 1}"], (), 2, AHEAD, last.columns, last.y_own)
    comb_back(LEVELS - 2, (0, 1), every)
    edge_got = send_back(LEVELS - 2)
    comb_back(0, (0, 1), high)
    states_back(0, high, 0, lv1.y // 8 + 1)
    states_back(0, low, lv1.yc // 8, lv1.y // 8)
    arrive(mask_got)
    arrive(got)
    mid_got = send_states(1, 1, mid_high, slice(0, mid.y), True)
    mid_got += send_rows_back(1, every, mid_high)
    mid_got += send_states(1, 1, mid_low, slice(mid.yc, mid.y), False)
    mid_got += send_rows_back(1, slice(1, 2), mid_low)
    value = last_level()
    arrive(edge_got)
    for copy in edge_got:
        copy.wait_send()
    done_ids = [id(copy) for copy in edge_got]
    sends[:] = [copy for copy in sends if id(copy) not in done_ids]
    place_last(value)

    for no in range(LEVELS - 2, 0, -1):
        lv = levels[no]
        if no < LEVELS - 2:
            comb_back(no, (0,), mid_low)
            states_back(no, mid_low, 0, lv.yc // 8)
            states_back(no, mid_low, lv.y // 8, lv.y // 8 + 1)
            got = send_rows_back(no, slice(0, 1), mid_low)
            got += send_states(no, 1, mid_low, slice(0, lv.yc), True)
            got += mid_got
            early = send_states(0, 1, high, slice(0, lv1.y), True)
            early += send_rows_back(0, every, high)
            early_low = send_states(0, 1, low, slice(lv1.yc, lv1.y), False)
            early_low += send_rows_back(0, slice(1, 2), low)
            arrive(got)
        z_merge(no, every)
        y_merge(no, every, r[f"yv{no}"])
        rows = r[f"yv{no}"][...].reshape(lv.z * lv.y, lv.x)
        done = split_product(rows, r[f"x_inv{no}"][...]).reshape(lv.z, lv.y, lv.x)
        up = levels[no - 1]
        r[f"e{no - 1}"][0, up.back : up.back + up.zc, 0 : up.yc, 0 : up.xc] = done

    comb_back(0, (0,), low)
    states_back(0, low, 0, lv1.yc // 8)
    states_back(0, low, lv1.y // 8, lv1.y // 8 + 1)
    got = send_states(0, 1, low, slice(0, lv1.yc), True)
    got += send_rows_back(0, slice(0, 1), low)
    arrive(early)
    z_merge(0, high)
    y_merge(0, high, r["yv0"])
    loads[-1].wait()

    def x_part(c):
        at = pl.ds(c * chunk, chunk)
        rows = r["yv0"][at, :, high].reshape(chunk * lv1.y, half)
        r["part"][at] = split_product(rows, r["x_inv0_v"][...]).reshape(chunk, lv1.y, lv1.x)

    for c in range(4):
        x_part(c)
    arrive(early_low)
    arrive(got)
    z_merge(0, low)
    y_merge(0, low, r["out"])
    for copy in sends:
        copy.wait_send()
    assert used[0] <= SENDS


def last_kernel(v, part, right, out, whole, sem):
    planes, y, x = part.shape
    half = x // 2
    copies = []
    for n in range(2):
        lanes = slice(n * half, (n + 1) * half)
        rows = v[...].reshape(planes * y, half)
        done = split_product(rows, right[:, lanes]).reshape(planes, y, half)
        whole[:, :, lanes] = done + part[:, :, lanes]
        copies.append(pltpu.make_async_copy(whole.at[:, :, lanes], out.at[:, :, lanes], sem.at[n]))
        copies[-1].start()
    for copy in copies:
        copy.wait()


def solution(mesh):
    nz, ny = mesh.shape["gz"], mesh.shape["gy"]

    def on_device(field, k1, k2, k3, k4, coarse):
        z, y, x = field.shape
        levels = [Level(z >> n, y >> n, x >> n) for n in range(LEVELS - 1)]
        levels.append(Last(z >> 3, y >> 3, x >> 3, ny))
        vmem = pl.BlockSpec(memory_space=pltpu.VMEM)
        hbm = pl.BlockSpec(memory_space=pl.ANY)
        names = ["field", "keep0", "keep1", "keep2", "keep3", "coarse"]
        operands = [field, k1, k2, k3, k4, coarse]
        last = None
        for no, lv in enumerate(levels):
            for name, matrix in lv.matrices().items():
                if no == 0 and name == "x_inv":
                    whole = x_matrix(x).T
                    last = jnp.asarray(right_matrix(whole[: x // 2]))
                    matrix = right_matrix(whole[x // 2 :])
                names.append(f"{name}{no}")
                operands.append(jnp.asarray(matrix))
        inputs = dict(zip(names[1:], operands[1:]))
        names += ["out", "part"]
        scratch = {
            "whole": pltpu.VMEM((z, y, x), F32),
            "x_fwd0_v": pltpu.VMEM((3 * x, x), BF16),
            "x_inv0_v": pltpu.VMEM((3 * x // 2, x), BF16),
            "yv0": pltpu.VMEM((z, y, x), F32),
            "keep0_v": pltpu.VMEM(k1.shape, jnp.int32),
        }
        end = levels[-1]
        pairs = BEHIND + 1
        last_shapes = {
            "a": (2 * (pairs + AHEAD), end.in_rows),
            "zx": (2 * pairs, end.in_rows),
            "e": (2, pairs, end.out_rows),
            "v": (8, end.out_rows),
            "mask": (2, pairs, end.out_rows),
        }
        for name, shape in last_shapes.items():
            scratch[f"{name}{LEVELS - 1}"] = pltpu.VMEM(shape + (end.x,), F32)
        for no, lv in enumerate(levels[:-1]):
            scratch[f"a{no}"] = pltpu.VMEM((lv.fwd_planes, lv.rows, lv.x), F32)
            scratch[f"zx{no}"] = pltpu.VMEM((2, lv.zc, lv.used, lv.x), F32)
            scratch[f"e{no}"] = pltpu.VMEM((2, lv.back + lv.zc, lv.rows, lv.x), F32)
            scratch[f"v{no}"] = pltpu.VMEM((lv.z, lv.used, lv.x), F32)
            scratch[f"mask{no}"] = pltpu.VMEM((2, lv.zc, lv.y, lv.x), F32)
            if no:
                scratch[f"yv{no}"] = pltpu.VMEM((lv.z, lv.y, lv.x), F32)
            if lv.states:
                for name, planes in (("fs", 5), ("fr", 6), ("bs", 5), ("br", 6)):
                    scratch[f"{name}{no}"] = pltpu.VMEM((planes, lv.rows, lv.x), F32)
        for name, value in inputs.items():
            if name not in LATE:
                scratch[f"{name}_v"] = pltpu.VMEM(value.shape, value.dtype)
        scratch["small_sem"] = pltpu.SemaphoreType.DMA((len(inputs),))
        scratch["load_sem"] = pltpu.SemaphoreType.DMA((LOADS,))
        scratch["send_sem"] = pltpu.SemaphoreType.DMA((SENDS,))
        scratch["recv_sem"] = pltpu.SemaphoreType.DMA((SENDS,))
        names += list(scratch)
        merged, part = pl.pallas_call(
            functools.partial(kernel, levels, nz, ny, names),
            out_shape=[
                jax.ShapeDtypeStruct((z, y, x // 2), F32),
                jax.ShapeDtypeStruct((z, y, x), F32),
            ],
            in_specs=[hbm] * len(operands),
            out_specs=[vmem, vmem],
            scratch_shapes=list(scratch.values()),
            compiler_params=pltpu.CompilerParams(
                collective_id=0, has_side_effects=True, vmem_limit_bytes=36 * 1024 * 1024
            ),
        )(*[pltpu.with_memory_space_constraint(o, pltpu.HBM) for o in operands])
        return pl.pallas_call(
            last_kernel,
            out_shape=jax.ShapeDtypeStruct((z, y, x), F32),
            in_specs=[vmem] * 3,
            out_specs=hbm,
            scratch_shapes=[pltpu.VMEM((z, y, x), F32), pltpu.SemaphoreType.DMA((2,))],
            compiler_params=pltpu.CompilerParams(vmem_limit_bytes=48 * 1024 * 1024),
        )(merged, part, last)

    in_specs = (
        P("gz", "gy", None),
        P(None, "gz", "gy", None),
        P(None, "gz", "gy", None),
        P(None, "gz", "gy", None),
        P(None, "gz", "gy", None),
        P("gz", "gy", None),
    )
    return jax.shard_map(
        on_device, mesh=mesh, in_specs=in_specs, out_specs=P("gz", "gy", None), check_vma=False
    )
```

```python
import functools

import jax
import jax.numpy as jnp
import ml_dtypes
import numpy as np
from jax import lax
from jax.experimental import pallas as pl
from jax.experimental.pallas import tpu as pltpu
from jax.sharding import PartitionSpec as P

low_taps = (
    0.11154074335008017,
    0.4946238903983854,
    0.7511339080215775,
    0.3152503517092432,
    -0.22626469396516913,
    -0.12976686756709563,
    0.09750160558707936,
    0.02752286553001629,
    -0.031582039318031156,
    0.0005538422009938016,
    0.004777257511010651,
    -0.00107730108499558,
)
high_taps = tuple(((-1.0) ** k * low_taps[11 - k] for k in range(12)))
LEVELS = 4
MESH = pl.DeviceIdType.MESH
BF16 = jnp.bfloat16
F32 = jnp.float32


def rotations():
    h, g = low_taps, high_taps
    now = [np.array([[h[2 * m], h[2 * m + 1]], [g[2 * m], g[2 * m + 1]]]) for m in range(6)]
    found = []
    while len(now) > 1:
        row = now[0][np.argmax(np.linalg.norm(now[0], axis=1))]
        a, b = row / np.linalg.norm(row)
        turn = np.array([[a, b], [-b, a]])
        rest = [m @ turn.T for m in now]
        now = [np.stack([rest[m][:, 0], rest[m + 1][:, 1]], 1) for m in range(len(now) - 1)]
        found.append(turn)
    found.append(now[0])
    sizes = [np.abs(m).max() for m in found]
    return [m / s for m, s in zip(found, sizes)], float(np.prod(sizes))


TURNS, SCALE = rotations()


def mix(a, x, b, y):
    if x is None and y is None:
        return None
    terms = []
    for c, v in ((float(a), x), (float(b), y)):
        if v is not None:
            terms.append((c, v))
    if len(terms) == 1:
        c, v = terms[0]
        return v if c == 1.0 else -v if c == -1.0 else c * v
    (c, v), (d, w) = terms
    if abs(d) == 1.0:
        (c, v), (d, w) = (d, w), (c, v)
    if c == 1.0:
        return v + d * w
    if c == -1.0:
        return d * w - v
    return c * v + d * w


def turn(m, u, w):
    return mix(m[0, 0], u, m[0, 1], w), mix(m[1, 0], u, m[1, 1], w)


def lattice_split(pairs, state=(None,) * 5):
    state = list(state)
    outs = [None] * len(pairs)
    for i in reversed(range(len(pairs))):
        u, w = turn(TURNS[0], *pairs[i]())
        for k in range(1, 6):
            w, state[k - 1] = state[k - 1], w
            u, w = turn(TURNS[k], u, w)
        outs[i] = (u, w)
    return outs, state


def lattice_merge(pairs, state=(None,) * 5):
    state = list(state)
    outs = []
    for pair in pairs:
        u, w = turn(TURNS[5].T, *pair())
        for k in range(5, 0, -1):
            w, state[k - 1] = state[k - 1], w
            u, w = turn(TURNS[k - 1].T, u, w)
        outs.append((u, w))
    return outs, state


def far_weight(lattice, first, last, pairs):
    state = [None] * 5
    state[first] = np.float64(1.0)
    left = lattice([lambda: (None, None)] * pairs, state)[1]
    return float(left[last])


def halves(matrix):
    matrix = matrix.astype(np.float32)
    high = matrix.astype(ml_dtypes.bfloat16)
    low = (matrix - high.astype(np.float32)).astype(ml_dtypes.bfloat16)
    return np.stack([high, low])


def x_matrix(x_len):
    half = x_len // 2
    matrix = np.zeros((x_len, x_len))
    for i in range(half):
        for k in range(12):
            matrix[(2 * i + k) % x_len, i] += low_taps[k]
            matrix[(2 * i + k) % x_len, half + i] += high_taps[k]
    return matrix


def y_split_parts(n):
    half = n // 2
    whole = np.zeros((n, n + 10))
    for i in range(half):
        for k in range(12):
            whole[i, 2 * i + k] = low_taps[k]
            whole[half + i, 2 * i + k] = high_taps[k]
    left, size, right = np.linalg.svd(whole[:, n:])
    return whole[:, :n], left[:, :5] * size[:5], right[:5]


def y_merge_parts(n):
    half = n // 2
    own = np.zeros((n, n))
    back = np.zeros((n, 10))
    for j in range(n):
        for t in range(6):
            k = 2 * t + j % 2
            c = j // 2 - t
            if c >= 0:
                own[j, c] += low_taps[k]
                own[j, half + c] += high_taps[k]
            else:
                back[j, 5 + c] += low_taps[k]
                back[j, 10 + c] += high_taps[k]
    left, size, right = np.linalg.svd(back)
    return own, left[:, :5] * size[:5], right[:5]


def distinct(offsets, n):
    found = []
    for o in sorted(offsets, key=abs):
        if all((o - p) % n for p in found):
            found.append(o)
    return sorted(found)


AHEAD, BEHIND = 5, 8


class Last:
    def __init__(self, z, y, x, ny):
        assert z == 2 and y == 8
        self.z, self.y, self.x = z, y, x
        self.zc, self.yc, self.xc = 1, 4, x // 2
        self.ny = ny
        self.columns = distinct(range(-2, 3), ny)
        self.kept = distinct(range(-2, 1), ny)
        self.in_rows, self.out_rows = 8 * len(self.columns), 8 * len(self.kept)
        self.z_own, self.y_own = 2 * BEHIND, 8 * self.columns.index(0)
        self.k_own = 8 * self.kept.index(0)

    def slot(self, found, o):
        return [(o - p) % self.ny == 0 for p in found].index(True)

    def matrices(self):
        fwd = np.zeros((self.out_rows, self.in_rows))
        for s, c in enumerate(self.kept):
            for i in range(4):
                for k in range(12):
                    at = 8 * c + 2 * i + k
                    col = 8 * self.slot(self.columns, at // 8) + at % 8
                    fwd[8 * s + i, col] += low_taps[k]
                    fwd[8 * s + 4 + i, col] += high_taps[k]
        inv = np.zeros((16, self.out_rows))
        for j in range(-5, 8):
            for t in range(6):
                k = 2 * t + j % 2
                c = j // 2 - t
                col = 8 * self.slot(self.kept, c // 4) + c % 4
                inv[8 + j, col] += low_taps[k]
                inv[8 + j, col + 4] += high_taps[k]
        return {
            "x_fwd": right_matrix(x_matrix(self.x)),
            "x_inv": right_matrix(x_matrix(self.x).T),
            "y_fwd": left_matrix(np.kron(np.eye(6), fwd * SCALE)),
            "y_inv": left_matrix(np.kron(np.eye(8), inv * SCALE)),
        }


class Level:
    z_own = y_own = 0

    def __init__(self, z, y, x):
        self.z, self.y, self.x = z, y, x
        self.zc, self.yc, self.xc = z // 2, y // 2, x // 2
        self.states = self.zc >= 4
        self.far = self.zc == 4
        self.comb = self.yc >= 8
        assert self.states or self.zc <= 2
        assert self.comb
        self.used = y + 8
        self.rows = y + 16
        self.fwd_planes = z if self.states else z + 10
        self.back = 0 if self.states else 5
        self.group = min(z, 8)
        self.back_group = max(min(self.zc, 8), 4)

    def matrices(self):
        n, half = self.y, self.yc
        own, ahead, pick = y_split_parts(n)
        fwd = np.zeros((n, self.used))
        fwd[:, :n] = own
        inv_own, behind, inv_pick = y_merge_parts(n)
        inv = np.zeros((n, self.used))
        inv[:, :n] = inv_own
        out = {"x_fwd": right_matrix(x_matrix(self.x)), "x_inv": right_matrix(x_matrix(self.x).T)}
        if self.comb:
            fwd[:, n : n + 5] = ahead
            inv[:, n : n + 5] = behind
            small = np.zeros((8, 16))
            small[:5, :10] = pick
            out["c_fwd"] = left_matrix(np.kron(np.eye(self.group), small))
            small = np.zeros((8, 16))
            small[:5, 3:8] = inv_pick[:, :5]
            small[:5, 11:16] = inv_pick[:, 5:]
            out["c_inv"] = left_matrix(np.kron(np.eye(self.back_group), small))
            if self.yc == 8:
                out["c_low"] = left_matrix(np.kron(np.eye(8), small[:, :8]))
        out["y_fwd"] = left_matrix(fwd * SCALE)
        out["y_inv"] = left_matrix(inv * SCALE)
        return out


def hop_list(length, rim):
    pieces = []
    done = 0
    hop = 1
    while done < rim:
        take = min(length, rim - done)
        pieces.append((hop, done, take))
        done += take
        hop += 1
    return pieces


def right_matrix(matrix):
    high, low = halves(matrix)
    return np.concatenate([high, high, low], axis=0)


def left_matrix(matrix):
    short = -matrix.shape[1] % 16
    high, low = halves(np.pad(matrix, ((0, 0), (0, short))))
    return np.concatenate([high, high, low], axis=1)


def split_product(data, right):
    high = data.astype(BF16)
    low = (data - high.astype(F32)).astype(BF16)
    depth = data.shape[1]
    if depth % 128:
        out = jnp.dot(high, right[0:depth], preferred_element_type=F32)
        out += jnp.dot(low, right[depth : 2 * depth], preferred_element_type=F32)
        return out + jnp.dot(high, right[2 * depth :], preferred_element_type=F32)
    wide = jnp.concatenate([high, low, high], axis=1)
    return jnp.dot(wide, right, preferred_element_type=F32)


def product_split(left, data):
    short = left.shape[1] // 3 - data.shape[0]
    if short:
        data = jnp.concatenate([data, jnp.zeros((short, data.shape[1]), F32)], axis=0)
    high = data.astype(BF16)
    low = (data - high.astype(F32)).astype(BF16)
    tall = jnp.concatenate([high, low, high], axis=0)
    return jnp.dot(left, tall, preferred_element_type=F32)


LATE = ("x_fwd0", "x_inv0", "keep0")
SENDS = 192
LOADS = 8


def kernel(levels, nz, ny, names, *refs):
    r = dict(zip(names, refs))
    lv1 = levels[0]
    half = lv1.xc
    lanes_of = (slice(0, half), slice(half, lv1.x))
    gz = lax.axis_index("gz")
    gy = lax.axis_index("gy")

    def device(dz, dy):
        return (lax.rem(gz + (dz + nz) % nz, nz), lax.rem(gy + (dy + ny) % ny, ny))

    offsets = sorted(
        {(dz % nz, dy % ny) for dz in range(-8, 9) for dy in range(-2, 3)} - {(0, 0)}
    )
    for no, lv in enumerate(levels[:-1]):
        for name in ("a", "e", "fr", "br"):
            if name in ("a", "e") or lv.states:
                buf = r[f"{name}{no}"]
                at = (slice(None),) * (len(buf.shape) - 2) + (slice(lv.y, lv.y + 8),)
                buf[at] = jnp.zeros(buf.shape[:-2] + (8, lv.x), F32)
    barrier = pltpu.get_barrier_semaphore()
    for dz, dy in offsets:
        pl.semaphore_signal(barrier, inc=1, device_id=device(dz, dy), device_id_type=MESH)

    chunk = lv1.z // 4
    matrix_loads = [
        pltpu.make_async_copy(
            r["x_fwd0"].at[:, lanes], r["x_fwd0_v"].at[:, lanes], r["load_sem"].at[n]
        )
        for n, lanes in ((4, lanes_of[0]), (7, lanes_of[1]))
    ]
    loads = [matrix_loads[0]]
    for c in range(4):
        at = pl.ds(c * chunk, chunk)
        loads.append(
            pltpu.make_async_copy(r["field"].at[at], r["whole"].at[at], r["load_sem"].at[c])
        )
    loads.append(pltpu.make_async_copy(r["keep0"], r["keep0_v"], r["load_sem"].at[5]))
    loads.append(pltpu.make_async_copy(r["x_inv0"], r["x_inv0_v"], r["load_sem"].at[6]))
    for load in loads:
        load.start()
    matrix_loads[1].start()
    small = [name for name in names if f"{name}_v" in r and name not in LATE]
    small_loads = []
    for n, name in enumerate(small):
        small_loads.append(
            pltpu.make_async_copy(r[name], r[f"{name}_v"], r["small_sem"].at[n])
        )
        small_loads[-1].start()
        r[name] = r[f"{name}_v"]

    used = [0]
    sends = []

    def send(src, dst, dz, dy):
        at = used[0]
        used[0] += 1
        copy = pltpu.make_async_remote_copy(
            src_ref=src,
            dst_ref=dst,
            send_sem=r["send_sem"].at[at],
            recv_sem=r["recv_sem"].at[at],
            device_id=device(dz, dy),
            device_id_type=MESH,
        )
        copy.start()
        sends.append(copy)
        return copy

    def loop(count, step, unroll=4):
        unroll = min(unroll, count)

        def several(i, carry):
            for n in range(unroll):
                step(i * unroll + n, 0)
            return carry

        if unroll == count:
            several(0, 0)
        else:
            lax.fori_loop(0, count // unroll, several, 0)

    def arrive(copies):
        for copy in copies:
            copy.wait_recv()

    fx = r["a0"]

    def x_split(lanes, first):
        for c in range(4):
            if first:
                loads[1 + c].wait()
                if c == 0:
                    loads[0].wait()
            at = pl.ds(c * chunk, chunk)
            rows = r["whole"][at].reshape(chunk * lv1.y, lv1.x)
            done = split_product(rows, r["x_fwd0_v"][:, lanes])
            fx[at, 0 : lv1.y, lanes] = done.reshape(chunk, lv1.y, half)

    def comb_forward(no, lanes=slice(None)):
        lv, a = levels[no], r[f"a{no}"]
        for start in range(0, lv.z, lv.group):
            at = slice(start, start + lv.group)
            rows = a[at, 0:16, lanes]
            wide = rows.shape[-1]
            done = product_split(r[f"c_fwd{no}"][...], rows.reshape(lv.group * 16, wide))
            a[at, lv.y + 8 : lv.y + 16, lanes] = done.reshape(lv.group, 8, wide)

    def row_of(tile, lv):
        return pl.multiple_of(jnp.where(tile < lv.y // 8, tile * 8, lv.y + 8), 8)

    def states_forward(no, lanes=slice(None)):
        lv, a, out = levels[no], r[f"a{no}"], r[f"fs{no}"]
        count = min(lv.zc, 5)

        def tile(t, carry):
            at = pl.ds(row_of(t, lv), 8)
            pairs = [
                lambda i=i: (a[2 * i, at, lanes], a[2 * i + 1, at, lanes]) for i in range(count)
            ]
            for k, value in enumerate(lattice_split(pairs)[1]):
                out[k, at, lanes] = value
            return carry

        lax.fori_loop(0, lv.y // 8 + 1, tile, 0)

    low, high = lanes_of
    x_split(low, True)
    for load in small_loads:
        load.wait()
    comb_forward(0, low)
    states_forward(0, low)

    pl.semaphore_wait(barrier, len(offsets))

    def send_states(no, sign, lanes, own, comb):
        lv = levels[no]
        src, dst = (r[f"fs{no}"], r[f"fr{no}"]) if sign < 0 else (r[f"bs{no}"], r[f"br{no}"])
        far = 0 if sign < 0 else 4
        top, in_at = lv.y + 8, slice(lv.y, lv.y + 5)
        copies = []
        if own is not None:
            copies.append(send(src.at[0:5, own, lanes], dst.at[0:5, own, lanes], sign, 0))
            if lv.far:
                copies.append(
                    send(src.at[far, own, lanes], dst.at[5, own, lanes], 2 * sign, 0)
                )
        if comb:
            copies.append(
                send(src.at[0:5, top : top + 5, lanes], dst.at[0:5, in_at, lanes], sign, sign)
            )
            if lv.far:
                copies.append(
                    send(
                        src.at[far, top : top + 5, lanes], dst.at[5, in_at, lanes], 2 * sign, sign
                    )
                )
        return copies

    every = slice(None)

    def send_forward(no, lanes):
        lv, a = levels[no], r[f"a{no}"]
        copies = []
        if lv.states:
            copies += send_states(no, -1, lanes, slice(0, lv.y), True)
            pieces = [(0, 0, lv.z)]
        else:
            pieces = [(0, 0, lv.z)] + hop_list(lv.z, 10)
        for hz, z_at, take in pieces:
            z_to = 0 if hz == 0 else lv.z + z_at
            if hz:
                copies.append(
                    send(a.at[0:take, 0 : lv.y, lanes], a.at[z_to : z_to + take, 0 : lv.y, lanes], -hz, 0)
                )
            copies.append(
                send(
                    a.at[0:take, lv.y + 8 : lv.y + 13, lanes],
                    a.at[z_to : z_to + take, lv.y : lv.y + 5, lanes],
                    -hz,
                    -1,
                )
            )
        return copies

    def z_split(no, lanes):
        lv, a, out = levels[no], r[f"a{no}"], r[f"zx{no}"]
        tall = 8 if lv.states else lv.used

        def tile(t, carry):
            at = pl.ds(pl.multiple_of(t * 8, 8), 8) if lv.states else slice(0, tall)
            state = [None] * 5
            if lv.states:
                got = r[f"fr{no}"]
                state = [got[k, at, lanes] for k in range(5)]
                if lv.far:
                    state[4] = state[4] + far_weight(lattice_split, 0, 4, 4) * got[5, at, lanes]
            count = lv.zc if lv.states else lv.zc + 5
            pairs = [
                lambda i=i: (a[2 * i, at, lanes], a[2 * i + 1, at, lanes]) for i in range(count)
            ]
            outs = lattice_split(pairs, state)[0]
            for i in range(lv.zc):
                for bz in range(2):
                    out[bz, i, at, lanes] = outs[i][bz]
            return carry

        if lv.states:
            lax.fori_loop(0, lv.used // 8, tile, 0)
        else:
            tile(0, 0)

    def y_split(no, bands, lanes):
        lv, src, coef, mask = levels[no], r[f"zx{no}"], r[f"e{no}"], r[f"mask{no}"]
        low = lanes.start in (None, 0)

        def plane(i, carry):
            for bz in bands:
                mixed = product_split(r[f"y_fwd{no}"][...], src[bz, i, 0 : lv.used, lanes])
                coef[bz, lv.back + i, 0 : lv.y, lanes] = mixed * mask[bz, i, :, lanes]
                if bz == 0 and low and no < LEVELS - 1:
                    down = levels[no + 1]
                    at = slice(down.y_own, down.y_own + lv.yc)
                    r[f"a{no + 1}"][down.z_own + i, at, :] = mixed[0 : lv.yc, 0 : lv.xc]
            return carry

        loop(lv.zc, plane)

    def comb_back(no, bands, lanes):
        lv, coef = levels[no], r[f"e{no}"]
        own = slice(lv.back, lv.back + lv.zc)
        planes = [(bz, lv.back + i) for bz in bands for i in range(lv.zc)]
        wide = lv.xc if no == 0 else lv.x
        for start in range(0, len(planes), lv.back_group):
            part = planes[start : start + lv.back_group]
            pieces = []
            for bz, i in part:
                pieces.append(coef[bz, i, lv.yc - 8 : lv.yc, lanes])
                pieces.append(coef[bz, i, 2 * lv.yc - 8 : 2 * lv.yc, lanes])
            done = product_split(r[f"c_inv{no}"][...], jnp.concatenate(pieces, axis=0))
            for n, (bz, i) in enumerate(part):
                coef[bz, i, lv.y + 8 : lv.y + 16, lanes] = done[8 * n : 8 * n + 8]

    def states_back(no, lanes, first, last):
        lv, coef, out = levels[no], r[f"e{no}"], r[f"bs{no}"]
        start = max(lv.zc - 5, 0)

        def tile(t, carry):
            at = pl.ds(row_of(t, lv), 8)
            pairs = [
                lambda i=i: (coef[0, i, at, lanes], coef[1, i, at, lanes])
                for i in range(start, lv.zc)
            ]
            for k, value in enumerate(lattice_merge(pairs)[1]):
                out[k, at, lanes] = value
            return carry

        lax.fori_loop(first, last, tile, 0)

    def send_rows_back(no, bands, lanes):
        lv, coef = levels[no], r[f"e{no}"]
        return [
            send(
                coef.at[bands, lv.back : lv.back + lv.zc, lv.y + 8 : lv.y + 13, lanes],
                coef.at[bands, lv.back : lv.back + lv.zc, lv.y : lv.y + 5, lanes],
                0,
                1,
            )
        ]

    def send_back(no):
        lv, coef = levels[no], r[f"e{no}"]
        copies = []
        if lv.states:
            copies += send_states(no, 1, every, slice(0, lv.y), True)
            return copies + send_rows_back(no, every, every)
        for hz, done, take in [(0, 0, lv.zc)] + hop_list(lv.zc, 5):
            src_at = slice(5 + lv.zc - take, 5 + lv.zc)
            dst_at = src_at if hz == 0 else slice(5 - done - take, 5 - done)
            if hz:
                copies.append(
                    send(coef.at[:, src_at, 0 : lv.y], coef.at[:, dst_at, 0 : lv.y], hz, 0)
                )
            copies.append(
                send(
                    coef.at[:, src_at, lv.y + 8 : lv.y + 13],
                    coef.at[:, dst_at, lv.y : lv.y + 5],
                    hz,
                    1,
                )
            )
        return copies

    def z_merge(no, lanes):
        lv, coef, out = levels[no], r[f"e{no}"], r[f"v{no}"]

        def tile(t, carry):
            at = pl.ds(pl.multiple_of(t * 8, 8), 8) if lv.states else slice(0, lv.used)
            state = [None] * 5
            if lv.states:
                got = r[f"br{no}"]
                state = [got[k, at, lanes] for k in range(5)]
                if lv.far:
                    state[0] = state[0] + far_weight(lattice_merge, 4, 0, 4) * got[5, at, lanes]
            pairs = [
                lambda i=i: (coef[0, i, at, lanes], coef[1, i, at, lanes])
                for i in range(lv.back + lv.zc)
            ]
            outs = lattice_merge(pairs, state)[0][lv.back :]
            for i in range(lv.zc):
                for p in range(2):
                    out[2 * i + p, at, lanes] = outs[i][p]
            return carry

        if lv.states:
            lax.fori_loop(0, lv.used // 8, tile, 0)
        else:
            tile(0, 0)

    def y_merge(no, lanes, out):
        lv, src = levels[no], r[f"v{no}"]

        def plane(z, carry):
            out[z, :, lanes] = product_split(r[f"y_inv{no}"][...], src[z, :, lanes])
            return carry

        loop(lv.z, plane)

    def fill_masks():
        loads[-2].wait()
        for no, lv in enumerate(levels):
            keep = r["keep0_v"] if no == 0 else r[f"keep{no}"]
            mask = r[f"mask{no}"]

            def fill(i, carry, lv=lv, keep=keep, mask=mask, no=no):
                for bz in range(2):
                    for by in range(2):
                        parts = []
                        for bx in range(2):
                            band = 4 * bz + 2 * by + bx
                            if band:
                                parts.append(keep[band - 1, i].astype(F32))
                            elif no == LEVELS - 1:
                                parts.append(r["coarse"][i].astype(F32))
                            else:
                                parts.append(jnp.zeros((lv.yc, lv.xc), F32))
                        first, z_first = by * lv.yc, 0
                        if no == LEVELS - 1:
                            first, z_first = first + lv.k_own, BEHIND
                        at = slice(first, first + lv.yc)
                        mask[bz, z_first + i, at, :] = jnp.concatenate(parts, axis=1)
                return carry

            lax.fori_loop(0, lv.zc, fill, 0)

    got = send_forward(0, low)
    matrix_loads[1].wait()
    x_split(high, False)
    comb_forward(0, high)
    states_forward(0, high)
    fill_masks()
    arrive(got)
    z_split(0, low)
    y_split(0, (0,), low)

    mid = levels[1]
    mid_low, mid_high = slice(0, mid.xc), slice(mid.xc, mid.x)
    last = levels[LEVELS - 1]
    edge = levels[LEVELS - 2]

    def gather(buf, lead, block, span, columns, own):
        copies = []
        for dz in range(-BEHIND, span + 1):
            for c, dy in enumerate(columns):
                if dz == 0 and dy == 0:
                    continue
                mine = slice(BEHIND * block, BEHIND * block + block)
                there = slice((BEHIND + dz) * block, (BEHIND + dz) * block + block)
                src = buf.at[lead + (mine, slice(own, own + 8))]
                dst = buf.at[lead + (there, slice(8 * c, 8 * c + 8))]
                copies.append(send(src, dst, -dz, -dy))
        return copies

    def last_level():
        no = LEVELS - 1
        a, zx, coef, v = r[f"a{no}"], r[f"zx{no}"], r[f"e{no}"], r[f"v{no}"]
        count = BEHIND + 1
        for t in range(last.in_rows // 8):
            at = slice(8 * t, 8 * t + 8)
            pairs = [
                lambda i=i: (a[2 * i, at, :], a[2 * i + 1, at, :]) for i in range(count + AHEAD)
            ]
            outs = lattice_split(pairs)[0]
            for i in range(count):
                for bz in range(2):
                    zx[bz * count + i, at, :] = outs[i][bz]
        rows = zx[...].reshape(2 * count * last.in_rows, last.x)
        done = split_product(rows, r[f"x_fwd{no}"][...])
        for g in range(2 * count // 6):
            part = done[6 * g * last.in_rows : 6 * (g + 1) * last.in_rows]
            mixed = product_split(r[f"y_fwd{no}"][...], part)
            mask = r[f"mask{no}"]
            for n in range(6):
                bz, i = divmod(6 * g + n, count)
                piece = mixed[n * last.out_rows : (n + 1) * last.out_rows]
                coef[bz, i] = piece * mask[bz, i]
        for t in range(last.out_rows // 8):
            at = slice(8 * t, 8 * t + 8)
            pairs = [lambda i=i: (coef[0, i, at, :], coef[1, i, at, :]) for i in range(count)]
            outs = lattice_merge(pairs)[0][count - 4 :]
            for i in range(4):
                for p in range(2):
                    v[2 * i + p, at, :] = outs[i][p]
        rows = v[...].reshape(8 * last.out_rows, last.x)
        done = product_split(r[f"y_inv{no}"][...], rows)
        return split_product(done, r[f"x_inv{no}"][...]).reshape(8, 16, last.x)

    def place_last(value):
        coef, planes = r[f"e{LEVELS - 2}"], edge.back + edge.zc
        coef[0, :, 0 : edge.yc, 0 : edge.xc] = value[8 - planes :, 8:16]
        done = product_split(r[f"c_low{LEVELS - 2}"][...], value[:, 0:8].reshape(64, last.x))
        done = done.reshape(8, 8, last.x)[8 - planes :]
        rim = slice(edge.y, edge.y + 8)
        coef[0, :, rim, 0 : edge.xc] = coef[0, :, rim, 0 : edge.xc] + done

    for no in range(1, LEVELS - 1):
        lv = levels[no]
        comb_forward(no)
        if lv.states:
            states_forward(no)
        got = send_forward(no, every)
        if no == 1:
            later = send_forward(0, high)
            y_split(0, (1,), low)
            comb_back(0, (1,), low)
        if no == 2:
            comb_back(1, (0, 1), mid_high)
            comb_back(1, (1,), mid_low)
            states_back(1, mid_high, 0, mid.y // 8 + 1)
            states_back(1, mid_low, mid.yc // 8, mid.y // 8)
            mask_got = gather(
                r[f"mask{LEVELS - 1}"], (every,), 1, 0, last.kept, last.k_own
            )
            arrive(later)
            z_split(0, high)
            y_split(0, (0, 1), high)
        arrive(got)
        z_split(no, every)
        count = 2 * lv.zc
        rows = r[f"zx{no}"][...].reshape(count * lv.used, lv.x)
        done = split_product(rows, r[f"x_fwd{no}"][...])
        r[f"zx{no}"][...] = done.reshape(2, lv.zc, lv.used, lv.x)
        y_split(no, (0, 1), every)

    got = gather(r[f"a{LEVELS - 1}"], (), 2, AHEAD, last.columns, last.y_own)
    comb_back(LEVELS - 2, (0, 1), every)
    edge_got = send_back(LEVELS - 2)
    comb_back(0, (0, 1), high)
    states_back(0, high, 0, lv1.y // 8 + 1)
    states_back(0, low, lv1.yc // 8, lv1.y // 8)
    arrive(mask_got)
    arrive(got)
    mid_got = send_states(1, 1, mid_high, slice(0, mid.y), True)
    mid_got += send_rows_back(1, every, mid_high)
    mid_got += send_states(1, 1, mid_low, slice(mid.yc, mid.y), False)
    mid_got += send_rows_back(1, slice(1, 2), mid_low)
    value = last_level()
    arrive(edge_got)
    for copy in edge_got:
        copy.wait_send()
    done_ids = [id(copy) for copy in edge_got]
    sends[:] = [copy for copy in sends if id(copy) not in done_ids]
    place_last(value)

    for no in range(LEVELS - 2, 0, -1):
        lv = levels[no]
        if no < LEVELS - 2:
            comb_back(no, (0,), mid_low)
            states_back(no, mid_low, 0, lv.yc // 8)
            states_back(no, mid_low, lv.y // 8, lv.y // 8 + 1)
            got = send_rows_back(no, slice(0, 1), mid_low)
            got += send_states(no, 1, mid_low, slice(0, lv.yc), True)
            got += mid_got
            early = send_states(0, 1, high, slice(0, lv1.y), True)
            early += send_rows_back(0, every, high)
            early_low = send_states(0, 1, low, slice(lv1.yc, lv1.y), False)
            early_low += send_rows_back(0, slice(1, 2), low)
            arrive(got)
        z_merge(no, every)
        y_merge(no, every, r[f"yv{no}"])
        rows = r[f"yv{no}"][...].reshape(lv.z * lv.y, lv.x)
        done = split_product(rows, r[f"x_inv{no}"][...]).reshape(lv.z, lv.y, lv.x)
        up = levels[no - 1]
        r[f"e{no - 1}"][0, up.back : up.back + up.zc, 0 : up.yc, 0 : up.xc] = done

    comb_back(0, (0,), low)
    states_back(0, low, 0, lv1.yc // 8)
    states_back(0, low, lv1.y // 8, lv1.y // 8 + 1)
    got = send_states(0, 1, low, slice(0, lv1.yc), True)
    got += send_rows_back(0, slice(0, 1), low)
    arrive(early)
    z_merge(0, high)
    y_merge(0, high, r["yv0"])
    loads[-1].wait()

    def x_part(c):
        at = pl.ds(c * chunk, chunk)
        rows = r["yv0"][at, :, high].reshape(chunk * lv1.y, half)
        r["part"][at] = split_product(rows, r["x_inv0_v"][...]).reshape(chunk, lv1.y, lv1.x)

    for c in range(4):
        x_part(c)
    arrive(early_low)
    arrive(got)
    z_merge(0, low)
    y_merge(0, low, r["out"])
    for copy in sends:
        copy.wait_send()
    assert used[0] <= SENDS


def last_kernel(v, part, right, out, whole, sem):
    planes, y, x = part.shape
    half = x // 2
    copies = []
    for n in range(2):
        lanes = slice(n * half, (n + 1) * half)
        rows = v[...].reshape(planes * y, half)
        done = split_product(rows, right[:, lanes]).reshape(planes, y, half)
        whole[:, :, lanes] = done + part[:, :, lanes]
        copies.append(pltpu.make_async_copy(whole.at[:, :, lanes], out.at[:, :, lanes], sem.at[n]))
        copies[-1].start()
    for copy in copies:
        copy.wait()


def solution(mesh):
    nz, ny = mesh.shape["gz"], mesh.shape["gy"]

    def on_device(field, k1, k2, k3, k4, coarse):
        z, y, x = field.shape
        levels = [Level(z >> n, y >> n, x >> n) for n in range(LEVELS - 1)]
        levels.append(Last(z >> 3, y >> 3, x >> 3, ny))
        vmem = pl.BlockSpec(memory_space=pltpu.VMEM)
        hbm = pl.BlockSpec(memory_space=pl.ANY)
        names = ["field", "keep0", "keep1", "keep2", "keep3", "coarse"]
        operands = [field, k1, k2, k3, k4, coarse]
        last = None
        for no, lv in enumerate(levels):
            for name, matrix in lv.matrices().items():
                if no == 0 and name == "x_inv":
                    whole = x_matrix(x).T
                    last = jnp.asarray(right_matrix(whole[: x // 2]))
                    matrix = right_matrix(whole[x // 2 :])
                names.append(f"{name}{no}")
                operands.append(jnp.asarray(matrix))
        inputs = dict(zip(names[1:], operands[1:]))
        names += ["out", "part"]
        scratch = {
            "whole": pltpu.VMEM((z, y, x), F32),
            "x_fwd0_v": pltpu.VMEM((3 * x, x), BF16),
            "x_inv0_v": pltpu.VMEM((3 * x // 2, x), BF16),
            "yv0": pltpu.VMEM((z, y, x), F32),
            "keep0_v": pltpu.VMEM(k1.shape, jnp.int32),
        }
        end = levels[-1]
        pairs = BEHIND + 1
        last_shapes = {
            "a": (2 * (pairs + AHEAD), end.in_rows),
            "zx": (2 * pairs, end.in_rows),
            "e": (2, pairs, end.out_rows),
            "v": (8, end.out_rows),
            "mask": (2, pairs, end.out_rows),
        }
        for name, shape in last_shapes.items():
            scratch[f"{name}{LEVELS - 1}"] = pltpu.VMEM(shape + (end.x,), F32)
        for no, lv in enumerate(levels[:-1]):
            scratch[f"a{no}"] = pltpu.VMEM((lv.fwd_planes, lv.rows, lv.x), F32)
            scratch[f"zx{no}"] = pltpu.VMEM((2, lv.zc, lv.used, lv.x), F32)
            scratch[f"e{no}"] = pltpu.VMEM((2, lv.back + lv.zc, lv.rows, lv.x), F32)
            scratch[f"v{no}"] = pltpu.VMEM((lv.z, lv.used, lv.x), F32)
            scratch[f"mask{no}"] = pltpu.VMEM((2, lv.zc, lv.y, lv.x), F32)
            if no:
                scratch[f"yv{no}"] = pltpu.VMEM((lv.z, lv.y, lv.x), F32)
            if lv.states:
                for name, planes in (("fs", 5), ("fr", 6), ("bs", 5), ("br", 6)):
                    scratch[f"{name}{no}"] = pltpu.VMEM((planes, lv.rows, lv.x), F32)
        for name, value in inputs.items():
            if name not in LATE:
                scratch[f"{name}_v"] = pltpu.VMEM(value.shape, value.dtype)
        scratch["small_sem"] = pltpu.SemaphoreType.DMA((len(inputs),))
        scratch["load_sem"] = pltpu.SemaphoreType.DMA((LOADS,))
        scratch["send_sem"] = pltpu.SemaphoreType.DMA((SENDS,))
        scratch["recv_sem"] = pltpu.SemaphoreType.DMA((SENDS,))
        names += list(scratch)
        merged, part = pl.pallas_call(
            functools.partial(kernel, levels, nz, ny, names),
            out_shape=[
                jax.ShapeDtypeStruct((z, y, x // 2), F32),
                jax.ShapeDtypeStruct((z, y, x), F32),
            ],
            in_specs=[hbm] * len(operands),
            out_specs=[vmem, vmem],
            scratch_shapes=list(scratch.values()),
            compiler_params=pltpu.CompilerParams(
                collective_id=0, has_side_effects=True, vmem_limit_bytes=36 * 1024 * 1024
            ),
        )(*[pltpu.with_memory_space_constraint(o, pltpu.HBM) for o in operands])
        return pl.pallas_call(
            last_kernel,
            out_shape=jax.ShapeDtypeStruct((z, y, x), F32),
            in_specs=[vmem] * 3,
            out_specs=hbm,
            scratch_shapes=[pltpu.VMEM((z, y, x), F32), pltpu.SemaphoreType.DMA((2,))],
            compiler_params=pltpu.CompilerParams(vmem_limit_bytes=48 * 1024 * 1024),
        )(merged, part, last)

    in_specs = (
        P("gz", "gy", None),
        P(None, "gz", "gy", None),
        P(None, "gz", "gy", None),
        P(None, "gz", "gy", None),
        P(None, "gz", "gy", None),
        P("gz", "gy", None),
    )
    return jax.shard_map(
        on_device, mesh=mesh, in_specs=in_specs, out_specs=P("gz", "gy", None), check_vma=False
    )
```
